32 devices in a mesh: req: 8 (over z, x), head: 4 (over y, core).
Axes of the slice: x: 2, y: 2, z: 4, core: 2. Of those that a mesh axis runs over, the one named last changes fastest.
Arguments:
- resid: bfloat16 [32, 4, 2048], P('req'), may hold values from -6 to 6
- proj: bfloat16 [32, 4, 3, 2048], P('req', None, None, 'head'), may hold values from -6 to 6
- conv_cache: bfloat16 [32, 3, 3, 2048], P('req', None, None, 'head'), may hold values from -6 to 6
- conv_weight: bfloat16 [4, 3, 2048], P(None, None, 'head'), may hold values from -3 to 3
- forget_bias: float32 [2048], P('head'), may hold values from -2 to 6
- owner: int32 [32], replicated, may hold values from 0 to 31, each once
- lengths: int32 [32], replicated, may hold values from 0 to 4096, as said below
- old_state: bfloat16 [32, 16, 128, 128], P('req', 'head'), may hold values from -6 to 6
- norm_gain: float32 [2048], P('head'), may hold values from 0.5 to 1.5
- out_weight: bfloat16 [2048, 2048], P('head'), may hold values from -0.125 to 0.125
Outputs:
- mixed: bfloat16 [32, 4, 2048], P('req')
- new_state: bfloat16 [32, 16, 128, 128], P('req', 'head')
The draws below stay inside these ranges and needn't reach their ends.
Inputs may be any that keep to these rules, and one draw needn't show every extreme that they name: `lengths`: short requests (below 3) and long ones are mixed; some request has length 0 and some 4096.
All inputs are finite; a program needn't handle non-finite values.
Results may differ from the reference program's by a relative error of at most 0.015.
Values may be sent and summed in bfloat16 or wider, within the bound.
No kernel may reach another device: no remote copies, remote signals or barrier semaphores. Data moves between devices by JAX's collectives and lax.ppermute only.
A program may use at most 64 MiB of HBM per device.

```python
import jax
import jax.numpy as jnp
from jax import lax

D = 2048
HEADS = 16
HD = 128
STEPS = 4
KW = 4
CONTEXT = 4096
R_DEV = 4
REQS = 32
N_REQ = 8


def draw_lengths(key, part):
    keys = jax.random.split(key, 5)
    short_lens = jax.random.randint(keys[0], (REQS,), 0, KW - 1)
    long_lens = jax.random.randint(keys[1], (REQS,), KW - 1, CONTEXT + 1)
    picker = jax.random.randint(keys[2], (REQS,), 0, 2)
    values = jnp.where(picker == 1, long_lens, short_lens)
    first_slot = jax.random.randint(keys[3], (), 0, REQS)
    second_slot = (first_slot + jax.random.randint(keys[4], (), 1, REQS)) % REQS
    values = values.at[first_slot].set(CONTEXT).at[second_slot].set(0)
    return values.astype(jnp.int32)


def level_of(key, shape, cuts, low, largest):
    level, own = 1.0, jax.random.fold_in(key, 6)
    for axis_at, blocks in cuts:
        draws = jnp.exp(jax.random.uniform(jax.random.fold_in(own, axis_at), (blocks,), jnp.float32, low / len(cuts), largest / len(cuts)))
        level = level * jnp.repeat(draws, shape[axis_at] // blocks).reshape([-1 if axis == axis_at else 1 for axis in range(len(shape))])
    return level


def normal_values(own_key, shape, width, bound, shards=(), kind=jnp.bfloat16):
    factor_of = level_of(own_key, shape, shards, -0.22, 0.18) if shards else 1.0
    result = jax.random.normal(own_key, shape, jnp.float32) * width * factor_of
    return jnp.minimum(jnp.maximum(result, -bound), bound).astype(kind)


def setup_inputs(seed: int = 0) -> dict:
    splits = jax.random.split(jax.random.key(seed), 11)
    resid = normal_values(splits[0], (REQS, STEPS, D), 1.0, 6.0, ((0, 8),))
    proj = normal_values(splits[1], (REQS, STEPS, 3, D), 1.0, 6.0, ((0, 8), (3, 4)))
    conv_cache = normal_values(splits[2], (REQS, KW - 1, 3, D), 1.0, 6.0, ((0, 8), (3, 4)))
    conv_weight = normal_values(splits[3], (KW, 3, D), 0.5, 3.0, ((2, 4),))
    forget_bias = jnp.clip(-2.0 + 8.0 * jax.random.uniform(splits[4], (D,), jnp.float32) ** level_of(splits[4], (D,), ((0, 4),), -0.2, 0.2), -2.0, 6.0)
    owner = jax.random.permutation(splits[5], REQS).astype(jnp.int32)
    lengths = draw_lengths(jax.random.fold_in(splits[10], 71), 0)
    old_state = normal_values(splits[7], (REQS, HEADS, HD, HD), 1.0, 6.0, ((0, 8), (1, 4)))
    norm_gain = jnp.clip(1.0 + 0.1 * jax.random.normal(splits[8], (D,), jnp.float32), 0.5, 1.5)
    out_weight = normal_values(splits[9], (D, D), D ** -0.5, 0.125, ((0, 4),))
    return dict(resid=resid, proj=proj, conv_cache=conv_cache, conv_weight=conv_weight, forget_bias=forget_bias, owner=owner, lengths=lengths, old_state=old_state, norm_gain=norm_gain, out_weight=out_weight)


def convolve(proj, conv_cache, conv_weight, lens):
    taps = conv_weight.shape[0]
    new_tokens = proj.shape[1]
    joined = jnp.concatenate([conv_cache, proj], axis=1).astype(jnp.float32)
    places = lens[:, None] + jnp.arange(-(taps - 1), new_tokens, dtype=jnp.int32)[None, :]
    joined = jnp.where((places >= 0)[:, :, None, None], joined, jnp.float32(0.0))
    summed = jnp.zeros(proj.shape, jnp.float32)
    for offset in range(taps):
        begin_at = taps - 1 - offset
        summed = summed + joined[:, begin_at:begin_at + new_tokens] * conv_weight[offset].astype(jnp.float32)
    return jax.nn.silu(summed).astype(jnp.bfloat16)

def recurrence(convolved, relocated, lens, forget_bias, norm_gain, head_size):
    local_reqs, new_tokens, _, channels = convolved.shape
    head_count = channels // head_size
    values = convolved.astype(jnp.float32).reshape(local_reqs, new_tokens, 3, head_count, head_size)
    queries = values[:, :, 0]
    keep_rate = jax.nn.sigmoid(values[:, :, 1] + forget_bias.astype(jnp.float32).reshape(head_count, head_size))
    inputs = values[:, :, 2]
    current = relocated.astype(jnp.float32) * (lens > 0).astype(jnp.float32)[:, None, None, None]
    outputs = []
    for position in range(new_tokens):
        rate_now = keep_rate[:, position]
        current = rate_now[..., None] * current + (1.0 - rate_now)[..., None] * inputs[:, position][:, :, None, :]
        outputs.append(jnp.einsum('rhk,rhkv->rhv', queries[:, position], current))
    stacked = jnp.stack(outputs, axis=1)
    inverse_rms = lax.rsqrt(lax.optimization_barrier(jnp.mean(stacked * stacked, axis=-1, keepdims=True)) + 1e-06)
    normed = (stacked * inverse_rms).reshape(local_reqs, new_tokens, channels) * norm_gain.astype(jnp.float32)
    return (normed.astype(jnp.bfloat16), current.astype(jnp.bfloat16))

def reference(resid, proj, conv_cache, conv_weight, forget_bias, owner, lengths, old_state, norm_gain, out_weight):
    inverse = jnp.zeros((REQS,), jnp.int32).at[owner].set(jnp.arange(REQS, dtype=jnp.int32))
    relocated = old_state[inverse]
    convolved = convolve(proj, conv_cache, conv_weight, lengths)

    def per_block(members):
        return recurrence(members[0], members[1], members[2], forget_bias, norm_gain, HD)
    normed, new_state = lax.map(per_block, (convolved.reshape(N_REQ, R_DEV, STEPS, 3, D), relocated.reshape(N_REQ, R_DEV, HEADS, HD, HD), lengths.reshape(N_REQ, R_DEV)))
    flat_normed = normed.reshape(REQS * STEPS, D)
    branch = jnp.dot(flat_normed, out_weight, preferred_element_type=jnp.float32)
    mixed = (resid.astype(jnp.float32).reshape(REQS * STEPS, D) + branch).astype(jnp.bfloat16).reshape(REQS, STEPS, D)
    return (mixed, new_state.reshape(REQS, HEADS, HD, HD))
```

```python
import functools

import jax
import jax.numpy as jnp
from jax import lax
from jax.experimental import pallas as pl
from jax.experimental.pallas import tpu as pltpu
from jax.sharding import PartitionSpec as P

BF16 = jnp.bfloat16
F32 = jnp.float32
VMEM = pltpu.VMEM


def convolve(proj, conv_cache, conv_weight, lens):
    taps = conv_weight.shape[0]
    new_tokens = proj.shape[1]
    joined = jnp.concatenate([conv_cache, proj], axis=1).astype(F32)
    places = lens[:, None] + jnp.arange(-(taps - 1), new_tokens, dtype=jnp.int32)[None, :]
    joined = jnp.where((places >= 0)[:, :, None, None], joined, F32(0.0))
    summed = jnp.zeros(proj.shape, F32)
    for offset in range(taps):
        begin_at = taps - 1 - offset
        summed = summed + joined[:, begin_at : begin_at + new_tokens] * conv_weight[offset].astype(F32)
    return jax.nn.silu(summed).astype(BF16)


def recurrence(convolved, relocated, lens, forget_bias, norm_gain, head_size):
    local_reqs, new_tokens, _, channels = convolved.shape
    head_count = channels // head_size
    values = convolved.astype(F32).reshape(local_reqs, new_tokens, 3, head_count, head_size)
    queries = values[:, :, 0]
    keep_rate = jax.nn.sigmoid(values[:, :, 1] + forget_bias.reshape(head_count, head_size))
    inputs = values[:, :, 2]
    current = relocated.astype(F32) * (lens > 0).astype(F32)[:, None, None, None]
    outputs = []
    for position in range(new_tokens):
        rate_now = keep_rate[:, position]
        current = (
            rate_now[..., None] * current
            + (1.0 - rate_now)[..., None] * inputs[:, position][:, :, None, :]
        )
        outputs.append(jnp.einsum("rhk,rhkv->rhv", queries[:, position], current))
    stacked = jnp.stack(outputs, axis=1)
    inverse_rms = lax.rsqrt(jnp.mean(stacked * stacked, axis=-1, keepdims=True) + 1e-06)
    normed = (stacked * inverse_rms).reshape(local_reqs, new_tokens, channels) * norm_gain
    return (normed.astype(BF16), current.astype(BF16))


def generic_body(
    resid, proj, conv_cache, conv_weight, forget_bias, owner, lengths, old_state, norm_gain, out_weight
):
    local_reqs, new_tokens = resid.shape[:2]
    devices = lax.axis_size("req")
    own_index = lax.axis_index("req")
    total_reqs = owner.shape[0]
    head_size = old_state.shape[-1]
    inverse = (
        jnp.zeros((total_reqs,), jnp.int32).at[owner].set(jnp.arange(total_reqs, dtype=jnp.int32))
    )
    local_lens = lax.dynamic_slice_in_dim(lengths, own_index * local_reqs, local_reqs)
    convolved = convolve(proj, conv_cache, conv_weight, local_lens)
    pieces = old_state.reshape(local_reqs, devices, -1)
    spread = lax.all_to_all(pieces, "req", split_axis=1, concat_axis=0, tiled=True)
    spread = spread.reshape(total_reqs, -1)
    picked = jnp.take(spread, inverse, axis=0).reshape(devices, local_reqs, 1, -1)
    routed = lax.all_to_all(picked, "req", split_axis=0, concat_axis=2, tiled=True)
    relocated = routed.reshape(old_state.shape)
    normed, new_state = recurrence(
        convolved, relocated, local_lens, forget_bias, norm_gain, head_size
    )
    flat_normed = normed.reshape(local_reqs * new_tokens, -1)
    flat_resid = resid.reshape(local_reqs * new_tokens, -1)
    partial_value = jnp.dot(flat_normed, out_weight, preferred_element_type=F32)
    summed = lax.psum(partial_value, "head")
    mixed = (flat_resid.astype(F32) + summed).astype(BF16).reshape(resid.shape)
    return (mixed, new_state)


def middle_kernel(blocks, reqs, steps, index_ref, *refs):
    own = refs[:blocks]
    sib = refs[blocks : 2 * blocks]
    packs = refs[2 * blocks : 3 * blocks]
    params_ref, live_ref = refs[3 * blocks : 3 * blocks + 2]
    at = 3 * blocks + 2
    states_out = refs[at : at + blocks]
    normed_out = refs[at + blocks : at + 2 * blocks]
    pool, flat, gathered, columns, lefts, local_out, state_out = refs[at + 2 * blocks :]
    count = blocks * reqs

    for s in range(blocks):
        pool[pl.ds(s * reqs, reqs)] = own[s][...]
        pool[pl.ds((blocks + s) * reqs, reqs)] = sib[s][...]
        flat[...] = packs[s][...].astype(F32)
        for row in range(3 * steps):
            gathered[row, pl.ds(s * reqs, reqs), :] = flat[pl.ds(row * reqs, reqs), :]

    bias = params_ref[0:1, :]
    gain = params_ref[1:2, :]
    live = live_ref[...]
    query = [gathered[t] for t in range(steps)]
    keep = [jax.nn.sigmoid(gathered[steps + t] + bias) for t in range(steps)]
    inputs = [gathered[2 * steps + t] for t in range(steps)]

    weights = []
    decay = live
    for t in range(steps):
        weights = [w * keep[t] for w in weights] + [1.0 - keep[t]]
        decay = decay * keep[t]
        lefts[pl.ds(t * count, count), :] = query[t] * decay
        out = jnp.zeros_like(query[t])
        for earlier in range(t + 1):
            score = jnp.sum(query[t] * weights[earlier], axis=-1, keepdims=True)
            out = out + score * inputs[earlier]
        local_out[pl.ds(t, count, stride=steps), :] = out

    columns[...] = jnp.zeros_like(columns)
    columns[pl.ds(0, count), :] = decay
    for t in range(steps):
        columns[pl.ds((1 + t) * count, count), :] = weights[t]
    turned = columns[...].T

    for i in range(count):
        old = pool[index_ref[i]]
        left = lefts[pl.ds(i, steps, stride=count), :].astype(BF16)
        state_out[pl.ds(i * steps, steps), :] = jnp.dot(left, old, preferred_element_type=F32)
        current = turned[:, i : i + 1] * old.astype(F32)
        for t in range(steps):
            column = (1 + t) * count + i
            current = current + turned[:, column : column + 1] * inputs[t][i : i + 1, :]
        states_out[i // reqs][i % reqs] = current.astype(BF16)

    head_out = state_out[...] + local_out[...]
    scale = lax.rsqrt(jnp.mean(head_out * head_out, axis=-1, keepdims=True) + 1e-06)
    normed = (head_out * scale * gain).astype(BF16)
    for s in range(blocks):
        normed_out[s][...] = normed[s * reqs * steps : (s + 1) * reqs * steps]


def middle(index, own, sib, packs, params, live, steps):
    blocks = len(own)
    reqs, head_size, _ = own[0].shape
    count = blocks * reqs
    spec = pl.BlockSpec(memory_space=VMEM)
    columns = -(-count * (1 + steps) // 128) * 128
    outs = pl.pallas_call(
        functools.partial(middle_kernel, blocks, reqs, steps),
        out_shape=[jax.ShapeDtypeStruct(own[0].shape, BF16)] * blocks
        + [jax.ShapeDtypeStruct((reqs * steps, head_size), BF16)] * blocks,
        in_specs=[pl.BlockSpec(memory_space=pltpu.SMEM)] + [spec] * (3 * blocks + 2),
        out_specs=[spec] * (2 * blocks),
        scratch_shapes=[
            VMEM((2 * count, head_size, head_size), BF16),
            VMEM((3 * steps * reqs, head_size), F32),
            VMEM((3 * steps, count, head_size), F32),
            VMEM((columns, head_size), F32),
            VMEM((steps * count, head_size), F32),
            VMEM((steps * count, head_size), F32),
            VMEM((steps * count, head_size), F32),
        ],
        name="middle",
    )(index, *own, *sib, *packs, params, live)
    return outs[:blocks], outs[blocks:]


def swapped_body(
    resid, proj, conv_cache, conv_weight, forget_bias, owner, lengths, old_state, norm_gain, out_weight
):
    local_reqs, steps, width = resid.shape
    blocks = old_state.shape[1]
    head_size = old_state.shape[-1]
    n_head = lax.axis_size("head")
    own_req = lax.axis_index("req")
    own_head = lax.axis_index("head")
    z, x, core = own_req // 2, own_req % 2, own_head % 2

    both = ("req", "head")
    sibling = [(i, i ^ 1) for i in range(n_head)]
    planes = range(n_head // 2)

    def swap(value, s):
        pairs = [
            ((a * 2 + b) * n_head + y * 2 + c, ((a ^ s) * 2 + c) * n_head + y * 2 + b)
            for a in range(blocks)
            for b in range(2)
            for y in planes
            for c in range(2)
        ]
        return lax.ppermute(value, both, pairs)

    def head_of(value, s, axis):
        return lax.dynamic_index_in_dim(value, z ^ s, axis, keepdims=False)

    order = [s for s in range(blocks - 1, -1, -1)]
    own = [None] * blocks
    for s in order:
        own[s] = swap(head_of(old_state, s, 1), s)

    params = jnp.stack([forget_bias, norm_gain]).reshape(2, blocks, head_size)
    other_params = lax.ppermute(params, "head", sibling)
    params = head_of(jnp.where(core == x, params, other_params), 0, 1)

    local_lens = lax.dynamic_slice_in_dim(lengths, own_req * local_reqs, local_reqs)
    convolved = convolve(proj, conv_cache, conv_weight, local_lens)
    convolved = convolved.reshape(local_reqs, steps, 3, blocks, head_size).transpose(3, 2, 1, 0, 4)
    convolved = convolved.reshape(blocks, 3 * steps * local_reqs, head_size)
    packs = [None] * blocks
    for s in order:
        packs[s] = swap(head_of(convolved, s, 0), s)
    sib = [None] * blocks
    for s in order:
        sib[s] = lax.ppermute(own[s], "head", sibling)

    zs = z ^ jnp.arange(blocks, dtype=jnp.int32)
    slots = ((zs * 2 + core) * local_reqs)[:, None] + jnp.arange(local_reqs, dtype=jnp.int32)[None, :]
    slots = slots.reshape(-1)
    total = owner.shape[0]
    hit = owner[None, :] == slots[:, None]
    source = jnp.sum(jnp.where(hit, jnp.arange(total, dtype=jnp.int32)[None, :], 0), axis=1)
    device, place = source // local_reqs, source % local_reqs
    away = (device % 2 != core).astype(jnp.int32)
    index = (away * blocks + ((device // 2) ^ z)) * local_reqs + place
    lens = jnp.sum(
        jnp.where(jnp.arange(total, dtype=jnp.int32)[None, :] == slots[:, None], lengths[None, :], 0),
        axis=1,
    )
    live = jnp.broadcast_to((lens > 0).astype(F32)[:, None], (slots.shape[0], head_size))

    states, normed = middle(index, own, sib, packs, params, live, steps)

    rows = [None] * blocks
    for s in order:
        rows[s] = swap(normed[s], s)
    back = [None] * blocks
    for s in order:
        back[s] = swap(states[s], s)

    flat = jnp.zeros((local_reqs * steps, blocks * head_size), BF16)
    for s in range(blocks):
        flat = lax.dynamic_update_slice(flat, rows[s], (0, (z ^ s) * head_size))
    part = jnp.dot(flat, out_weight, preferred_element_type=F32)
    part = part + lax.ppermute(part, "head", sibling)
    part = part.astype(BF16)
    part = part.astype(F32) + lax.ppermute(
        part, "head", [(i, (i + 2) % n_head) for i in range(n_head)]
    ).astype(F32)
    mixed = (resid.reshape(-1, width).astype(F32) + part).astype(BF16).reshape(resid.shape)

    new_state = jnp.zeros(old_state.shape, BF16)
    for s in range(blocks):
        new_state = lax.dynamic_update_slice(new_state, back[s][:, None], (0, z ^ s, 0, 0))
    return (mixed, new_state)


def solution(mesh):
    in_specs = (
        P("req", None, None),
        P("req", None, None, "head"),
        P("req", None, None, "head"),
        P(None, None, "head"),
        P("head"),
        P(),
        P(),
        P("req", "head", None, None),
        P("head"),
        P("head", None),
    )
    out_specs = (P("req", None, None), P("req", "head", None, None))

    def body(*args):
        heads = args[7].shape[1]
        swapped = (
            mesh.shape["req"] == 2 * heads and heads & (heads - 1) == 0 and mesh.shape["head"] == 4
        )
        return (swapped_body if swapped else generic_body)(*args)

    return jax.shard_map(body, mesh=mesh, in_specs=in_specs, out_specs=out_specs, check_vma=False)
```

```python
import functools

import jax
import jax.numpy as jnp
from jax import lax
from jax.experimental import pallas as pl
from jax.experimental.pallas import tpu as pltpu
from jax.sharding import PartitionSpec as P

BF16 = jnp.bfloat16
F32 = jnp.float32
VMEM = pltpu.VMEM


def convolve(proj, conv_cache, conv_weight, lens):
    taps = conv_weight.shape[0]
    new_tokens = proj.shape[1]
    joined = jnp.concatenate([conv_cache, proj], axis=1).astype(F32)
    places = lens[:, None] + jnp.arange(-(taps - 1), new_tokens, dtype=jnp.int32)[None, :]
    joined = jnp.where((places >= 0)[:, :, None, None], joined, F32(0.0))
    summed = jnp.zeros(proj.shape, F32)
    for offset in range(taps):
        begin_at = taps - 1 - offset
        summed = summed + joined[:, begin_at : begin_at + new_tokens] * conv_weight[offset].astype(F32)
    return jax.nn.silu(summed).astype(BF16)


def recurrence(convolved, relocated, lens, forget_bias, norm_gain, head_size):
    local_reqs, new_tokens, _, channels = convolved.shape
    head_count = channels // head_size
    values = convolved.astype(F32).reshape(local_reqs, new_tokens, 3, head_count, head_size)
    queries = values[:, :, 0]
    keep_rate = jax.nn.sigmoid(values[:, :, 1] + forget_bias.reshape(head_count, head_size))
    inputs = values[:, :, 2]
    current = relocated.astype(F32) * (lens > 0).astype(F32)[:, None, None, None]
    outputs = []
    for position in range(new_tokens):
        rate_now = keep_rate[:, position]
        current = (
            rate_now[..., None] * current
            + (1.0 - rate_now)[..., None] * inputs[:, position][:, :, None, :]
        )
        outputs.append(jnp.einsum("rhk,rhkv->rhv", queries[:, position], current))
    stacked = jnp.stack(outputs, axis=1)
    inverse_rms = lax.rsqrt(jnp.mean(stacked * stacked, axis=-1, keepdims=True) + 1e-06)
    normed = (stacked * inverse_rms).reshape(local_reqs, new_tokens, channels) * norm_gain
    return (normed.astype(BF16), current.astype(BF16))


def generic_body(
    resid, proj, conv_cache, conv_weight, forget_bias, owner, lengths, old_state, norm_gain, out_weight
):
    local_reqs, new_tokens = resid.shape[:2]
    devices = lax.axis_size("req")
    own_index = lax.axis_index("req")
    total_reqs = owner.shape[0]
    head_size = old_state.shape[-1]
    inverse = (
        jnp.zeros((total_reqs,), jnp.int32).at[owner].set(jnp.arange(total_reqs, dtype=jnp.int32))
    )
    local_lens = lax.dynamic_slice_in_dim(lengths, own_index * local_reqs, local_reqs)
    convolved = convolve(proj, conv_cache, conv_weight, local_lens)
    pieces = old_state.reshape(local_reqs, devices, -1)
    spread = lax.all_to_all(pieces, "req", split_axis=1, concat_axis=0, tiled=True)
    spread = spread.reshape(total_reqs, -1)
    picked = jnp.take(spread, inverse, axis=0).reshape(devices, local_reqs, 1, -1)
    routed = lax.all_to_all(picked, "req", split_axis=0, concat_axis=2, tiled=True)
    relocated = routed.reshape(old_state.shape)
    normed, new_state = recurrence(
        convolved, relocated, local_lens, forget_bias, norm_gain, head_size
    )
    flat_normed = normed.reshape(local_reqs * new_tokens, -1)
    flat_resid = resid.reshape(local_reqs * new_tokens, -1)
    partial_value = jnp.dot(flat_normed, out_weight, preferred_element_type=F32)
    summed = lax.psum(partial_value, "head")
    mixed = (flat_resid.astype(F32) + summed).astype(BF16).reshape(resid.shape)
    return (mixed, new_state)


def pack_kernel(blocks, taps, lens_ref, *refs):
    proj_ref, cache_ref, weight_ref, bias_ref, gain_ref, state_ref = refs[:6]
    outs = refs[6 : 6 + blocks]
    joined, conv, tail, sems = refs[6 + blocks :]
    reqs, _, steps, _ = proj_ref.shape
    head_size = state_ref.shape[-1]
    req = lax.axis_index("req")
    z = req // 2
    rows = reqs * head_size
    copies = []
    for s in range(blocks - 1, -1, -1):
        for r in range(reqs):
            copy = pltpu.make_async_copy(
                state_ref.at[r, z ^ s],
                outs[s].at[pl.ds(r * head_size, head_size), :],
                sems.at[s * reqs + r],
            )
            copy.start()
            copies.append(copy)

    past = taps - 1
    for p in range(3):
        weight = weight_ref[p].astype(F32)
        old = [cache_ref[j, p].astype(F32) for j in range(past)]
        for r in range(reqs):
            length = lens_ref[req * reqs + r]
            for j in range(past):
                seen = (length >= past - j).astype(F32)
                joined[j : j + 1, :] = old[j][r : r + 1, :] * seen
            joined[past : past + steps, :] = proj_ref[r, p].astype(F32)
            total = joined[past : past + steps, :] * weight[0:1, :]
            for tap in range(1, taps):
                total = total + joined[past - tap : past - tap + steps, :] * weight[tap : tap + 1, :]
            at = (p * reqs + r) * steps
            conv[at : at + steps, :] = total / (1.0 + jnp.exp(-total))

    count = 3 * reqs * steps
    tail[...] = jnp.zeros_like(tail)
    for s in range(blocks):
        head = z ^ s
        lanes = pl.ds(pl.multiple_of(head * head_size, head_size), head_size)
        tail[0:count, :] = conv[:, lanes]
        for k, ref in enumerate((bias_ref, gain_ref)):
            rest = ref[pl.ds(head, 1), :]
            for piece in range(3):
                value = rest.astype(BF16).astype(F32)
                tail[count + 3 * k + piece : count + 3 * k + piece + 1, :] = value
                rest = rest - value
        outs[s][rows:, :] = tail[...].astype(BF16)
    for copy in copies:
        copy.wait()


def pack(lengths, proj, conv_cache, conv_weight, forget_bias, norm_gain, old_state):
    reqs, blocks, head_size, _ = old_state.shape
    taps = conv_weight.shape[0]
    steps, width = proj.shape[1], proj.shape[-1]
    extra = 3 * reqs * steps + 6
    extra += -extra % 8
    spec = pl.BlockSpec(memory_space=VMEM)
    return pl.pallas_call(
        functools.partial(pack_kernel, blocks, taps),
        out_shape=[VMEM((reqs * head_size + extra, head_size), BF16)] * blocks,
        in_specs=[pl.BlockSpec(memory_space=pltpu.SMEM)]
        + [spec] * 5
        + [pl.BlockSpec(memory_space=pl.ANY)],
        out_specs=[spec] * blocks,
        scratch_shapes=[
            VMEM((taps - 1 + steps + 1, width), F32),
            VMEM((3 * reqs * steps, width), F32),
            VMEM((extra, head_size), F32),
            pltpu.SemaphoreType.DMA((blocks * reqs,)),
        ],
        name="pack",
    )(
        lengths,
        proj.transpose(0, 2, 1, 3),
        conv_cache.transpose(1, 2, 0, 3),
        conv_weight.transpose(1, 0, 2),
        forget_bias.reshape(blocks, head_size),
        norm_gain.reshape(blocks, head_size),
        old_state,
    )


def rows_kernel(blocks, reqs, steps, index_ref, *refs):
    own = refs[:blocks][::-1]
    sib = refs[blocks : 2 * blocks][::-1]
    live_ref = refs[2 * blocks]
    normed_out = refs[2 * blocks + 1 : 3 * blocks + 1]
    pool, turned, values = refs[3 * blocks + 1 : 3 * blocks + 4]
    flat, gathered, columns, lefts, local_out, state_out = refs[3 * blocks + 4 :]
    count = blocks * reqs
    head_size = pool.shape[-1]
    rows = reqs * head_size

    for s in range(blocks):
        flat[...] = own[s][rows:, :].astype(F32)
        for part in range(3):
            for t in range(steps):
                gathered[part * steps + t, pl.ds(s * reqs, reqs), :] = flat[
                    pl.ds(part * reqs * steps + t, reqs, stride=steps), :
                ]
        for r in range(reqs):
            here = slice(r * head_size, (r + 1) * head_size)
            pool[s * reqs + r] = own[s][here, :]
            pool[(blocks + s) * reqs + r] = sib[s][here, :]

    base = 3 * steps * reqs
    bias = flat[base : base + 1, :] + flat[base + 1 : base + 2, :] + flat[base + 2 : base + 3, :]
    gain = flat[base + 3 : base + 4, :] + flat[base + 4 : base + 5, :] + flat[base + 5 : base + 6, :]
    live = live_ref[...]
    query = [gathered[t] for t in range(steps)]
    keep = [jax.nn.sigmoid(gathered[steps + t] + bias) for t in range(steps)]
    inputs = [gathered[2 * steps + t] for t in range(steps)]

    weights = []
    decay = live
    for t in range(steps):
        weights = [w * keep[t] for w in weights] + [1.0 - keep[t]]
        decay = decay * keep[t]
        lefts[pl.ds(t * count, count), :] = query[t] * decay
        values[pl.ds(t * count, count), :] = inputs[t]
        out = jnp.zeros_like(query[t])
        for earlier in range(t + 1):
            score = jnp.sum(query[t] * weights[earlier], axis=-1, keepdims=True)
            out = out + score * inputs[earlier]
        local_out[pl.ds(t, count, stride=steps), :] = out

    for i in range(count):
        left = lefts[pl.ds(i, steps, stride=count), :].astype(BF16)
        state_out[pl.ds(i * steps, steps), :] = jnp.dot(
            left, pool[index_ref[i]], preferred_element_type=F32
        )
    head_out = state_out[...] + local_out[...]
    scale = lax.rsqrt(jnp.mean(head_out * head_out, axis=-1, keepdims=True) + 1e-06)
    normed = (head_out * scale * gain).astype(BF16)
    for s in range(blocks):
        normed_out[s][...] = normed[s * reqs * steps : (s + 1) * reqs * steps]

    columns[...] = jnp.zeros_like(columns)
    columns[pl.ds(0, count), :] = decay
    for t in range(steps):
        columns[pl.ds((1 + t) * count, count), :] = weights[t]
    turned[...] = columns[...].T


def states_kernel(blocks, reqs, steps, apart, index_ref, pool, turned_ref, values, *refs):
    riders = refs[: blocks - len(apart)]
    outs = refs[blocks - len(apart) :]
    head_size = pool.shape[-1]
    count = blocks * reqs
    turned = turned_ref[...]
    for i in range(count):
        current = turned[:, i : i + 1] * pool[index_ref[i]].astype(F32)
        for t in range(steps):
            column = (1 + t) * count + i
            value = values[t * count + i : t * count + i + 1, :]
            current = current + turned[:, column : column + 1] * value
        row = i % reqs * head_size
        outs[i // reqs][row : row + head_size, :] = current.astype(BF16)
    for k, s in enumerate(s for s in range(blocks) if s not in apart):
        outs[s][reqs * head_size :, :] = riders[k][...]


def place_kernel(blocks, *refs):
    parts, out, sems = refs[:blocks], refs[blocks], refs[blocks + 1]
    reqs, _, head_size, _ = out.shape
    z = lax.axis_index("req") // 2
    copies = []
    for s in range(blocks):
        for r in range(reqs):
            copy = pltpu.make_async_copy(
                parts[blocks - 1 - s].at[pl.ds(r * head_size, head_size), :],
                out.at[r, z ^ s],
                sems.at[s * reqs + r],
            )
            copy.start()
            copies.append(copy)
    for copy in copies:
        copy.wait()


def place(back, reqs):
    blocks = len(back)
    head_size = back[0].shape[-1]
    return pl.pallas_call(
        functools.partial(place_kernel, blocks),
        out_shape=jax.ShapeDtypeStruct((reqs, blocks, head_size, head_size), BF16),
        in_specs=[pl.BlockSpec(memory_space=VMEM)] * blocks,
        out_specs=pl.BlockSpec(memory_space=pl.ANY),
        scratch_shapes=[pltpu.SemaphoreType.DMA((blocks * reqs,))],
        name="place",
    )(*on_chip(*back[::-1]))


def on_chip(*arrays):
    return [pltpu.with_memory_space_constraint(value, VMEM) for value in arrays]


def middle_rows(index, own, sib, live, reqs, steps):
    blocks = len(own)
    count = blocks * reqs
    head_size = own[0].shape[-1]
    extra = own[0].shape[0] - reqs * head_size
    columns = -(-count * (1 + steps) // 128) * 128
    spec = pl.BlockSpec(memory_space=VMEM)
    outs = pl.pallas_call(
        functools.partial(rows_kernel, blocks, reqs, steps),
        out_shape=[VMEM((reqs * steps, head_size), BF16)] * blocks
        + [
            VMEM((2 * count, head_size, head_size), BF16),
            VMEM((head_size, columns), F32),
            VMEM((steps * count, head_size), F32),
        ],
        in_specs=[pl.BlockSpec(memory_space=pltpu.SMEM)] + [spec] * (2 * blocks + 1),
        out_specs=[spec] * (blocks + 3),
        scratch_shapes=[
            VMEM((extra, head_size), F32),
            VMEM((3 * steps, count, head_size), F32),
            VMEM((columns, head_size), F32),
            VMEM((steps * count, head_size), F32),
            VMEM((steps * count, head_size), F32),
            VMEM((steps * count, head_size), F32),
        ],
        name="rows",
    )(index, *on_chip(*own[::-1], *sib[::-1], live))
    return outs[:blocks], outs[blocks:]


def middle_states(index, kept, riders, blocks, reqs, steps, apart):
    head_size = kept[0].shape[-1]
    spec = pl.BlockSpec(memory_space=VMEM)
    rows = [reqs * head_size + (0 if s in apart else reqs * steps) for s in range(blocks)]
    return pl.pallas_call(
        functools.partial(states_kernel, blocks, reqs, steps, apart),
        out_shape=[VMEM((r, head_size), BF16) for r in rows],
        in_specs=[pl.BlockSpec(memory_space=pltpu.SMEM)] + [spec] * (3 + len(riders)),
        out_specs=[spec] * blocks,
        name="states",
    )(index, *on_chip(*kept, *riders))


def swapped_body(
    resid, proj, conv_cache, conv_weight, forget_bias, owner, lengths, old_state, norm_gain, out_weight
):
    local_reqs, steps, width = resid.shape
    blocks = old_state.shape[1]
    head_size = old_state.shape[-1]
    n_head = lax.axis_size("head")
    own_req = lax.axis_index("req")
    own_head = lax.axis_index("head")
    z, core = own_req // 2, own_head % 2
    state_rows = local_reqs * head_size

    both = ("req", "head")
    sibling = [(i, i ^ 1) for i in range(n_head)]
    across = [(i, (i + 2) % n_head) for i in range(n_head)]

    def swap(value, s):
        pairs = [
            ((a * 2 + b) * n_head + y * 2 + c, ((a ^ s) * 2 + c) * n_head + y * 2 + b)
            for a in range(blocks)
            for b in range(2)
            for y in range(n_head // 2)
            for c in range(2)
        ]
        return lax.ppermute(value, both, pairs)

    packs = pack(lengths, proj, conv_cache, conv_weight, forget_bias, norm_gain, old_state)
    own = [swap(packs[s], s) for s in range(blocks)]
    sib = [lax.ppermute(own[s][:state_rows], "head", sibling) for s in range(blocks)]

    zs = z ^ jnp.arange(blocks, dtype=jnp.int32)
    slots = ((zs * 2 + core) * local_reqs)[:, None] + jnp.arange(local_reqs, dtype=jnp.int32)[None, :]
    slots = slots.reshape(-1)
    every = jnp.arange(owner.shape[0], dtype=jnp.int32)[None, :]
    source = jnp.sum(jnp.where(owner[None, :] == slots[:, None], every, 0), axis=1)
    device, pos = source // local_reqs, source % local_reqs
    away = (device % 2 != core).astype(jnp.int32)
    index = (away * blocks + ((device // 2) ^ z)) * local_reqs + pos
    lens = jnp.sum(jnp.where(every == slots[:, None], lengths[None, :], 0), axis=1)
    live = jnp.broadcast_to((lens > 0).astype(F32)[:, None], (slots.shape[0], head_size))

    apart = tuple(range(blocks // 2, blocks))
    normed, kept = middle_rows(index, own, sib, live, local_reqs, steps)
    rows = [swap(normed[s], s) if s in apart else None for s in range(blocks)]
    riders = [normed[s] for s in range(blocks) if s not in apart]
    states = middle_states(index, kept, riders, blocks, local_reqs, steps, apart)
    held = lax.optimization_barrier((*states, *[rows[s] for s in apart]))
    states, far = held[:blocks], held[blocks:]
    for s, value in zip(apart, far):
        rows[s] = value
    back = [swap(states[s], s) for s in range(blocks)]

    flat = jnp.zeros((local_reqs * steps, blocks * head_size), BF16)
    for s in range(blocks):
        if s not in apart:
            rows[s] = back[s][state_rows:]
        flat = lax.dynamic_update_slice(flat, rows[s], (0, (z ^ s) * head_size))
    new_state = place(back, local_reqs)
    part = jnp.dot(flat, out_weight, preferred_element_type=F32)
    part = part + lax.ppermute(part, "head", sibling)
    part = part.astype(BF16)
    part = part.astype(F32) + lax.ppermute(part, "head", across).astype(F32)
    mixed = (resid.reshape(-1, width).astype(F32) + part).astype(BF16).reshape(resid.shape)
    return (mixed, new_state)


def solution(mesh):
    in_specs = (
        P("req", None, None),
        P("req", None, None, "head"),
        P("req", None, None, "head"),
        P(None, None, "head"),
        P("head"),
        P(),
        P(),
        P("req", "head", None, None),
        P("head"),
        P("head", None),
    )
    out_specs = (P("req", None, None), P("req", "head", None, None))

    def body(*args):
        heads = args[7].shape[1]
        swapped = (
            mesh.shape["req"] == 2 * heads and heads & (heads - 1) == 0 and mesh.shape["head"] == 4
        )
        return (swapped_body if swapped else generic_body)(*args)

    return jax.shard_map(body, mesh=mesh, in_specs=in_specs, out_specs=out_specs, check_vma=False)
```

```python
import functools

import jax
import jax.numpy as jnp
from jax import lax
from jax.experimental import pallas as pl
from jax.experimental.pallas import tpu as pltpu
from jax.sharding import PartitionSpec as P

BF16 = jnp.bfloat16
F32 = jnp.float32
VMEM = pltpu.VMEM


def convolve(proj, conv_cache, conv_weight, lens):
    taps = conv_weight.shape[0]
    new_tokens = proj.shape[1]
    joined = jnp.concatenate([conv_cache, proj], axis=1).astype(F32)
    places = lens[:, None] + jnp.arange(-(taps - 1), new_tokens, dtype=jnp.int32)[None, :]
    joined = jnp.where((places >= 0)[:, :, None, None], joined, F32(0.0))
    summed = jnp.zeros(proj.shape, F32)
    for offset in range(taps):
        begin_at = taps - 1 - offset
        summed = summed + joined[:, begin_at : begin_at + new_tokens] * conv_weight[offset].astype(F32)
    return jax.nn.silu(summed).astype(BF16)


def recurrence(convolved, relocated, lens, forget_bias, norm_gain, head_size):
    local_reqs, new_tokens, _, channels = convolved.shape
    head_count = channels // head_size
    values = convolved.astype(F32).reshape(local_reqs, new_tokens, 3, head_count, head_size)
    queries = values[:, :, 0]
    keep_rate = jax.nn.sigmoid(values[:, :, 1] + forget_bias.reshape(head_count, head_size))
    inputs = values[:, :, 2]
    current = relocated.astype(F32) * (lens > 0).astype(F32)[:, None, None, None]
    outputs = []
    for position in range(new_tokens):
        rate_now = keep_rate[:, position]
        current = (
            rate_now[..., None] * current
            + (1.0 - rate_now)[..., None] * inputs[:, position][:, :, None, :]
        )
        outputs.append(jnp.einsum("rhk,rhkv->rhv", queries[:, position], current))
    stacked = jnp.stack(outputs, axis=1)
    inverse_rms = lax.rsqrt(jnp.mean(stacked * stacked, axis=-1, keepdims=True) + 1e-06)
    normed = (stacked * inverse_rms).reshape(local_reqs, new_tokens, channels) * norm_gain
    return (normed.astype(BF16), current.astype(BF16))


def generic_body(
    resid, proj, conv_cache, conv_weight, forget_bias, owner, lengths, old_state, norm_gain, out_weight
):
    local_reqs, new_tokens = resid.shape[:2]
    devices = lax.axis_size("req")
    own_index = lax.axis_index("req")
    total_reqs = owner.shape[0]
    head_size = old_state.shape[-1]
    inverse = (
        jnp.zeros((total_reqs,), jnp.int32).at[owner].set(jnp.arange(total_reqs, dtype=jnp.int32))
    )
    local_lens = lax.dynamic_slice_in_dim(lengths, own_index * local_reqs, local_reqs)
    convolved = convolve(proj, conv_cache, conv_weight, local_lens)
    pieces = old_state.reshape(local_reqs, devices, -1)
    spread = lax.all_to_all(pieces, "req", split_axis=1, concat_axis=0, tiled=True)
    spread = spread.reshape(total_reqs, -1)
    picked = jnp.take(spread, inverse, axis=0).reshape(devices, local_reqs, 1, -1)
    routed = lax.all_to_all(picked, "req", split_axis=0, concat_axis=2, tiled=True)
    relocated = routed.reshape(old_state.shape)
    normed, new_state = recurrence(
        convolved, relocated, local_lens, forget_bias, norm_gain, head_size
    )
    flat_normed = normed.reshape(local_reqs * new_tokens, -1)
    flat_resid = resid.reshape(local_reqs * new_tokens, -1)
    partial_value = jnp.dot(flat_normed, out_weight, preferred_element_type=F32)
    summed = lax.psum(partial_value, "head")
    mixed = (flat_resid.astype(F32) + summed).astype(BF16).reshape(resid.shape)
    return (mixed, new_state)


def pack_kernel(blocks, taps, lens_ref, *refs):
    proj_ref, cache_ref, weight_ref, bias_ref, gain_ref, state_ref = refs[:6]
    outs = refs[6 : 6 + blocks]
    joined, conv, tail, sems = refs[6 + blocks :]
    reqs, _, steps, _ = proj_ref.shape
    head_size = state_ref.shape[-1]
    req = lax.axis_index("req")
    z = req // 2
    rows = reqs * head_size
    copies = []
    for s in range(blocks - 1, -1, -1):
        for r in range(reqs):
            copy = pltpu.make_async_copy(
                state_ref.at[r, z ^ s],
                outs[s].at[pl.ds(r * head_size, head_size), :],
                sems.at[s * reqs + r],
            )
            copy.start()
            copies.append(copy)

    past = taps - 1
    for p in range(3):
        weight = weight_ref[p].astype(F32)
        old = [cache_ref[j, p].astype(F32) for j in range(past)]
        for r in range(reqs):
            length = lens_ref[req * reqs + r]
            for j in range(past):
                seen = (length >= past - j).astype(F32)
                joined[j : j + 1, :] = old[j][r : r + 1, :] * seen
            joined[past : past + steps, :] = proj_ref[r, p].astype(F32)
            total = joined[past : past + steps, :] * weight[0:1, :]
            for tap in range(1, taps):
                total = total + joined[past - tap : past - tap + steps, :] * weight[tap : tap + 1, :]
            at = (p * reqs + r) * steps
            conv[at : at + steps, :] = total / (1.0 + jnp.exp(-total))

    count = 3 * reqs * steps
    tail[...] = jnp.zeros_like(tail)
    for s in range(blocks):
        head = z ^ s
        lanes = pl.ds(pl.multiple_of(head * head_size, head_size), head_size)
        tail[0:count, :] = conv[:, lanes]
        for k, ref in enumerate((bias_ref, gain_ref)):
            rest = ref[pl.ds(head, 1), :]
            for piece in range(3):
                value = rest.astype(BF16).astype(F32)
                tail[count + 3 * k + piece : count + 3 * k + piece + 1, :] = value
                rest = rest - value
        outs[s][rows:, :] = tail[...].astype(BF16)
    for copy in copies:
        copy.wait()


def pack(lengths, proj, conv_cache, conv_weight, forget_bias, norm_gain, old_state):
    reqs, blocks, head_size, _ = old_state.shape
    taps = conv_weight.shape[0]
    steps, width = proj.shape[1], proj.shape[-1]
    extra = 3 * reqs * steps + 6
    extra += -extra % 8
    spec = pl.BlockSpec(memory_space=VMEM)
    return pl.pallas_call(
        functools.partial(pack_kernel, blocks, taps),
        out_shape=[VMEM((reqs * head_size + extra, head_size), BF16)] * blocks,
        in_specs=[pl.BlockSpec(memory_space=pltpu.SMEM)]
        + [spec] * 5
        + [pl.BlockSpec(memory_space=pl.ANY)],
        out_specs=[spec] * blocks,
        scratch_shapes=[
            VMEM((taps - 1 + steps + 1, width), F32),
            VMEM((3 * reqs * steps, width), F32),
            VMEM((extra, head_size), F32),
            pltpu.SemaphoreType.DMA((blocks * reqs,)),
        ],
        name="pack",
    )(
        lengths,
        proj.transpose(0, 2, 1, 3),
        conv_cache.transpose(1, 2, 0, 3),
        conv_weight.transpose(1, 0, 2),
        forget_bias.reshape(blocks, head_size),
        norm_gain.reshape(blocks, head_size),
        old_state,
    )


def rows_kernel(blocks, reqs, steps, index_ref, *refs):
    own = refs[:blocks][::-1]
    sib = refs[blocks : 2 * blocks][::-1]
    live_ref = refs[2 * blocks]
    normed_out = refs[2 * blocks + 1 : 3 * blocks + 1]
    pool, turned, values = refs[3 * blocks + 1 : 3 * blocks + 4]
    flat, gathered, columns, lefts, local_out, state_out = refs[3 * blocks + 4 :]
    count = blocks * reqs
    head_size = pool.shape[-1]
    rows = reqs * head_size

    for s in range(blocks):
        flat[...] = own[s][rows:, :].astype(F32)
        for part in range(3):
            for t in range(steps):
                gathered[part * steps + t, pl.ds(s * reqs, reqs), :] = flat[
                    pl.ds(part * reqs * steps + t, reqs, stride=steps), :
                ]
        for r in range(reqs):
            here = slice(r * head_size, (r + 1) * head_size)
            pool[s * reqs + r] = own[s][here, :]
            pool[(blocks + s) * reqs + r] = sib[s][here, :]

    base = 3 * steps * reqs
    bias = flat[base : base + 1, :] + flat[base + 1 : base + 2, :] + flat[base + 2 : base + 3, :]
    gain = flat[base + 3 : base + 4, :] + flat[base + 4 : base + 5, :] + flat[base + 5 : base + 6, :]
    live = live_ref[...]
    query = [gathered[t] for t in range(steps)]
    keep = [jax.nn.sigmoid(gathered[steps + t] + bias) for t in range(steps)]
    inputs = [gathered[2 * steps + t] for t in range(steps)]

    weights = []
    decay = live
    for t in range(steps):
        weights = [w * keep[t] for w in weights] + [1.0 - keep[t]]
        decay = decay * keep[t]
        lefts[pl.ds(t * count, count), :] = query[t] * decay
        values[pl.ds(t * count, count), :] = inputs[t]
        out = jnp.zeros_like(query[t])
        for earlier in range(t + 1):
            score = jnp.sum(query[t] * weights[earlier], axis=-1, keepdims=True)
            out = out + score * inputs[earlier]
        local_out[pl.ds(t, count, stride=steps), :] = out

    for i in range(count):
        left = lefts[pl.ds(i, steps, stride=count), :].astype(BF16)
        state_out[pl.ds(i * steps, steps), :] = jnp.dot(
            left, pool[index_ref[i]], preferred_element_type=F32
        )
    head_out = state_out[...] + local_out[...]
    scale = lax.rsqrt(jnp.mean(head_out * head_out, axis=-1, keepdims=True) + 1e-06)
    normed = (head_out * scale * gain).astype(BF16)
    for s in range(blocks):
        normed_out[s][...] = normed[s * reqs * steps : (s + 1) * reqs * steps]

    columns[...] = jnp.zeros_like(columns)
    columns[pl.ds(0, count), :] = decay
    for t in range(steps):
        columns[pl.ds((1 + t) * count, count), :] = weights[t]
    turned[...] = columns[...].T


def states_kernel(blocks, reqs, steps, apart, index_ref, pool, turned_ref, values, *refs):
    riders = refs[: blocks - len(apart)]
    outs = refs[blocks - len(apart) :]
    head_size = pool.shape[-1]
    count = blocks * reqs
    turned = turned_ref[...]
    for i in range(count):
        current = turned[:, i : i + 1] * pool[index_ref[i]].astype(F32)
        for t in range(steps):
            column = (1 + t) * count + i
            value = values[t * count + i : t * count + i + 1, :]
            current = current + turned[:, column : column + 1] * value
        row = i % reqs * head_size
        outs[i // reqs][row : row + head_size, :] = current.astype(BF16)
    for k, s in enumerate(s for s in range(blocks) if s not in apart):
        outs[s][reqs * head_size :, :] = riders[k][...]


def place_kernel(blocks, *refs):
    parts, out, sems = refs[:blocks], refs[blocks], refs[blocks + 1]
    reqs, _, head_size, _ = out.shape
    z = lax.axis_index("req") // 2
    copies = []
    for s in range(blocks):
        for r in range(reqs):
            copy = pltpu.make_async_copy(
                parts[blocks - 1 - s].at[pl.ds(r * head_size, head_size), :],
                out.at[r, z ^ s],
                sems.at[s * reqs + r],
            )
            copy.start()
            copies.append(copy)
    for copy in copies:
        copy.wait()


def place(back, reqs):
    blocks = len(back)
    head_size = back[0].shape[-1]
    return pl.pallas_call(
        functools.partial(place_kernel, blocks),
        out_shape=jax.ShapeDtypeStruct((reqs, blocks, head_size, head_size), BF16),
        in_specs=[pl.BlockSpec(memory_space=VMEM)] * blocks,
        out_specs=pl.BlockSpec(memory_space=pl.ANY),
        scratch_shapes=[pltpu.SemaphoreType.DMA((blocks * reqs,))],
        name="place",
    )(*on_chip(*back[::-1]))


def on_chip(*arrays):
    return [pltpu.with_memory_space_constraint(value, VMEM) for value in arrays]


def middle_rows(index, own, sib, live, reqs, steps):
    blocks = len(own)
    count = blocks * reqs
    head_size = own[0].shape[-1]
    extra = own[0].shape[0] - reqs * head_size
    columns = -(-count * (1 + steps) // 128) * 128
    spec = pl.BlockSpec(memory_space=VMEM)
    outs = pl.pallas_call(
        functools.partial(rows_kernel, blocks, reqs, steps),
        out_shape=[VMEM((reqs * steps, head_size), BF16)] * blocks
        + [
            VMEM((2 * count, head_size, head_size), BF16),
            VMEM((head_size, columns), F32),
            VMEM((steps * count, head_size), F32),
        ],
        in_specs=[pl.BlockSpec(memory_space=pltpu.SMEM)] + [spec] * (2 * blocks + 1),
        out_specs=[spec] * (blocks + 3),
        scratch_shapes=[
            VMEM((extra, head_size), F32),
            VMEM((3 * steps, count, head_size), F32),
            VMEM((columns, head_size), F32),
            VMEM((steps * count, head_size), F32),
            VMEM((steps * count, head_size), F32),
            VMEM((steps * count, head_size), F32),
        ],
        name="rows",
    )(index, *on_chip(*own[::-1], *sib[::-1], live))
    return outs[:blocks], outs[blocks:]


def middle_states(index, kept, riders, blocks, reqs, steps, apart):
    head_size = kept[0].shape[-1]
    spec = pl.BlockSpec(memory_space=VMEM)
    rows = [reqs * head_size + (0 if s in apart else reqs * steps) for s in range(blocks)]
    return pl.pallas_call(
        functools.partial(states_kernel, blocks, reqs, steps, apart),
        out_shape=[VMEM((r, head_size), BF16) for r in rows],
        in_specs=[pl.BlockSpec(memory_space=pltpu.SMEM)] + [spec] * (3 + len(riders)),
        out_specs=[spec] * blocks,
        name="states",
    )(index, *on_chip(*kept, *riders))


def swapped_body(
    resid, proj, conv_cache, conv_weight, forget_bias, owner, lengths, old_state, norm_gain, out_weight
):
    local_reqs, steps, width = resid.shape
    blocks = old_state.shape[1]
    head_size = old_state.shape[-1]
    n_head = lax.axis_size("head")
    own_req = lax.axis_index("req")
    own_head = lax.axis_index("head")
    z, core = own_req // 2, own_head % 2
    state_rows = local_reqs * head_size

    both = ("req", "head")
    sibling = [(i, i ^ 1) for i in range(n_head)]

    def swap(value, s):
        pairs = [
            ((a * 2 + b) * n_head + y * 2 + c, ((a ^ s) * 2 + c) * n_head + y * 2 + b)
            for a in range(blocks)
            for b in range(2)
            for y in range(n_head // 2)
            for c in range(2)
        ]
        return lax.ppermute(value, both, pairs)

    packs = pack(lengths, proj, conv_cache, conv_weight, forget_bias, norm_gain, old_state)
    own = [swap(packs[s], s) for s in range(blocks)]
    sib = [lax.ppermute(own[s][:state_rows], "head", sibling) for s in range(blocks)]

    zs = z ^ jnp.arange(blocks, dtype=jnp.int32)
    slots = ((zs * 2 + core) * local_reqs)[:, None] + jnp.arange(local_reqs, dtype=jnp.int32)[None, :]
    slots = slots.reshape(-1)
    every = jnp.arange(owner.shape[0], dtype=jnp.int32)[None, :]
    source = jnp.sum(jnp.where(owner[None, :] == slots[:, None], every, 0), axis=1)
    device, pos = source // local_reqs, source % local_reqs
    away = (device % 2 != core).astype(jnp.int32)
    index = (away * blocks + ((device // 2) ^ z)) * local_reqs + pos
    lens = jnp.sum(jnp.where(every == slots[:, None], lengths[None, :], 0), axis=1)
    live = jnp.broadcast_to((lens > 0).astype(F32)[:, None], (slots.shape[0], head_size))

    apart = tuple(range(blocks // 2, blocks))
    normed, kept = middle_rows(index, own, sib, live, local_reqs, steps)
    rows = [swap(normed[s], s) if s in apart else None for s in range(blocks)]
    riders = [normed[s] for s in range(blocks) if s not in apart]
    states = middle_states(index, kept, riders, blocks, local_reqs, steps, apart)
    held = lax.optimization_barrier((*states, *[rows[s] for s in apart]))
    states, far = held[:blocks], held[blocks:]
    for s, value in zip(apart, far):
        rows[s] = value
    back = [swap(states[s], s) for s in range(blocks)]

    flat = jnp.zeros((local_reqs * steps, blocks * head_size), BF16)
    for s in range(blocks):
        if s not in apart:
            rows[s] = back[s][state_rows:]
        flat = lax.dynamic_update_slice(flat, rows[s], (0, (z ^ s) * head_size))
    new_state = place(back, local_reqs)
    part = jnp.dot(flat, out_weight, preferred_element_type=F32)
    part = part.astype(BF16)
    parts = [part] + [
        lax.ppermute(part, "head", [(i, i ^ k) for i in range(n_head)]) for k in range(1, n_head)
    ]
    parts = [value.astype(F32) for value in parts]
    part = (parts[0] + parts[1]) + (parts[2] + parts[3])
    mixed = (resid.reshape(-1, width).astype(F32) + part).astype(BF16).reshape(resid.shape)
    return (mixed, new_state)


def solution(mesh):
    in_specs = (
        P("req", None, None),
        P("req", None, None, "head"),
        P("req", None, None, "head"),
        P(None, None, "head"),
        P("head"),
        P(),
        P(),
        P("req", "head", None, None),
        P("head"),
        P("head", None),
    )
    out_specs = (P("req", None, None), P("req", "head", None, None))

    def body(*args):
        heads = args[7].shape[1]
        swapped = (
            mesh.shape["req"] == 2 * heads and heads & (heads - 1) == 0 and mesh.shape["head"] == 4
        )
        return (swapped_body if swapped else generic_body)(*args)

    return jax.shard_map(body, mesh=mesh, in_specs=in_specs, out_specs=out_specs, check_vma=False)
```

```python
import functools

import jax
import jax.numpy as jnp
from jax import lax
from jax.experimental import pallas as pl
from jax.experimental.pallas import tpu as pltpu
from jax.sharding import PartitionSpec as P

BF16 = jnp.bfloat16
F32 = jnp.float32
VMEM = pltpu.VMEM
PARAMS = pltpu.CompilerParams(vmem_limit_bytes=16 * 2**20)


def convolve(proj, conv_cache, conv_weight, lens):
    taps = conv_weight.shape[0]
    new_tokens = proj.shape[1]
    joined = jnp.concatenate([conv_cache, proj], axis=1).astype(F32)
    places = lens[:, None] + jnp.arange(-(taps - 1), new_tokens, dtype=jnp.int32)[None, :]
    joined = jnp.where((places >= 0)[:, :, None, None], joined, F32(0.0))
    summed = jnp.zeros(proj.shape, F32)
    for offset in range(taps):
        begin_at = taps - 1 - offset
        summed = summed + joined[:, begin_at : begin_at + new_tokens] * conv_weight[offset].astype(F32)
    return jax.nn.silu(summed).astype(BF16)


def recurrence(convolved, relocated, lens, forget_bias, norm_gain, head_size):
    local_reqs, new_tokens, _, channels = convolved.shape
    head_count = channels // head_size
    values = convolved.astype(F32).reshape(local_reqs, new_tokens, 3, head_count, head_size)
    queries = values[:, :, 0]
    keep_rate = jax.nn.sigmoid(values[:, :, 1] + forget_bias.reshape(head_count, head_size))
    inputs = values[:, :, 2]
    current = relocated.astype(F32) * (lens > 0).astype(F32)[:, None, None, None]
    outputs = []
    for position in range(new_tokens):
        rate_now = keep_rate[:, position]
        current = (
            rate_now[..., None] * current
            + (1.0 - rate_now)[..., None] * inputs[:, position][:, :, None, :]
        )
        outputs.append(jnp.einsum("rhk,rhkv->rhv", queries[:, position], current))
    stacked = jnp.stack(outputs, axis=1)
    inverse_rms = lax.rsqrt(jnp.mean(stacked * stacked, axis=-1, keepdims=True) + 1e-06)
    normed = (stacked * inverse_rms).reshape(local_reqs, new_tokens, channels) * norm_gain
    return (normed.astype(BF16), current.astype(BF16))


def generic_body(
    resid, proj, conv_cache, conv_weight, forget_bias, owner, lengths, old_state, norm_gain, out_weight
):
    local_reqs, new_tokens = resid.shape[:2]
    devices = lax.axis_size("req")
    own_index = lax.axis_index("req")
    total_reqs = owner.shape[0]
    head_size = old_state.shape[-1]
    inverse = (
        jnp.zeros((total_reqs,), jnp.int32).at[owner].set(jnp.arange(total_reqs, dtype=jnp.int32))
    )
    local_lens = lax.dynamic_slice_in_dim(lengths, own_index * local_reqs, local_reqs)
    convolved = convolve(proj, conv_cache, conv_weight, local_lens)
    pieces = old_state.reshape(local_reqs, devices, -1)
    spread = lax.all_to_all(pieces, "req", split_axis=1, concat_axis=0, tiled=True)
    spread = spread.reshape(total_reqs, -1)
    picked = jnp.take(spread, inverse, axis=0).reshape(devices, local_reqs, 1, -1)
    routed = lax.all_to_all(picked, "req", split_axis=0, concat_axis=2, tiled=True)
    relocated = routed.reshape(old_state.shape)
    normed, new_state = recurrence(
        convolved, relocated, local_lens, forget_bias, norm_gain, head_size
    )
    flat_normed = normed.reshape(local_reqs * new_tokens, -1)
    flat_resid = resid.reshape(local_reqs * new_tokens, -1)
    partial_value = jnp.dot(flat_normed, out_weight, preferred_element_type=F32)
    summed = lax.psum(partial_value, "head")
    mixed = (flat_resid.astype(F32) + summed).astype(BF16).reshape(resid.shape)
    return (mixed, new_state)


def pack_kernel(blocks, taps, lens_ref, *refs):
    proj_ref, cache_ref, weight_ref, bias_ref, gain_ref, state_ref = refs[:6]
    outs = refs[6 : 6 + blocks]
    joined, conv, tail, sems = refs[6 + blocks :]
    reqs, _, steps, _ = proj_ref.shape
    head_size = state_ref.shape[-1]
    req = lax.axis_index("req")
    z = req // 2
    rows = reqs * head_size
    copies = []
    for s in range(blocks - 1, -1, -1):
        for r in range(reqs):
            copy = pltpu.make_async_copy(
                state_ref.at[r, z ^ s],
                outs[s].at[pl.ds(r * head_size, head_size), :],
                sems.at[s * reqs + r],
            )
            copy.start()
            copies.append(copy)

    past = taps - 1
    for p in range(3):
        weight = weight_ref[p].astype(F32)
        old = [cache_ref[j, p].astype(F32) for j in range(past)]
        for r in range(reqs):
            length = lens_ref[req * reqs + r]
            own = p * reqs + r
            for j in range(past):
                seen = (length >= past - j).astype(F32)
                joined[own, j : j + 1, :] = old[j][r : r + 1, :] * seen
            joined[own, past : past + steps, :] = proj_ref[r, p].astype(F32)
            total = joined[own, past : past + steps, :] * weight[0:1, :]
            for tap in range(1, taps):
                begin = past - tap
                total = total + joined[own, begin : begin + steps, :] * weight[tap : tap + 1, :]
            at = own * steps
            conv[at : at + steps, :] = total / (1.0 + jnp.exp(-total))

    count = 3 * reqs * steps
    tail[...] = jnp.zeros_like(tail)
    for s in range(blocks):
        head = z ^ s
        lanes = pl.ds(pl.multiple_of(head * head_size, head_size), head_size)
        tail[0:count, :] = conv[:, lanes]
        for k, ref in enumerate((bias_ref, gain_ref)):
            rest = ref[pl.ds(head, 1), :]
            for piece in range(3):
                value = rest.astype(BF16).astype(F32)
                tail[count + 3 * k + piece : count + 3 * k + piece + 1, :] = value
                rest = rest - value
        outs[s][rows:, :] = tail[...].astype(BF16)
    for copy in copies:
        copy.wait()


def pack(lengths, proj, conv_cache, conv_weight, forget_bias, norm_gain, old_state):
    reqs, blocks, head_size, _ = old_state.shape
    taps = conv_weight.shape[0]
    steps, width = proj.shape[1], proj.shape[-1]
    extra = 3 * reqs * steps + 6
    extra += -extra % 8
    spec = pl.BlockSpec(memory_space=VMEM)
    return pl.pallas_call(
        functools.partial(pack_kernel, blocks, taps),
        out_shape=[VMEM((reqs * head_size + extra, head_size), BF16)] * blocks,
        in_specs=[pl.BlockSpec(memory_space=pltpu.SMEM)]
        + [spec] * 5
        + [pl.BlockSpec(memory_space=pl.ANY)],
        out_specs=[spec] * blocks,
        scratch_shapes=[
            VMEM((3 * reqs, taps + steps, width), F32),
            VMEM((3 * reqs * steps, width), F32),
            VMEM((extra, head_size), F32),
            pltpu.SemaphoreType.DMA((blocks * reqs,)),
        ],
        name="pack",
    )(
        lengths,
        proj.transpose(0, 2, 1, 3),
        conv_cache.transpose(1, 2, 0, 3),
        conv_weight.transpose(1, 0, 2),
        forget_bias.reshape(blocks, head_size),
        norm_gain.reshape(blocks, head_size),
        old_state,
    )


def rows_kernel(blocks, reqs, steps, index_ref, *refs):
    own = refs[:blocks][::-1]
    sib = refs[blocks : 2 * blocks]
    live_ref = refs[2 * blocks]
    normed_out = refs[2 * blocks + 1 : 3 * blocks + 1]
    pool, turned, lasting, values = refs[3 * blocks + 1 : 3 * blocks + 5]
    flat, gathered, columns, lefts, local_out, state_out = refs[3 * blocks + 5 :]
    count = blocks * reqs
    head_size = pool.shape[-1]
    rows = reqs * head_size

    for s in range(blocks):
        flat[...] = own[s][rows:, :].astype(F32)
        for part in range(3):
            for t in range(steps):
                gathered[part * steps + t, pl.ds(s * reqs, reqs), :] = flat[
                    pl.ds(part * reqs * steps + t, reqs, stride=steps), :
                ]
        for r in range(reqs):
            here = slice(r * head_size, (r + 1) * head_size)
            pool[s * reqs + r] = own[s][here, :]
            pool[(blocks + s) * reqs + r] = sib[s][here, :]

    base = 3 * steps * reqs
    bias = flat[base : base + 1, :] + flat[base + 1 : base + 2, :] + flat[base + 2 : base + 3, :]
    gain = flat[base + 3 : base + 4, :] + flat[base + 4 : base + 5, :] + flat[base + 5 : base + 6, :]
    live = live_ref[...]
    query = [gathered[t] for t in range(steps)]
    keep = [jax.nn.sigmoid(gathered[steps + t] + bias) for t in range(steps)]
    inputs = [gathered[2 * steps + t] for t in range(steps)]

    weights = []
    decay = live
    for t in range(steps):
        weights = [w * keep[t] for w in weights] + [1.0 - keep[t]]
        decay = decay * keep[t]
        lefts[pl.ds(t * count, count), :] = query[t] * decay
        out = jnp.zeros_like(query[t])
        for earlier in range(t + 1):
            score = jnp.sum(query[t] * weights[earlier], axis=-1, keepdims=True)
            out = out + score * inputs[earlier]
        local_out[pl.ds(t, count, stride=steps), :] = out

    for i in range(count):
        left = lefts[pl.ds(i, steps, stride=count), :].astype(BF16)
        state_out[pl.ds(i * steps, steps), :] = jnp.dot(
            left, pool[index_ref[i]], preferred_element_type=F32
        )
    head_out = state_out[...] + local_out[...]
    scale = lax.rsqrt(jnp.mean(head_out * head_out, axis=-1, keepdims=True) + 1e-06)
    normed = (head_out * scale * gain).astype(BF16)
    for s in range(blocks):
        normed_out[s][...] = normed[s * reqs * steps : (s + 1) * reqs * steps]

    columns[...] = jnp.zeros_like(columns)
    columns[pl.ds(0, count), :] = decay
    turned[...] = columns[...].T
    for s in range(blocks):
        for t in range(steps):
            here = pl.ds((s * steps + t) * reqs, reqs)
            lasting[here, :] = weights[t][s * reqs : (s + 1) * reqs, :]
            values[here, :] = inputs[t][s * reqs : (s + 1) * reqs, :]


def states_kernel(blocks, reqs, steps, apart, index_ref, pool, turned_ref, lasting, values, *refs):
    riders = refs[: blocks - len(apart)]
    outs = refs[blocks - len(apart) :]
    head_size = pool.shape[-1]
    turned = turned_ref[...]
    of_req = lax.broadcasted_iota(jnp.int32, (steps * reqs, head_size), 0) % reqs
    for s in range(blocks):
        here = slice(s * steps * reqs, (s + 1) * steps * reqs)
        left = lasting[here, :]
        high = left.astype(BF16)
        low = (left - high.astype(F32)).astype(BF16)
        value = values[here, :]
        spread = [jnp.where(of_req == r, value, 0.0).astype(BF16) for r in range(reqs)]
        spread = jnp.concatenate(spread, axis=1)
        added = lax.dot_general(
            jnp.concatenate([high, low], axis=0),
            jnp.concatenate([spread, spread], axis=0),
            (((0,), (0,)), ((), ())),
            preferred_element_type=F32,
        )
        for r in range(reqs):
            i = s * reqs + r
            span = slice(r * head_size, (r + 1) * head_size)
            current = turned[:, i : i + 1] * pool[index_ref[i]].astype(F32) + added[:, span]
            outs[s][span, :] = current.astype(BF16)
    for k, s in enumerate(s for s in range(blocks) if s not in apart):
        outs[s][reqs * head_size :, :] = riders[k][...]


def project_kernel(blocks, *refs):
    parts, weight, out, left = refs[:blocks], refs[blocks], refs[blocks + 1], refs[blocks + 2]
    rows, head_size = out.shape[0], parts[0].shape[-1]
    z = lax.axis_index("req") // 2
    for s in range(blocks):
        lanes = pl.ds(pl.multiple_of((z ^ s) * head_size, head_size), head_size)
        left[:, lanes] = parts[s][parts[s].shape[0] - rows :, :]
    out[...] = jnp.dot(left[...], weight[...], preferred_element_type=F32).astype(BF16)


def project(parts, weight, rows):
    spec = pl.BlockSpec(memory_space=VMEM)
    return pl.pallas_call(
        functools.partial(project_kernel, len(parts)),
        out_shape=VMEM((rows, weight.shape[1]), BF16),
        in_specs=[spec] * (len(parts) + 1),
        out_specs=spec,
        scratch_shapes=[VMEM((rows, weight.shape[0]), BF16)],
        name="project",
        compiler_params=PARAMS,
    )(*on_chip(*parts, weight))


def finish_kernel(blocks, terms, *refs):
    parts = refs[:blocks][::-1]
    resid = refs[blocks]
    added = refs[blocks + 1 : blocks + 1 + terms]
    mixed, out, sems = refs[blocks + 1 + terms :]
    reqs, _, head_size, _ = out.shape
    z = lax.axis_index("req") // 2
    copies = []
    for s in range(blocks):
        for r in range(reqs):
            copy = pltpu.make_async_copy(
                parts[s].at[pl.ds(r * head_size, head_size), :],
                out.at[r, z ^ s],
                sems.at[s * reqs + r],
            )
            copy.start()
            copies.append(copy)
    total = [value[...].astype(F32) for value in added]
    total = (total[0] + total[1]) + (total[2] + total[3])
    steps = total.shape[0] // reqs
    for r in range(reqs):
        mixed[r] = (resid[r].astype(F32) + total[r * steps : (r + 1) * steps, :]).astype(BF16)
    for copy in copies:
        copy.wait()


def finish(back, resid, added, reqs):
    blocks = len(back)
    head_size = back[0].shape[-1]
    spec = pl.BlockSpec(memory_space=VMEM)
    return pl.pallas_call(
        functools.partial(finish_kernel, blocks, len(added)),
        out_shape=[
            jax.ShapeDtypeStruct(resid.shape, BF16),
            jax.ShapeDtypeStruct((reqs, blocks, head_size, head_size), BF16),
        ],
        in_specs=[spec] * (blocks + 1 + len(added)),
        out_specs=[spec, pl.BlockSpec(memory_space=pl.ANY)],
        scratch_shapes=[pltpu.SemaphoreType.DMA((blocks * reqs,))],
        name="finish",
        compiler_params=PARAMS,
    )(*on_chip(*back[::-1], resid, *added))


def on_chip(*arrays):
    return [pltpu.with_memory_space_constraint(value, VMEM) for value in arrays]


def middle_rows(index, own, sib, live, reqs, steps):
    blocks = len(own)
    count = blocks * reqs
    head_size = own[0].shape[-1]
    extra = own[0].shape[0] - reqs * head_size
    columns = -(-count // 128) * 128
    spec = pl.BlockSpec(memory_space=VMEM)
    outs = pl.pallas_call(
        functools.partial(rows_kernel, blocks, reqs, steps),
        out_shape=[VMEM((reqs * steps, head_size), BF16)] * blocks
        + [
            VMEM((2 * count, head_size, head_size), BF16),
            VMEM((head_size, columns), F32),
            VMEM((steps * count, head_size), F32),
            VMEM((steps * count, head_size), F32),
        ],
        in_specs=[pl.BlockSpec(memory_space=pltpu.SMEM)] + [spec] * (2 * blocks + 1),
        out_specs=[spec] * (blocks + 4),
        scratch_shapes=[
            VMEM((extra, head_size), F32),
            VMEM((3 * steps, count, head_size), F32),
            VMEM((columns, head_size), F32),
            VMEM((steps * count, head_size), F32),
            VMEM((steps * count, head_size), F32),
            VMEM((steps * count, head_size), F32),
        ],
        name="rows",
        compiler_params=PARAMS,
    )(index, *on_chip(*own[::-1], *sib, live))
    return outs[:blocks], outs[blocks:]


def middle_states(index, kept, riders, blocks, reqs, steps, apart):
    head_size = kept[0].shape[-1]
    spec = pl.BlockSpec(memory_space=VMEM)
    rows = [reqs * head_size + (0 if s in apart else reqs * steps) for s in range(blocks)]
    return pl.pallas_call(
        functools.partial(states_kernel, blocks, reqs, steps, apart),
        out_shape=[VMEM((r, head_size), BF16) for r in rows],
        in_specs=[pl.BlockSpec(memory_space=pltpu.SMEM)] + [spec] * (4 + len(riders)),
        out_specs=[spec] * blocks,
        name="states",
        compiler_params=PARAMS,
    )(index, *on_chip(*kept, *riders))


def swapped_body(
    resid, proj, conv_cache, conv_weight, forget_bias, owner, lengths, old_state, norm_gain, out_weight
):
    local_reqs, steps, width = resid.shape
    blocks = old_state.shape[1]
    head_size = old_state.shape[-1]
    n_head = lax.axis_size("head")
    own_req = lax.axis_index("req")
    own_head = lax.axis_index("head")
    z, core = own_req // 2, own_head % 2
    state_rows = local_reqs * head_size

    both = ("req", "head")
    sibling = [(i, i ^ 1) for i in range(n_head)]

    def swap(value, s):
        pairs = [
            ((a * 2 + b) * n_head + y * 2 + c, ((a ^ s) * 2 + c) * n_head + y * 2 + b)
            for a in range(blocks)
            for b in range(2)
            for y in range(n_head // 2)
            for c in range(2)
        ]
        return lax.ppermute(value, both, pairs)

    packs = pack(lengths, proj, conv_cache, conv_weight, forget_bias, norm_gain, old_state)
    own = [swap(packs[s], s) for s in range(blocks)]
    near, far = range(blocks // 2), range(blocks // 2, blocks)
    sib = [lax.ppermute(own[s][:state_rows], "head", sibling) for s in near]
    held = lax.optimization_barrier((*sib, *[own[s] for s in far]))
    sib = list(held[: len(near)])
    own = own[: len(near)] + list(held[len(near) :])
    sib += [lax.ppermute(own[s][:state_rows], "head", sibling) for s in far]

    zs = z ^ jnp.arange(blocks, dtype=jnp.int32)
    slots = ((zs * 2 + core) * local_reqs)[:, None] + jnp.arange(local_reqs, dtype=jnp.int32)[None, :]
    slots = slots.reshape(-1)
    every = jnp.arange(owner.shape[0], dtype=jnp.int32)[None, :]
    source = jnp.sum(jnp.where(owner[None, :] == slots[:, None], every, 0), axis=1)
    device, pos = source // local_reqs, source % local_reqs
    away = (device % 2 != core).astype(jnp.int32)
    index = (away * blocks + ((device // 2) ^ z)) * local_reqs + pos
    lens = jnp.sum(jnp.where(every == slots[:, None], lengths[None, :], 0), axis=1)
    live = jnp.broadcast_to((lens > 0).astype(F32)[:, None], (slots.shape[0], head_size))

    apart = tuple(range(blocks // 2, blocks))
    normed, kept = middle_rows(index, own, sib, live, local_reqs, steps)
    rows = [swap(normed[s], s) if s in apart else None for s in range(blocks)]
    riders = [normed[s] for s in range(blocks) if s not in apart]
    states = middle_states(index, kept, riders, blocks, local_reqs, steps, apart)
    held = lax.optimization_barrier((*states, *[rows[s] for s in apart]))
    states, far = held[:blocks], held[blocks:]
    for s, value in zip(apart, far):
        rows[s] = value
    back = [swap(states[s], s) for s in range(blocks)]

    rows = [rows[s] if s in apart else back[s] for s in range(blocks)]
    part = project(rows, out_weight, local_reqs * steps)
    added = [part] + [
        lax.ppermute(part, "head", [(i, i ^ k) for i in range(n_head)]) for k in range(1, n_head)
    ]
    return tuple(finish(back, resid, added, local_reqs))


def solution(mesh):
    in_specs = (
        P("req", None, None),
        P("req", None, None, "head"),
        P("req", None, None, "head"),
        P(None, None, "head"),
        P("head"),
        P(),
        P(),
        P("req", "head", None, None),
        P("head"),
        P("head", None),
    )
    out_specs = (P("req", None, None), P("req", "head", None, None))

    def body(*args):
        heads = args[7].shape[1]
        swapped = (
            mesh.shape["req"] == 2 * heads and heads & (heads - 1) == 0 and mesh.shape["head"] == 4
        )
        return (swapped_body if swapped else generic_body)(*args)

    return jax.shard_map(body, mesh=mesh, in_specs=in_specs, out_specs=out_specs, check_vma=False)
```

```python
import functools

import jax
import jax.numpy as jnp
from jax import lax
from jax.experimental import pallas as pl
from jax.experimental.pallas import tpu as pltpu
from jax.sharding import PartitionSpec as P

BF16 = jnp.bfloat16
F32 = jnp.float32
VMEM = pltpu.VMEM
PARAMS = pltpu.CompilerParams(vmem_limit_bytes=16 * 2**20)


def convolve(proj, conv_cache, conv_weight, lens):
    taps = conv_weight.shape[0]
    new_tokens = proj.shape[1]
    joined = jnp.concatenate([conv_cache, proj], axis=1).astype(F32)
    places = lens[:, None] + jnp.arange(-(taps - 1), new_tokens, dtype=jnp.int32)[None, :]
    joined = jnp.where((places >= 0)[:, :, None, None], joined, F32(0.0))
    summed = jnp.zeros(proj.shape, F32)
    for offset in range(taps):
        begin_at = taps - 1 - offset
        summed = summed + joined[:, begin_at : begin_at + new_tokens] * conv_weight[offset].astype(F32)
    return jax.nn.silu(summed).astype(BF16)


def recurrence(convolved, relocated, lens, forget_bias, norm_gain, head_size):
    local_reqs, new_tokens, _, channels = convolved.shape
    head_count = channels // head_size
    values = convolved.astype(F32).reshape(local_reqs, new_tokens, 3, head_count, head_size)
    queries = values[:, :, 0]
    keep_rate = jax.nn.sigmoid(values[:, :, 1] + forget_bias.reshape(head_count, head_size))
    inputs = values[:, :, 2]
    current = relocated.astype(F32) * (lens > 0).astype(F32)[:, None, None, None]
    outputs = []
    for position in range(new_tokens):
        rate_now = keep_rate[:, position]
        current = (
            rate_now[..., None] * current
            + (1.0 - rate_now)[..., None] * inputs[:, position][:, :, None, :]
        )
        outputs.append(jnp.einsum("rhk,rhkv->rhv", queries[:, position], current))
    stacked = jnp.stack(outputs, axis=1)
    inverse_rms = lax.rsqrt(jnp.mean(stacked * stacked, axis=-1, keepdims=True) + 1e-06)
    normed = (stacked * inverse_rms).reshape(local_reqs, new_tokens, channels) * norm_gain
    return (normed.astype(BF16), current.astype(BF16))


def generic_body(
    resid, proj, conv_cache, conv_weight, forget_bias, owner, lengths, old_state, norm_gain, out_weight
):
    local_reqs, new_tokens = resid.shape[:2]
    devices = lax.axis_size("req")
    own_index = lax.axis_index("req")
    total_reqs = owner.shape[0]
    head_size = old_state.shape[-1]
    inverse = (
        jnp.zeros((total_reqs,), jnp.int32).at[owner].set(jnp.arange(total_reqs, dtype=jnp.int32))
    )
    local_lens = lax.dynamic_slice_in_dim(lengths, own_index * local_reqs, local_reqs)
    convolved = convolve(proj, conv_cache, conv_weight, local_lens)
    pieces = old_state.reshape(local_reqs, devices, -1)
    spread = lax.all_to_all(pieces, "req", split_axis=1, concat_axis=0, tiled=True)
    spread = spread.reshape(total_reqs, -1)
    picked = jnp.take(spread, inverse, axis=0).reshape(devices, local_reqs, 1, -1)
    routed = lax.all_to_all(picked, "req", split_axis=0, concat_axis=2, tiled=True)
    relocated = routed.reshape(old_state.shape)
    normed, new_state = recurrence(
        convolved, relocated, local_lens, forget_bias, norm_gain, head_size
    )
    flat_normed = normed.reshape(local_reqs * new_tokens, -1)
    flat_resid = resid.reshape(local_reqs * new_tokens, -1)
    partial_value = jnp.dot(flat_normed, out_weight, preferred_element_type=F32)
    summed = lax.psum(partial_value, "head")
    mixed = (flat_resid.astype(F32) + summed).astype(BF16).reshape(resid.shape)
    return (mixed, new_state)


def pack_kernel(blocks, lens_far, *refs):
    state_ref = refs[0]
    small = refs[1:6]
    outs = refs[6 : 6 + blocks]
    joined, conv, tail, state_sems, small_sems, lens_ref = refs[6 + blocks : 12 + blocks]
    held = refs[12 + blocks :]
    reqs, head_size = state_ref.shape[0], state_ref.shape[-1]
    req = lax.axis_index("req")
    z = req // 2
    rows = reqs * head_size
    fetches = [
        pltpu.make_async_copy(ref, to, small_sems.at[k])
        for k, (ref, to) in enumerate(zip((*small, lens_far), (*held, lens_ref)))
    ]
    for fetch in fetches:
        fetch.start()
    copies = []
    for s in range(blocks - 1, -1, -1):
        for r in range(reqs):
            copy = pltpu.make_async_copy(
                state_ref.at[r, z ^ s],
                outs[s].at[pl.ds(r * head_size, head_size), :],
                state_sems.at[s * reqs + r],
            )
            copy.start()
            copies.append(copy)
    tail[...] = jnp.zeros_like(tail)
    for fetch in fetches:
        fetch.wait()

    proj_ref, cache_ref, weight_ref, bias_ref, gain_ref = held
    steps = proj_ref.shape[2]
    taps = weight_ref.shape[1]
    past = taps - 1
    for p in range(3):
        weight = weight_ref[p].astype(F32)
        old = [cache_ref[j, p].astype(F32) for j in range(past)]
        for r in range(reqs):
            length = lens_ref[req * reqs + r]
            own = p * reqs + r
            for j in range(past):
                seen = (length >= past - j).astype(F32)
                joined[own, j : j + 1, :] = old[j][r : r + 1, :] * seen
            joined[own, past : past + steps, :] = proj_ref[r, p].astype(F32)
            total = joined[own, past : past + steps, :] * weight[0:1, :]
            for tap in range(1, taps):
                begin = past - tap
                total = total + joined[own, begin : begin + steps, :] * weight[tap : tap + 1, :]
            at = own * steps
            conv[at : at + steps, :] = total / (1.0 + jnp.exp(-total))

    count = 3 * reqs * steps
    for s in range(blocks):
        head = z ^ s
        lanes = pl.ds(pl.multiple_of(head * head_size, head_size), head_size)
        tail[0:count, :] = conv[:, lanes]
        for k, ref in enumerate((bias_ref, gain_ref)):
            rest = ref[pl.ds(head, 1), :]
            for piece in range(3):
                value = rest.astype(BF16).astype(F32)
                tail[count + 3 * k + piece : count + 3 * k + piece + 1, :] = value
                rest = rest - value
        outs[s][rows:, :] = tail[...].astype(BF16)
    for copy in copies:
        copy.wait()


def pack(lengths, proj, conv_cache, conv_weight, forget_bias, norm_gain, old_state):
    reqs, blocks, head_size, _ = old_state.shape
    taps = conv_weight.shape[0]
    steps, width = proj.shape[1], proj.shape[-1]
    extra = 3 * reqs * steps + 6
    extra += -extra % 8
    spec = pl.BlockSpec(memory_space=VMEM)
    small = (
        proj.transpose(0, 2, 1, 3),
        conv_cache.transpose(1, 2, 0, 3),
        conv_weight.transpose(1, 0, 2),
        forget_bias.reshape(blocks, head_size),
        norm_gain.reshape(blocks, head_size),
    )
    return pl.pallas_call(
        functools.partial(pack_kernel, blocks),
        out_shape=[VMEM((reqs * head_size + extra, head_size), BF16)] * blocks,
        in_specs=[pl.BlockSpec(memory_space=pl.ANY)] * 7,
        out_specs=[spec] * blocks,
        scratch_shapes=[
            VMEM((3 * reqs, taps + steps, width), F32),
            VMEM((3 * reqs * steps, width), F32),
            VMEM((extra, head_size), F32),
            pltpu.SemaphoreType.DMA((blocks * reqs,)),
            pltpu.SemaphoreType.DMA((len(small) + 1,)),
            pltpu.SMEM(lengths.shape, jnp.int32),
        ]
        + [VMEM(value.shape, value.dtype) for value in small],
        name="pack",
    )(lengths, old_state, *small)


def middle_kernel(blocks, reqs, steps, index_far, *refs):
    own = refs[:blocks][::-1]
    sib = refs[blocks : 2 * blocks]
    live_ref = refs[2 * blocks]
    outs = refs[2 * blocks + 1 : 3 * blocks + 1]
    pool, flat, gathered, columns, lefts, lasting, values, heard = refs[3 * blocks + 1 : -2]
    index_ref, sem = refs[-2:]
    fetch = pltpu.make_async_copy(index_far, index_ref, sem)
    fetch.start()
    count = blocks * reqs
    head_size = pool.shape[-1]
    rows = reqs * head_size

    for s in range(blocks):
        flat[...] = own[s][rows:, :].astype(F32)
        for part in range(3):
            for t in range(steps):
                gathered[part * steps + t, pl.ds(s * reqs, reqs), :] = flat[
                    pl.ds(part * reqs * steps + t, reqs, stride=steps), :
                ]
        for r in range(reqs):
            here = slice(r * head_size, (r + 1) * head_size)
            pool[s * reqs + r] = own[s][here, :]
            pool[(blocks + s) * reqs + r] = sib[s][here, :]
    base = 3 * steps * reqs
    bias = flat[base : base + 1, :] + flat[base + 1 : base + 2, :] + flat[base + 2 : base + 3, :]
    gain = flat[base + 3 : base + 4, :] + flat[base + 4 : base + 5, :] + flat[base + 5 : base + 6, :]
    live = live_ref[...]
    query = [gathered[t] for t in range(steps)]
    keep = [jax.nn.sigmoid(gathered[steps + t] + bias) for t in range(steps)]
    inputs = [gathered[2 * steps + t] for t in range(steps)]

    weights = []
    decay = live
    for t in range(steps):
        weights = [w * keep[t] for w in weights] + [1.0 - keep[t]]
        decay = decay * keep[t]
        lefts[pl.ds(t * count, count), :] = query[t] * decay
        out = jnp.zeros_like(query[t])
        for earlier in range(t + 1):
            score = jnp.sum(query[t] * weights[earlier], axis=-1, keepdims=True)
            out = out + score * inputs[earlier]
        heard[pl.ds(t, count, stride=steps), :] = out

    columns[...] = jnp.zeros_like(columns)
    columns[pl.ds(0, count), :] = decay
    turned = columns[...].T
    for s in range(blocks):
        mine = slice(s * reqs, (s + 1) * reqs)
        for t in range(steps):
            here = pl.ds((s * steps + t) * reqs, reqs)
            values[here, :] = inputs[t][mine, :]
            lasting[here, :] = weights[t][mine, :]

    fetch.wait()
    of_req = lax.broadcasted_iota(jnp.int32, (steps * reqs, head_size), 0) % reqs
    for s in range(blocks):
        here = slice(s * steps * reqs, (s + 1) * steps * reqs)
        left = lasting[here, :]
        high = left.astype(BF16)
        low = (left - high.astype(F32)).astype(BF16)
        value = values[here, :]
        spread = [jnp.where(of_req == r, value, 0.0).astype(BF16) for r in range(reqs)]
        spread = jnp.concatenate(spread, axis=1)
        added = lax.dot_general(
            jnp.concatenate([high, low], axis=0),
            jnp.concatenate([spread, spread], axis=0),
            (((0,), (0,)), ((), ())),
            preferred_element_type=F32,
        )
        for r in range(reqs):
            i = s * reqs + r
            old = pool[index_ref[i]]
            wanted = lefts[pl.ds(i, steps, stride=count), :].astype(BF16)
            said = jnp.dot(wanted, old, preferred_element_type=F32)
            heard[pl.ds(i * steps, steps), :] += said
            span = slice(r * head_size, (r + 1) * head_size)
            current = turned[:, i : i + 1] * old.astype(F32) + added[:, span]
            outs[s][span, :] = current.astype(BF16)

    head_out = heard[...]
    scale = lax.rsqrt(jnp.mean(head_out * head_out, axis=-1, keepdims=True) + 1e-06)
    normed = (head_out * scale * gain).astype(BF16)
    for s in range(blocks):
        outs[s][rows:, :] = normed[s * reqs * steps : (s + 1) * reqs * steps]


def middle(index, own, sib, live, reqs, steps):
    blocks = len(own)
    count = blocks * reqs
    head_size = own[0].shape[-1]
    extra = own[0].shape[0] - reqs * head_size
    columns = -(-count // 128) * 128
    spec = pl.BlockSpec(memory_space=VMEM)
    table = VMEM((steps * count, head_size), F32)
    return pl.pallas_call(
        functools.partial(middle_kernel, blocks, reqs, steps),
        out_shape=[VMEM((reqs * (head_size + steps), head_size), BF16)] * blocks,
        in_specs=[pl.BlockSpec(memory_space=pl.ANY)] + [spec] * (2 * blocks + 1),
        out_specs=[spec] * blocks,
        scratch_shapes=[
            VMEM((2 * count, head_size, head_size), BF16),
            VMEM((extra, head_size), F32),
            VMEM((3 * steps, count, head_size), F32),
            VMEM((columns, head_size), F32),
            table,
            table,
            table,
            table,
            pltpu.SMEM(index.shape, jnp.int32),
            pltpu.SemaphoreType.DMA(()),
        ],
        name="middle",
        compiler_params=PARAMS,
    )(index, *on_chip(*own[::-1], *sib, live))


def fetch_kernel(far_ref, out, sem):
    copy = pltpu.make_async_copy(far_ref, out, sem)
    copy.start()
    copy.wait()


def fetch(value):
    return pl.pallas_call(
        fetch_kernel,
        out_shape=VMEM(value.shape, value.dtype),
        in_specs=[pl.BlockSpec(memory_space=pl.ANY)],
        out_specs=pl.BlockSpec(memory_space=VMEM),
        scratch_shapes=[pltpu.SemaphoreType.DMA(())],
        name="fetch",
        compiler_params=PARAMS,
    )(pltpu.with_memory_space_constraint(value, pltpu.HBM))


def project_kernel(blocks, *refs):
    parts, weight, out, left = refs[:blocks][::-1], refs[blocks], refs[blocks + 1], refs[blocks + 2]
    rows, head_size = out.shape[0], parts[0].shape[-1]
    z = lax.axis_index("req") // 2
    for s in range(blocks):
        lanes = pl.ds(pl.multiple_of((z ^ s) * head_size, head_size), head_size)
        left[:, lanes] = parts[s][parts[s].shape[0] - rows :, :]
    out[...] = jnp.dot(left[...], weight[...], preferred_element_type=F32).astype(BF16)


def project(parts, weight, rows):
    spec = pl.BlockSpec(memory_space=VMEM)
    return pl.pallas_call(
        functools.partial(project_kernel, len(parts)),
        out_shape=VMEM((rows, weight.shape[1]), BF16),
        in_specs=[spec] * (len(parts) + 1),
        out_specs=spec,
        scratch_shapes=[VMEM((rows, weight.shape[0]), BF16)],
        name="project",
        compiler_params=PARAMS,
    )(*on_chip(*parts[::-1], weight))


def place_kernel(blocks, *refs):
    parts, out, sems = refs[:blocks][::-1], refs[blocks], refs[blocks + 1]
    reqs, _, head_size, _ = out.shape
    z = lax.axis_index("req") // 2
    copies = []
    for s in range(blocks):
        for r in range(reqs):
            copy = pltpu.make_async_copy(
                parts[s].at[pl.ds(r * head_size, head_size), :],
                out.at[r, z ^ s],
                sems.at[s * reqs + r],
            )
            copy.start()
            copies.append(copy)
    for copy in copies:
        copy.wait()


def place(back, shape):
    return pl.pallas_call(
        functools.partial(place_kernel, len(back)),
        out_shape=jax.ShapeDtypeStruct(shape, BF16),
        in_specs=[pl.BlockSpec(memory_space=VMEM)] * len(back),
        out_specs=pl.BlockSpec(memory_space=pl.ANY),
        scratch_shapes=[pltpu.SemaphoreType.DMA((len(back) * shape[0],))],
        name="place",
        compiler_params=PARAMS,
    )(*on_chip(*back[::-1]))


def add_kernel(resid, *refs):
    out = refs[-1]
    total = [value[...].astype(F32) for value in refs[:-1]]
    while len(total) > 1:
        total = [total[k] + total[k + 1] for k in range(0, len(total), 2)]
    reqs = resid.shape[0]
    steps = total[0].shape[0] // reqs
    for r in range(reqs):
        out[r] = (resid[r].astype(F32) + total[0][r * steps : (r + 1) * steps, :]).astype(BF16)


def add(resid, terms):
    spec = pl.BlockSpec(memory_space=VMEM)
    return pl.pallas_call(
        add_kernel,
        out_shape=jax.ShapeDtypeStruct(resid.shape, BF16),
        in_specs=[spec] * (1 + len(terms)),
        out_specs=spec,
        name="add",
        compiler_params=PARAMS,
    )(*on_chip(resid, *terms))


def on_chip(*arrays):
    return [pltpu.with_memory_space_constraint(value, VMEM) for value in arrays]


def swapped_body(
    resid, proj, conv_cache, conv_weight, forget_bias, owner, lengths, old_state, norm_gain, out_weight
):
    local_reqs, steps, width = resid.shape
    blocks = old_state.shape[1]
    head_size = old_state.shape[-1]
    n_head = lax.axis_size("head")
    own_req = lax.axis_index("req")
    own_head = lax.axis_index("head")
    z, core = own_req // 2, own_head % 2

    both = ("req", "head")
    sibling = [(i, i ^ 1) for i in range(n_head)]

    def swap(value, s):
        pairs = [
            ((a * 2 + b) * n_head + y * 2 + c, ((a ^ s) * 2 + c) * n_head + y * 2 + b)
            for a in range(blocks)
            for b in range(2)
            for y in range(n_head // 2)
            for c in range(2)
        ]
        return lax.ppermute(value, both, pairs)

    packs = pack(lengths, proj, conv_cache, conv_weight, forget_bias, norm_gain, old_state)
    own = [swap(packs[s], s) for s in range(blocks)]
    near, far = range(blocks // 2), range(blocks // 2, blocks)
    sib = [lax.ppermute(own[s], "head", sibling) for s in near]
    held = lax.optimization_barrier((*sib, *[own[s] for s in far]))
    sib = list(held[: len(near)])
    own = own[: len(near)] + list(held[len(near) :])
    sib += [lax.ppermute(own[s], "head", sibling) for s in far]

    zs = z ^ jnp.arange(blocks, dtype=jnp.int32)
    slots = ((zs * 2 + core) * local_reqs)[:, None] + jnp.arange(local_reqs, dtype=jnp.int32)[None, :]
    slots = slots.reshape(-1)
    every = jnp.arange(owner.shape[0], dtype=jnp.int32)[None, :]
    source = jnp.sum(jnp.where(owner[None, :] == slots[:, None], every, 0), axis=1)
    device, pos = source // local_reqs, source % local_reqs
    away = (device % 2 != core).astype(jnp.int32)
    index = (away * blocks + ((device // 2) ^ z)) * local_reqs + pos
    lens = jnp.sum(jnp.where(every == slots[:, None], lengths[None, :], 0), axis=1)
    live = jnp.broadcast_to((lens > 0).astype(F32)[:, None], (slots.shape[0], head_size))

    states = middle(index, own, sib, live, local_reqs, steps)
    back = [swap(states[s], s) for s in range(blocks)]
    weight, *_ = lax.optimization_barrier((out_weight, *states))
    part = project(back, fetch(weight), local_reqs * steps)
    terms = [part] + [
        lax.ppermute(part, "head", [(i, i ^ k) for i in range(n_head)]) for k in range(1, n_head)
    ]
    held = lax.optimization_barrier((*back, part))
    new_state = place(held[:blocks], old_state.shape)
    return add(resid, terms), new_state


def solution(mesh):
    in_specs = (
        P("req", None, None),
        P("req", None, None, "head"),
        P("req", None, None, "head"),
        P(None, None, "head"),
        P("head"),
        P(),
        P(),
        P("req", "head", None, None),
        P("head"),
        P("head", None),
    )
    out_specs = (P("req", None, None), P("req", "head", None, None))

    def body(*args):
        heads = args[7].shape[1]
        swapped = (
            mesh.shape["req"] == 2 * heads and heads & (heads - 1) == 0 and mesh.shape["head"] == 4
        )
        return (swapped_body if swapped else generic_body)(*args)

    return jax.shard_map(body, mesh=mesh, in_specs=in_specs, out_specs=out_specs, check_vma=False)
```

```python
import functools

import jax
import jax.numpy as jnp
from jax import lax
from jax.experimental import pallas as pl
from jax.experimental.pallas import tpu as pltpu
from jax.sharding import PartitionSpec as P

BF16 = jnp.bfloat16
F32 = jnp.float32
VMEM = pltpu.VMEM
PARAMS = pltpu.CompilerParams(vmem_limit_bytes=16 * 2**20)


def convolve(proj, conv_cache, conv_weight, lens):
    taps = conv_weight.shape[0]
    new_tokens = proj.shape[1]
    joined = jnp.concatenate([conv_cache, proj], axis=1).astype(F32)
    places = lens[:, None] + jnp.arange(-(taps - 1), new_tokens, dtype=jnp.int32)[None, :]
    joined = jnp.where((places >= 0)[:, :, None, None], joined, F32(0.0))
    summed = jnp.zeros(proj.shape, F32)
    for offset in range(taps):
        begin_at = taps - 1 - offset
        summed = summed + joined[:, begin_at : begin_at + new_tokens] * conv_weight[offset].astype(F32)
    return jax.nn.silu(summed).astype(BF16)


def recurrence(convolved, relocated, lens, forget_bias, norm_gain, head_size):
    local_reqs, new_tokens, _, channels = convolved.shape
    head_count = channels // head_size
    values = convolved.astype(F32).reshape(local_reqs, new_tokens, 3, head_count, head_size)
    queries = values[:, :, 0]
    keep_rate = jax.nn.sigmoid(values[:, :, 1] + forget_bias.reshape(head_count, head_size))
    inputs = values[:, :, 2]
    current = relocated.astype(F32) * (lens > 0).astype(F32)[:, None, None, None]
    outputs = []
    for position in range(new_tokens):
        rate_now = keep_rate[:, position]
        current = (
            rate_now[..., None] * current
            + (1.0 - rate_now)[..., None] * inputs[:, position][:, :, None, :]
        )
        outputs.append(jnp.einsum("rhk,rhkv->rhv", queries[:, position], current))
    stacked = jnp.stack(outputs, axis=1)
    inverse_rms = lax.rsqrt(jnp.mean(stacked * stacked, axis=-1, keepdims=True) + 1e-06)
    normed = (stacked * inverse_rms).reshape(local_reqs, new_tokens, channels) * norm_gain
    return (normed.astype(BF16), current.astype(BF16))


def generic_body(
    resid, proj, conv_cache, conv_weight, forget_bias, owner, lengths, old_state, norm_gain, out_weight
):
    local_reqs, new_tokens = resid.shape[:2]
    devices = lax.axis_size("req")
    own_index = lax.axis_index("req")
    total_reqs = owner.shape[0]
    head_size = old_state.shape[-1]
    inverse = (
        jnp.zeros((total_reqs,), jnp.int32).at[owner].set(jnp.arange(total_reqs, dtype=jnp.int32))
    )
    local_lens = lax.dynamic_slice_in_dim(lengths, own_index * local_reqs, local_reqs)
    convolved = convolve(proj, conv_cache, conv_weight, local_lens)
    pieces = old_state.reshape(local_reqs, devices, -1)
    spread = lax.all_to_all(pieces, "req", split_axis=1, concat_axis=0, tiled=True)
    spread = spread.reshape(total_reqs, -1)
    picked = jnp.take(spread, inverse, axis=0).reshape(devices, local_reqs, 1, -1)
    routed = lax.all_to_all(picked, "req", split_axis=0, concat_axis=2, tiled=True)
    relocated = routed.reshape(old_state.shape)
    normed, new_state = recurrence(
        convolved, relocated, local_lens, forget_bias, norm_gain, head_size
    )
    flat_normed = normed.reshape(local_reqs * new_tokens, -1)
    flat_resid = resid.reshape(local_reqs * new_tokens, -1)
    partial_value = jnp.dot(flat_normed, out_weight, preferred_element_type=F32)
    summed = lax.psum(partial_value, "head")
    mixed = (flat_resid.astype(F32) + summed).astype(BF16).reshape(resid.shape)
    return (mixed, new_state)


def pack_kernel(blocks, lens_far, *refs):
    state_ref = refs[0]
    small = refs[1:6]
    outs = refs[6 : 6 + blocks]
    joined, conv, tail, state_sems, small_sems, lens_ref = refs[6 + blocks : 12 + blocks]
    held = refs[12 + blocks :]
    reqs, head_size = state_ref.shape[0], state_ref.shape[-1]
    req = lax.axis_index("req")
    z = req // 2
    rows = reqs * head_size
    fetches = [
        pltpu.make_async_copy(ref, to, small_sems.at[k])
        for k, (ref, to) in enumerate(zip((*small, lens_far), (*held, lens_ref)))
    ]
    for fetch in fetches:
        fetch.start()
    copies = []
    for s in range(blocks - 1, -1, -1):
        for r in range(reqs):
            copy = pltpu.make_async_copy(
                state_ref.at[r, z ^ s],
                outs[s].at[pl.ds(r * head_size, head_size), :],
                state_sems.at[s * reqs + r],
            )
            copy.start()
            copies.append(copy)
    tail[...] = jnp.zeros_like(tail)
    for fetch in fetches:
        fetch.wait()

    proj_ref, cache_ref, weight_ref, bias_ref, gain_ref = held
    steps = proj_ref.shape[2]
    taps = weight_ref.shape[1]
    past = taps - 1
    for p in range(3):
        weight = weight_ref[p].astype(F32)
        old = [cache_ref[j, p].astype(F32) for j in range(past)]
        for r in range(reqs):
            length = lens_ref[req * reqs + r]
            own = p * reqs + r
            for j in range(past):
                seen = (length >= past - j).astype(F32)
                joined[own, j : j + 1, :] = old[j][r : r + 1, :] * seen
            joined[own, past : past + steps, :] = proj_ref[r, p].astype(F32)
            total = joined[own, past : past + steps, :] * weight[0:1, :]
            for tap in range(1, taps):
                begin = past - tap
                total = total + joined[own, begin : begin + steps, :] * weight[tap : tap + 1, :]
            at = own * steps
            conv[at : at + steps, :] = total / (1.0 + jnp.exp(-total))

    count = 3 * reqs * steps
    for s in range(blocks):
        head = z ^ s
        lanes = pl.ds(pl.multiple_of(head * head_size, head_size), head_size)
        tail[0:count, :] = conv[:, lanes]
        for k, ref in enumerate((bias_ref, gain_ref)):
            rest = ref[pl.ds(head, 1), :]
            for piece in range(3):
                value = rest.astype(BF16).astype(F32)
                tail[count + 3 * k + piece : count + 3 * k + piece + 1, :] = value
                rest = rest - value
        outs[s][rows:, :] = tail[...].astype(BF16)
    for copy in copies:
        copy.wait()


def pack(lengths, proj, conv_cache, conv_weight, forget_bias, norm_gain, old_state):
    reqs, blocks, head_size, _ = old_state.shape
    taps = conv_weight.shape[0]
    steps, width = proj.shape[1], proj.shape[-1]
    extra = 3 * reqs * steps + 6
    extra += -extra % 8
    spec = pl.BlockSpec(memory_space=VMEM)
    small = (
        proj.transpose(0, 2, 1, 3),
        conv_cache.transpose(1, 2, 0, 3),
        conv_weight.transpose(1, 0, 2),
        forget_bias.reshape(blocks, head_size),
        norm_gain.reshape(blocks, head_size),
    )
    return pl.pallas_call(
        functools.partial(pack_kernel, blocks),
        out_shape=[VMEM((reqs * head_size + extra, head_size), BF16)] * blocks,
        in_specs=[pl.BlockSpec(memory_space=pl.ANY)] * 7,
        out_specs=[spec] * blocks,
        scratch_shapes=[
            VMEM((3 * reqs, taps + steps, width), F32),
            VMEM((3 * reqs * steps, width), F32),
            VMEM((extra, head_size), F32),
            pltpu.SemaphoreType.DMA((blocks * reqs,)),
            pltpu.SemaphoreType.DMA((len(small) + 1,)),
            pltpu.SMEM(lengths.shape, jnp.int32),
        ]
        + [VMEM(value.shape, value.dtype) for value in small],
        name="pack",
    )(lengths, old_state, *small)


def middle_kernel(blocks, reqs, steps, index_far, *refs):
    own = in_order(refs[:blocks], order_out(blocks))
    sib = in_order(refs[blocks : 2 * blocks], order_out(blocks))
    live_ref = refs[2 * blocks]
    outs = refs[2 * blocks + 1 : 3 * blocks + 1]
    pool, flat, gathered, columns, lefts, lasting, values, heard = refs[3 * blocks + 1 : -2]
    index_ref, sem = refs[-2:]
    fetch = pltpu.make_async_copy(index_far, index_ref, sem)
    fetch.start()
    count = blocks * reqs
    head_size = pool.shape[-1]
    rows = reqs * head_size

    for s in range(blocks):
        flat[...] = own[s][rows:, :].astype(F32)
        for part in range(3):
            for t in range(steps):
                gathered[part * steps + t, pl.ds(s * reqs, reqs), :] = flat[
                    pl.ds(part * reqs * steps + t, reqs, stride=steps), :
                ]
        for r in range(reqs):
            here = slice(r * head_size, (r + 1) * head_size)
            pool[s * reqs + r] = own[s][here, :]
            pool[(blocks + s) * reqs + r] = sib[s][here, :]
    base = 3 * steps * reqs
    bias = flat[base : base + 1, :] + flat[base + 1 : base + 2, :] + flat[base + 2 : base + 3, :]
    gain = flat[base + 3 : base + 4, :] + flat[base + 4 : base + 5, :] + flat[base + 5 : base + 6, :]
    live = live_ref[...]
    query = [gathered[t] for t in range(steps)]
    keep = [jax.nn.sigmoid(gathered[steps + t] + bias) for t in range(steps)]
    inputs = [gathered[2 * steps + t] for t in range(steps)]

    weights = []
    decay = live
    for t in range(steps):
        weights = [w * keep[t] for w in weights] + [1.0 - keep[t]]
        decay = decay * keep[t]
        lefts[pl.ds(t * count, count), :] = query[t] * decay
        out = jnp.zeros_like(query[t])
        for earlier in range(t + 1):
            score = jnp.sum(query[t] * weights[earlier], axis=-1, keepdims=True)
            out = out + score * inputs[earlier]
        heard[pl.ds(t, count, stride=steps), :] = out

    columns[...] = jnp.zeros_like(columns)
    columns[pl.ds(0, count), :] = decay
    turned = columns[...].T
    for s in range(blocks):
        mine = slice(s * reqs, (s + 1) * reqs)
        for t in range(steps):
            here = pl.ds((s * steps + t) * reqs, reqs)
            values[here, :] = inputs[t][mine, :]
            lasting[here, :] = weights[t][mine, :]

    fetch.wait()
    of_req = lax.broadcasted_iota(jnp.int32, (steps * reqs, head_size), 0) % reqs
    for s in range(blocks):
        here = slice(s * steps * reqs, (s + 1) * steps * reqs)
        left = lasting[here, :]
        high = left.astype(BF16)
        low = (left - high.astype(F32)).astype(BF16)
        value = values[here, :]
        spread = [jnp.where(of_req == r, value, 0.0).astype(BF16) for r in range(reqs)]
        spread = jnp.concatenate(spread, axis=1)
        added = lax.dot_general(
            jnp.concatenate([high, low], axis=0),
            jnp.concatenate([spread, spread], axis=0),
            (((0,), (0,)), ((), ())),
            preferred_element_type=F32,
        )
        for r in range(reqs):
            i = s * reqs + r
            old = pool[index_ref[i]]
            wanted = lefts[pl.ds(i, steps, stride=count), :].astype(BF16)
            said = jnp.dot(wanted, old, preferred_element_type=F32)
            heard[pl.ds(i * steps, steps), :] += said
            span = slice(r * head_size, (r + 1) * head_size)
            current = turned[:, i : i + 1] * old.astype(F32) + added[:, span]
            outs[s][span, :] = current.astype(BF16)

    head_out = heard[...]
    scale = lax.rsqrt(jnp.mean(head_out * head_out, axis=-1, keepdims=True) + 1e-06)
    normed = (head_out * scale * gain).astype(BF16)
    for s in range(blocks):
        outs[s][rows:, :] = normed[s * reqs * steps : (s + 1) * reqs * steps]


def middle(index, own, sib, live, reqs, steps):
    blocks = len(own)
    count = blocks * reqs
    head_size = own[0].shape[-1]
    extra = own[0].shape[0] - reqs * head_size
    columns = -(-count // 128) * 128
    spec = pl.BlockSpec(memory_space=VMEM)
    table = VMEM((steps * count, head_size), F32)
    return pl.pallas_call(
        functools.partial(middle_kernel, blocks, reqs, steps),
        out_shape=[VMEM((reqs * (head_size + steps), head_size), BF16)] * blocks,
        in_specs=[pl.BlockSpec(memory_space=pl.ANY)] + [spec] * (2 * blocks + 1),
        out_specs=[spec] * blocks,
        scratch_shapes=[
            VMEM((2 * count, head_size, head_size), BF16),
            VMEM((extra, head_size), F32),
            VMEM((3 * steps, count, head_size), F32),
            VMEM((columns, head_size), F32),
            table,
            table,
            table,
            table,
            pltpu.SMEM(index.shape, jnp.int32),
            pltpu.SemaphoreType.DMA(()),
        ],
        name="middle",
        compiler_params=PARAMS,
    )(index, *on_chip(*[own[s] for s in order_out(blocks)], *[sib[s] for s in order_out(blocks)], live))


def fetch_kernel(far_ref, out, sem):
    copy = pltpu.make_async_copy(far_ref, out, sem)
    copy.start()
    copy.wait()


def fetch(value):
    return pl.pallas_call(
        fetch_kernel,
        out_shape=VMEM(value.shape, value.dtype),
        in_specs=[pl.BlockSpec(memory_space=pl.ANY)],
        out_specs=pl.BlockSpec(memory_space=VMEM),
        scratch_shapes=[pltpu.SemaphoreType.DMA(())],
        name="fetch",
        compiler_params=PARAMS,
    )(pltpu.with_memory_space_constraint(value, pltpu.HBM))


def project_kernel(blocks, *refs):
    parts, weight, out, left = in_order(refs[:blocks], order_back(blocks)), refs[blocks], refs[blocks + 1], refs[blocks + 2]
    rows, head_size = out.shape[0], parts[0].shape[-1]
    z = lax.axis_index("req") // 2
    for s in range(blocks):
        lanes = pl.ds(pl.multiple_of((z ^ s) * head_size, head_size), head_size)
        left[:, lanes] = parts[s][parts[s].shape[0] - rows :, :]
    out[...] = jnp.dot(left[...], weight[...], preferred_element_type=F32).astype(BF16)


def project(parts, weight, rows):
    spec = pl.BlockSpec(memory_space=VMEM)
    return pl.pallas_call(
        functools.partial(project_kernel, len(parts)),
        out_shape=VMEM((rows, weight.shape[1]), BF16),
        in_specs=[spec] * (len(parts) + 1),
        out_specs=spec,
        scratch_shapes=[VMEM((rows, weight.shape[0]), BF16)],
        name="project",
        compiler_params=PARAMS,
    )(*on_chip(*[parts[s] for s in order_back(len(parts))], weight))


def place_kernel(blocks, *refs):
    parts, out, sems = in_order(refs[:blocks], order_back(blocks)), refs[blocks], refs[blocks + 1]
    reqs, _, head_size, _ = out.shape
    z = lax.axis_index("req") // 2
    copies = []
    for s in range(blocks):
        for r in range(reqs):
            copy = pltpu.make_async_copy(
                parts[s].at[pl.ds(r * head_size, head_size), :],
                out.at[r, z ^ s],
                sems.at[s * reqs + r],
            )
            copy.start()
            copies.append(copy)
    for copy in copies:
        copy.wait()


def place(back, shape):
    return pl.pallas_call(
        functools.partial(place_kernel, len(back)),
        out_shape=jax.ShapeDtypeStruct(shape, BF16),
        in_specs=[pl.BlockSpec(memory_space=VMEM)] * len(back),
        out_specs=pl.BlockSpec(memory_space=pl.ANY),
        scratch_shapes=[pltpu.SemaphoreType.DMA((len(back) * shape[0],))],
        name="place",
        compiler_params=PARAMS,
    )(*on_chip(*[back[s] for s in order_back(len(back))]))


def add_kernel(resid, *refs):
    out = refs[-1]
    total = [value[...].astype(F32) for value in refs[:-1]]
    while len(total) > 1:
        total = [total[k] + total[k + 1] for k in range(0, len(total), 2)]
    reqs = resid.shape[0]
    steps = total[0].shape[0] // reqs
    for r in range(reqs):
        out[r] = (resid[r].astype(F32) + total[0][r * steps : (r + 1) * steps, :]).astype(BF16)


def add(resid, terms):
    spec = pl.BlockSpec(memory_space=VMEM)
    return pl.pallas_call(
        add_kernel,
        out_shape=jax.ShapeDtypeStruct(resid.shape, BF16),
        in_specs=[spec] * (1 + len(terms)),
        out_specs=spec,
        name="add",
        compiler_params=PARAMS,
    )(*on_chip(resid, *terms))


def order_out(blocks):
    half = blocks // 2
    return (blocks - 1, *range(half - 1, -1, -1), *range(half, blocks - 1))


def order_back(blocks):
    return tuple(range(blocks - 1, -1, -1))


def in_order(refs, order):
    return [refs[order.index(s)] for s in range(len(refs))]


def on_chip(*arrays):
    return [pltpu.with_memory_space_constraint(value, VMEM) for value in arrays]


def swapped_body(
    resid, proj, conv_cache, conv_weight, forget_bias, owner, lengths, old_state, norm_gain, out_weight
):
    local_reqs, steps, width = resid.shape
    blocks = old_state.shape[1]
    head_size = old_state.shape[-1]
    n_head = lax.axis_size("head")
    own_req = lax.axis_index("req")
    own_head = lax.axis_index("head")
    z, core = own_req // 2, own_head % 2

    both = ("req", "head")
    sibling = [(i, i ^ 1) for i in range(n_head)]

    def swap(value, s):
        pairs = [
            ((a * 2 + b) * n_head + y * 2 + c, ((a ^ s) * 2 + c) * n_head + y * 2 + b)
            for a in range(blocks)
            for b in range(2)
            for y in range(n_head // 2)
            for c in range(2)
        ]
        return lax.ppermute(value, both, pairs)

    packs = pack(lengths, proj, conv_cache, conv_weight, forget_bias, norm_gain, old_state)
    own = [swap(packs[s], s) for s in range(blocks)]
    sib = [lax.ppermute(own[s], "head", sibling) for s in range(blocks)]

    zs = z ^ jnp.arange(blocks, dtype=jnp.int32)
    slots = ((zs * 2 + core) * local_reqs)[:, None] + jnp.arange(local_reqs, dtype=jnp.int32)[None, :]
    slots = slots.reshape(-1)
    every = jnp.arange(owner.shape[0], dtype=jnp.int32)[None, :]
    source = jnp.sum(jnp.where(owner[None, :] == slots[:, None], every, 0), axis=1)
    device, pos = source // local_reqs, source % local_reqs
    away = (device % 2 != core).astype(jnp.int32)
    index = (away * blocks + ((device // 2) ^ z)) * local_reqs + pos
    lens = jnp.sum(jnp.where(every == slots[:, None], lengths[None, :], 0), axis=1)
    live = jnp.broadcast_to((lens > 0).astype(F32)[:, None], (slots.shape[0], head_size))

    states = middle(index, own, sib, live, local_reqs, steps)
    back = [swap(states[s], s) for s in range(blocks)]
    weight, *_ = lax.optimization_barrier((out_weight, *states))
    part = project(back, fetch(weight), local_reqs * steps)
    terms = [part] + [
        lax.ppermute(part, "head", [(i, i ^ k) for i in range(n_head)]) for k in range(1, n_head)
    ]
    held = lax.optimization_barrier((*back, part))
    new_state = place(held[:blocks], old_state.shape)
    return add(resid, terms), new_state


def solution(mesh):
    in_specs = (
        P("req", None, None),
        P("req", None, None, "head"),
        P("req", None, None, "head"),
        P(None, None, "head"),
        P("head"),
        P(),
        P(),
        P("req", "head", None, None),
        P("head"),
        P("head", None),
    )
    out_specs = (P("req", None, None), P("req", "head", None, None))

    def body(*args):
        heads = args[7].shape[1]
        swapped = (
            mesh.shape["req"] == 2 * heads and heads & (heads - 1) == 0 and mesh.shape["head"] == 4
        )
        return (swapped_body if swapped else generic_body)(*args)

    return jax.shard_map(body, mesh=mesh, in_specs=in_specs, out_specs=out_specs, check_vma=False)
```

```python
import functools

import jax
import jax.numpy as jnp
from jax import lax
from jax.experimental import pallas as pl
from jax.experimental.pallas import tpu as pltpu
from jax.sharding import PartitionSpec as P

BF16 = jnp.bfloat16
F32 = jnp.float32
VMEM = pltpu.VMEM
PARAMS = pltpu.CompilerParams(vmem_limit_bytes=16 * 2**20)


def convolve(proj, conv_cache, conv_weight, lens):
    taps = conv_weight.shape[0]
    new_tokens = proj.shape[1]
    joined = jnp.concatenate([conv_cache, proj], axis=1).astype(F32)
    places = lens[:, None] + jnp.arange(-(taps - 1), new_tokens, dtype=jnp.int32)[None, :]
    joined = jnp.where((places >= 0)[:, :, None, None], joined, F32(0.0))
    summed = jnp.zeros(proj.shape, F32)
    for offset in range(taps):
        begin_at = taps - 1 - offset
        summed = summed + joined[:, begin_at : begin_at + new_tokens] * conv_weight[offset].astype(F32)
    return jax.nn.silu(summed).astype(BF16)


def recurrence(convolved, relocated, lens, forget_bias, norm_gain, head_size):
    local_reqs, new_tokens, _, channels = convolved.shape
    head_count = channels // head_size
    values = convolved.astype(F32).reshape(local_reqs, new_tokens, 3, head_count, head_size)
    queries = values[:, :, 0]
    keep_rate = jax.nn.sigmoid(values[:, :, 1] + forget_bias.reshape(head_count, head_size))
    inputs = values[:, :, 2]
    current = relocated.astype(F32) * (lens > 0).astype(F32)[:, None, None, None]
    outputs = []
    for position in range(new_tokens):
        rate_now = keep_rate[:, position]
        current = (
            rate_now[..., None] * current
            + (1.0 - rate_now)[..., None] * inputs[:, position][:, :, None, :]
        )
        outputs.append(jnp.einsum("rhk,rhkv->rhv", queries[:, position], current))
    stacked = jnp.stack(outputs, axis=1)
    inverse_rms = lax.rsqrt(jnp.mean(stacked * stacked, axis=-1, keepdims=True) + 1e-06)
    normed = (stacked * inverse_rms).reshape(local_reqs, new_tokens, channels) * norm_gain
    return (normed.astype(BF16), current.astype(BF16))


def generic_body(
    resid, proj, conv_cache, conv_weight, forget_bias, owner, lengths, old_state, norm_gain, out_weight
):
    local_reqs, new_tokens = resid.shape[:2]
    devices = lax.axis_size("req")
    own_index = lax.axis_index("req")
    total_reqs = owner.shape[0]
    head_size = old_state.shape[-1]
    inverse = (
        jnp.zeros((total_reqs,), jnp.int32).at[owner].set(jnp.arange(total_reqs, dtype=jnp.int32))
    )
    local_lens = lax.dynamic_slice_in_dim(lengths, own_index * local_reqs, local_reqs)
    convolved = convolve(proj, conv_cache, conv_weight, local_lens)
    pieces = old_state.reshape(local_reqs, devices, -1)
    spread = lax.all_to_all(pieces, "req", split_axis=1, concat_axis=0, tiled=True)
    spread = spread.reshape(total_reqs, -1)
    picked = jnp.take(spread, inverse, axis=0).reshape(devices, local_reqs, 1, -1)
    routed = lax.all_to_all(picked, "req", split_axis=0, concat_axis=2, tiled=True)
    relocated = routed.reshape(old_state.shape)
    normed, new_state = recurrence(
        convolved, relocated, local_lens, forget_bias, norm_gain, head_size
    )
    flat_normed = normed.reshape(local_reqs * new_tokens, -1)
    flat_resid = resid.reshape(local_reqs * new_tokens, -1)
    partial_value = jnp.dot(flat_normed, out_weight, preferred_element_type=F32)
    summed = lax.psum(partial_value, "head")
    mixed = (flat_resid.astype(F32) + summed).astype(BF16).reshape(resid.shape)
    return (mixed, new_state)


def pack_kernel(blocks, state_ref, *refs):
    outs, sems = refs[:blocks], refs[blocks]
    reqs, head_size = state_ref.shape[0], state_ref.shape[-1]
    z = lax.axis_index("req") // 2
    copies = []
    for s in range(blocks - 1, -1, -1):
        for r in range(reqs):
            copy = pltpu.make_async_copy(
                state_ref.at[r, z ^ s],
                outs[s].at[pl.ds(r * head_size, head_size), :],
                sems.at[s * reqs + r],
            )
            copy.start()
            copies.append(copy)
    for copy in copies:
        copy.wait()


def pack(old_state):
    reqs, blocks, head_size, _ = old_state.shape
    return pl.pallas_call(
        functools.partial(pack_kernel, blocks),
        out_shape=[VMEM((reqs * head_size, head_size), BF16)] * blocks,
        in_specs=[pl.BlockSpec(memory_space=pl.ANY)],
        out_specs=[pl.BlockSpec(memory_space=VMEM)] * blocks,
        scratch_shapes=[pltpu.SemaphoreType.DMA((blocks * reqs,))],
        name="pack",
    )(old_state)


def prepare_kernel(blocks, lens_ref, *refs):
    proj_ref, cache_ref, weight_ref, bias_ref = refs[:4]
    turned, lefts, lasting, values, heard = refs[4:9]
    joined, conv, flat, columns = refs[9:]
    reqs, _, steps, _ = proj_ref.shape
    head_size = turned.shape[0]
    req = lax.axis_index("req")
    z = req // 2
    taps = weight_ref.shape[1]
    past = taps - 1
    row = lax.broadcasted_iota(jnp.int32, (reqs, head_size), 0)
    live = jnp.zeros((reqs, head_size), F32)
    for r in range(reqs):
        live = jnp.where(row == r, (lens_ref[req * reqs + r] > 0).astype(F32), live)

    for p in range(3):
        weight = weight_ref[p].astype(F32)
        old = [cache_ref[j, p].astype(F32) for j in range(past)]
        for r in range(reqs):
            length = lens_ref[req * reqs + r]
            own = p * reqs + r
            for j in range(past):
                seen = (length >= past - j).astype(F32)
                joined[own, j : j + 1, :] = old[j][r : r + 1, :] * seen
            joined[own, past : past + steps, :] = proj_ref[r, p].astype(F32)
            total = joined[own, past : past + steps, :] * weight[0:1, :]
            for tap in range(1, taps):
                begin = past - tap
                total = total + joined[own, begin : begin + steps, :] * weight[tap : tap + 1, :]
            at = own * steps
            conv[at : at + steps, :] = total / (1.0 + jnp.exp(-total))

    columns[...] = jnp.zeros_like(columns)
    for s in range(blocks):
        head = z ^ s
        lanes = pl.ds(pl.multiple_of(head * head_size, head_size), head_size)
        flat[...] = conv[:, lanes].astype(BF16).astype(F32)
        parts = [
            [flat[pl.ds(p * reqs * steps + t, reqs, stride=steps), :] for t in range(steps)]
            for p in range(3)
        ]
        query, inputs = parts[0], parts[2]
        bias = bias_ref[pl.ds(head, 1), :]
        keep = [jax.nn.sigmoid(gate + bias) for gate in parts[1]]
        base = s * steps * reqs
        weights = []
        decay = live
        for t in range(steps):
            weights = [w * keep[t] for w in weights] + [1.0 - keep[t]]
            decay = decay * keep[t]
            lefts[pl.ds(base + t * reqs, reqs), :] = query[t] * decay
            values[pl.ds(base + t * reqs, reqs), :] = inputs[t]
            out = jnp.zeros_like(query[t])
            for earlier in range(t + 1):
                score = jnp.sum(query[t] * weights[earlier], axis=-1, keepdims=True)
                out = out + score * inputs[earlier]
            heard[pl.ds(base + t, reqs, stride=steps), :] = out
        for t in range(steps):
            lasting[pl.ds(base + t * reqs, reqs), :] = weights[t]
        columns[pl.ds(s * reqs, reqs), :] = decay
    turned[...] = columns[...].T


def prepare(lengths, proj, conv_cache, conv_weight, forget_bias, blocks, head_size):
    reqs, steps, _, width = proj.shape
    taps = conv_weight.shape[0]
    columns = -(-blocks * reqs // 128) * 128
    spec = pl.BlockSpec(memory_space=VMEM)
    table = VMEM((blocks * steps * reqs, head_size), F32)
    return pl.pallas_call(
        functools.partial(prepare_kernel, blocks),
        out_shape=[VMEM((head_size, columns), F32)] + [table] * 4,
        in_specs=[pl.BlockSpec(memory_space=pltpu.SMEM)] + [spec] * 4,
        out_specs=[spec] * 5,
        scratch_shapes=[
            VMEM((3 * reqs, taps + steps, width), F32),
            VMEM((3 * reqs * steps, width), F32),
            VMEM((3 * reqs * steps, head_size), F32),
            VMEM((columns, head_size), F32),
        ],
        name="prepare",
    )(
        lengths,
        proj.transpose(0, 2, 1, 3),
        conv_cache.transpose(1, 2, 0, 3),
        conv_weight.transpose(1, 0, 2),
        forget_bias.reshape(blocks, head_size),
    )


def route_kernel(blocks, index_far, *refs):
    own = in_order(refs[:blocks], order_out(blocks))
    sib = in_order(refs[blocks : 2 * blocks], order_out(blocks))
    outs = refs[2 * blocks : 3 * blocks]
    pool, index_ref, sem = refs[3 * blocks :]
    fetch = pltpu.make_async_copy(index_far, index_ref, sem)
    fetch.start()
    head_size = pool.shape[-1]
    reqs = outs[0].shape[0] // head_size
    for s in range(blocks):
        for r in range(reqs):
            here = slice(r * head_size, (r + 1) * head_size)
            pool[s * reqs + r] = own[s][here, :]
            pool[(blocks + s) * reqs + r] = sib[s][here, :]
    fetch.wait()
    for s in range(blocks):
        for r in range(reqs):
            outs[s][r * head_size : (r + 1) * head_size, :] = pool[index_ref[s * reqs + r]]


def route(index, own, sib):
    blocks = len(own)
    rows, head_size = own[0].shape
    spec = pl.BlockSpec(memory_space=VMEM)
    return pl.pallas_call(
        functools.partial(route_kernel, blocks),
        out_shape=[VMEM((rows, head_size), BF16)] * blocks,
        in_specs=[pl.BlockSpec(memory_space=pl.ANY)] + [spec] * (2 * blocks),
        out_specs=[spec] * blocks,
        scratch_shapes=[
            VMEM((2 * blocks * rows // head_size, head_size, head_size), BF16),
            pltpu.SMEM(index.shape, jnp.int32),
            pltpu.SemaphoreType.DMA(()),
        ],
        name="route",
        compiler_params=PARAMS,
    )(index, *on_chip(*[own[s] for s in order_out(blocks)], *[sib[s] for s in order_out(blocks)]))


def fetch_kernel(far_ref, out, sem):
    copy = pltpu.make_async_copy(far_ref, out, sem)
    copy.start()
    copy.wait()


def fetch(value):
    return pl.pallas_call(
        fetch_kernel,
        out_shape=VMEM(value.shape, value.dtype),
        in_specs=[pl.BlockSpec(memory_space=pl.ANY)],
        out_specs=pl.BlockSpec(memory_space=VMEM),
        scratch_shapes=[pltpu.SemaphoreType.DMA(())],
        name="fetch",
        compiler_params=PARAMS,
    )(pltpu.with_memory_space_constraint(value, pltpu.HBM))


def home_kernel(blocks, reqs, steps, *refs):
    back = in_order(refs[:blocks], order_back(blocks))
    turned_ref, lefts, lasting, values, heard_in, gain_ref, weight = refs[blocks : blocks + 7]
    outs = refs[blocks + 7 : 2 * blocks + 7]
    part = refs[2 * blocks + 7]
    heard, normed = refs[2 * blocks + 8 :]
    head_size = turned_ref.shape[0]
    z = lax.axis_index("req") // 2
    turned = turned_ref[...]
    heard[...] = heard_in[...]
    of_req = lax.broadcasted_iota(jnp.int32, (steps * reqs, head_size), 0) % reqs
    for s in range(blocks):
        here = slice(s * steps * reqs, (s + 1) * steps * reqs)
        left = lasting[here, :]
        high = left.astype(BF16)
        low = (left - high.astype(F32)).astype(BF16)
        value = values[here, :]
        spread = [jnp.where(of_req == r, value, 0.0).astype(BF16) for r in range(reqs)]
        spread = jnp.concatenate(spread, axis=1)
        added = lax.dot_general(
            jnp.concatenate([high, low], axis=0),
            jnp.concatenate([spread, spread], axis=0),
            (((0,), (0,)), ((), ())),
            preferred_element_type=F32,
        )
        for r in range(reqs):
            i = s * reqs + r
            span = slice(r * head_size, (r + 1) * head_size)
            old = back[s][span, :]
            wanted = lefts[pl.ds(here.start + r, steps, stride=reqs), :].astype(BF16)
            said = jnp.dot(wanted, old, preferred_element_type=F32)
            heard[pl.ds(i * steps, steps), :] += said
            current = turned[:, i : i + 1] * old.astype(F32) + added[:, span]
            outs[s][span, :] = current.astype(BF16)
        head_out = heard[here, :]
        scale = lax.rsqrt(jnp.mean(head_out * head_out, axis=-1, keepdims=True) + 1e-06)
        gain = gain_ref[pl.ds(z ^ s, 1), :]
        lanes = pl.ds(pl.multiple_of((z ^ s) * head_size, head_size), head_size)
        normed[:, lanes] = (head_out * scale * gain).astype(BF16)
    part[...] = jnp.dot(normed[...], weight[...], preferred_element_type=F32).astype(BF16)


def home(back, prepared, norm_gain, weight, reqs, steps):
    blocks = len(back)
    head_size = back[0].shape[-1]
    spec = pl.BlockSpec(memory_space=VMEM)
    gain = norm_gain.reshape(blocks, head_size)
    *states, part = pl.pallas_call(
        functools.partial(home_kernel, blocks, reqs, steps),
        out_shape=[VMEM(back[0].shape, BF16)] * blocks
        + [VMEM((reqs * steps, weight.shape[1]), BF16)],
        in_specs=[spec] * (blocks + 7),
        out_specs=[spec] * (blocks + 1),
        scratch_shapes=[
            VMEM((blocks * reqs * steps, head_size), F32),
            VMEM((reqs * steps, weight.shape[0]), BF16),
        ],
        name="home",
        compiler_params=PARAMS,
    )(*on_chip(*[back[s] for s in order_back(blocks)], *prepared, gain, weight))
    return states, part


def place_kernel(blocks, *refs):
    parts, out, sems = in_order(refs[:blocks], order_back(blocks)), refs[blocks], refs[blocks + 1]
    reqs, _, head_size, _ = out.shape
    z = lax.axis_index("req") // 2
    copies = []
    for s in range(blocks):
        for r in range(reqs):
            copy = pltpu.make_async_copy(
                parts[s].at[pl.ds(r * head_size, head_size), :],
                out.at[r, z ^ s],
                sems.at[s * reqs + r],
            )
            copy.start()
            copies.append(copy)
    for copy in copies:
        copy.wait()


def place(back, shape):
    return pl.pallas_call(
        functools.partial(place_kernel, len(back)),
        out_shape=jax.ShapeDtypeStruct(shape, BF16),
        in_specs=[pl.BlockSpec(memory_space=VMEM)] * len(back),
        out_specs=pl.BlockSpec(memory_space=pl.ANY),
        scratch_shapes=[pltpu.SemaphoreType.DMA((len(back) * shape[0],))],
        name="place",
        compiler_params=PARAMS,
    )(*on_chip(*[back[s] for s in order_back(len(back))]))


def add_kernel(resid, *refs):
    out = refs[-1]
    total = [value[...].astype(F32) for value in refs[:-1]]
    while len(total) > 1:
        total = [total[k] + total[k + 1] for k in range(0, len(total), 2)]
    reqs = resid.shape[0]
    steps = total[0].shape[0] // reqs
    for r in range(reqs):
        out[r] = (resid[r].astype(F32) + total[0][r * steps : (r + 1) * steps, :]).astype(BF16)


def add(resid, terms):
    spec = pl.BlockSpec(memory_space=VMEM)
    return pl.pallas_call(
        add_kernel,
        out_shape=jax.ShapeDtypeStruct(resid.shape, BF16),
        in_specs=[spec] * (1 + len(terms)),
        out_specs=spec,
        name="add",
        compiler_params=PARAMS,
    )(*on_chip(resid, *terms))


def order_out(blocks):
    half = blocks // 2
    return (blocks - 1, *range(half - 1, -1, -1), *range(half, blocks - 1))


def order_back(blocks):
    return tuple(range(blocks - 1, -1, -1))


def in_order(refs, order):
    return [refs[order.index(s)] for s in range(len(refs))]


def on_chip(*arrays):
    return [pltpu.with_memory_space_constraint(value, VMEM) for value in arrays]


def swapped_body(
    resid, proj, conv_cache, conv_weight, forget_bias, owner, lengths, old_state, norm_gain, out_weight
):
    local_reqs, steps, width = resid.shape
    blocks = old_state.shape[1]
    head_size = old_state.shape[-1]
    n_head = lax.axis_size("head")
    own_req = lax.axis_index("req")
    own_head = lax.axis_index("head")
    z, core = own_req // 2, own_head % 2

    both = ("req", "head")
    sibling = [(i, i ^ 1) for i in range(n_head)]

    def swap(value, s):
        pairs = [
            ((a * 2 + b) * n_head + y * 2 + c, ((a ^ s) * 2 + c) * n_head + y * 2 + b)
            for a in range(blocks)
            for b in range(2)
            for y in range(n_head // 2)
            for c in range(2)
        ]
        return lax.ppermute(value, both, pairs)

    packs = pack(old_state)
    own = [swap(packs[s], s) for s in range(blocks)]
    proj, conv_cache, conv_weight, forget_bias, norm_gain, *_ = lax.optimization_barrier(
        (proj, conv_cache, conv_weight, forget_bias, norm_gain, *packs)
    )
    prepared = prepare(lengths, proj, conv_cache, conv_weight, forget_bias, blocks, head_size)
    sib = [lax.ppermute(own[s], "head", sibling) for s in range(blocks)]

    zs = z ^ jnp.arange(blocks, dtype=jnp.int32)
    slots = ((zs * 2 + core) * local_reqs)[:, None] + jnp.arange(local_reqs, dtype=jnp.int32)[None, :]
    slots = slots.reshape(-1)
    every = jnp.arange(owner.shape[0], dtype=jnp.int32)[None, :]
    source = jnp.sum(jnp.where(owner[None, :] == slots[:, None], every, 0), axis=1)
    device, pos = source // local_reqs, source % local_reqs
    away = (device % 2 != core).astype(jnp.int32)
    index = (away * blocks + ((device // 2) ^ z)) * local_reqs + pos

    routed = route(index, own, sib)
    back = [swap(routed[s], s) for s in range(blocks)]
    weight, *_ = lax.optimization_barrier((out_weight, *routed))
    states, part = home(back, prepared, norm_gain, fetch(weight), local_reqs, steps)
    terms = [part] + [
        lax.ppermute(part, "head", [(i, i ^ k) for i in range(n_head)]) for k in range(1, n_head)
    ]
    held = lax.optimization_barrier((*states, part))
    new_state = place(held[:blocks], old_state.shape)
    return add(resid, terms), new_state


def solution(mesh):
    in_specs = (
        P("req", None, None),
        P("req", None, None, "head"),
        P("req", None, None, "head"),
        P(None, None, "head"),
        P("head"),
        P(),
        P(),
        P("req", "head", None, None),
        P("head"),
        P("head", None),
    )
    out_specs = (P("req", None, None), P("req", "head", None, None))

    def body(*args):
        heads = args[7].shape[1]
        swapped = (
            mesh.shape["req"] == 2 * heads and heads & (heads - 1) == 0 and mesh.shape["head"] == 4
        )
        return (swapped_body if swapped else generic_body)(*args)

    return jax.shard_map(body, mesh=mesh, in_specs=in_specs, out_specs=out_specs, check_vma=False)
```

```python
import functools

import jax
import jax.numpy as jnp
from jax import lax
from jax.experimental import pallas as pl
from jax.experimental.pallas import tpu as pltpu
from jax.sharding import PartitionSpec as P

BF16 = jnp.bfloat16
F32 = jnp.float32
VMEM = pltpu.VMEM
PARAMS = pltpu.CompilerParams(vmem_limit_bytes=16 * 2**20)


def convolve(proj, conv_cache, conv_weight, lens):
    taps = conv_weight.shape[0]
    new_tokens = proj.shape[1]
    joined = jnp.concatenate([conv_cache, proj], axis=1).astype(F32)
    places = lens[:, None] + jnp.arange(-(taps - 1), new_tokens, dtype=jnp.int32)[None, :]
    joined = jnp.where((places >= 0)[:, :, None, None], joined, F32(0.0))
    summed = jnp.zeros(proj.shape, F32)
    for offset in range(taps):
        begin_at = taps - 1 - offset
        summed = summed + joined[:, begin_at : begin_at + new_tokens] * conv_weight[offset].astype(F32)
    return jax.nn.silu(summed).astype(BF16)


def recurrence(convolved, relocated, lens, forget_bias, norm_gain, head_size):
    local_reqs, new_tokens, _, channels = convolved.shape
    head_count = channels // head_size
    values = convolved.astype(F32).reshape(local_reqs, new_tokens, 3, head_count, head_size)
    queries = values[:, :, 0]
    keep_rate = jax.nn.sigmoid(values[:, :, 1] + forget_bias.reshape(head_count, head_size))
    inputs = values[:, :, 2]
    current = relocated.astype(F32) * (lens > 0).astype(F32)[:, None, None, None]
    outputs = []
    for position in range(new_tokens):
        rate_now = keep_rate[:, position]
        current = (
            rate_now[..., None] * current
            + (1.0 - rate_now)[..., None] * inputs[:, position][:, :, None, :]
        )
        outputs.append(jnp.einsum("rhk,rhkv->rhv", queries[:, position], current))
    stacked = jnp.stack(outputs, axis=1)
    inverse_rms = lax.rsqrt(jnp.mean(stacked * stacked, axis=-1, keepdims=True) + 1e-06)
    normed = (stacked * inverse_rms).reshape(local_reqs, new_tokens, channels) * norm_gain
    return (normed.astype(BF16), current.astype(BF16))


def generic_body(
    resid, proj, conv_cache, conv_weight, forget_bias, owner, lengths, old_state, norm_gain, out_weight
):
    local_reqs, new_tokens = resid.shape[:2]
    devices = lax.axis_size("req")
    own_index = lax.axis_index("req")
    total_reqs = owner.shape[0]
    head_size = old_state.shape[-1]
    inverse = (
        jnp.zeros((total_reqs,), jnp.int32).at[owner].set(jnp.arange(total_reqs, dtype=jnp.int32))
    )
    local_lens = lax.dynamic_slice_in_dim(lengths, own_index * local_reqs, local_reqs)
    convolved = convolve(proj, conv_cache, conv_weight, local_lens)
    pieces = old_state.reshape(local_reqs, devices, -1)
    spread = lax.all_to_all(pieces, "req", split_axis=1, concat_axis=0, tiled=True)
    spread = spread.reshape(total_reqs, -1)
    picked = jnp.take(spread, inverse, axis=0).reshape(devices, local_reqs, 1, -1)
    routed = lax.all_to_all(picked, "req", split_axis=0, concat_axis=2, tiled=True)
    relocated = routed.reshape(old_state.shape)
    normed, new_state = recurrence(
        convolved, relocated, local_lens, forget_bias, norm_gain, head_size
    )
    flat_normed = normed.reshape(local_reqs * new_tokens, -1)
    flat_resid = resid.reshape(local_reqs * new_tokens, -1)
    partial_value = jnp.dot(flat_normed, out_weight, preferred_element_type=F32)
    summed = lax.psum(partial_value, "head")
    mixed = (flat_resid.astype(F32) + summed).astype(BF16).reshape(resid.shape)
    return (mixed, new_state)


def pack_kernel(blocks, state_ref, *refs):
    outs, sems = refs[:blocks], refs[blocks]
    reqs, head_size = state_ref.shape[0], state_ref.shape[-1]
    z = lax.axis_index("req") // 2
    copies = []
    for s in range(blocks - 1, -1, -1):
        for r in range(reqs):
            copy = pltpu.make_async_copy(
                state_ref.at[r, z ^ s],
                outs[s].at[pl.ds(r * head_size, head_size), :],
                sems.at[s * reqs + r],
            )
            copy.start()
            copies.append(copy)
    for copy in copies:
        copy.wait()


def pack(old_state):
    reqs, blocks, head_size, _ = old_state.shape
    return pl.pallas_call(
        functools.partial(pack_kernel, blocks),
        out_shape=[VMEM((reqs * head_size, head_size), BF16)] * blocks,
        in_specs=[pl.BlockSpec(memory_space=pl.ANY)],
        out_specs=[pl.BlockSpec(memory_space=VMEM)] * blocks,
        scratch_shapes=[pltpu.SemaphoreType.DMA((blocks * reqs,))],
        name="pack",
    )(old_state)


def prepare_kernel(blocks, lens_ref, *refs):
    proj_ref, cache_ref, weight_ref, bias_ref = refs[:4]
    turned, lefts, lasting, values, heard = refs[4:9]
    joined, conv, flat, columns = refs[9:]
    reqs, _, steps, _ = proj_ref.shape
    head_size = turned.shape[0]
    req = lax.axis_index("req")
    z = req // 2
    taps = weight_ref.shape[1]
    past = taps - 1
    row = lax.broadcasted_iota(jnp.int32, (reqs, head_size), 0)
    live = jnp.zeros((reqs, head_size), F32)
    for r in range(reqs):
        live = jnp.where(row == r, (lens_ref[req * reqs + r] > 0).astype(F32), live)

    for p in range(3):
        weight = weight_ref[p].astype(F32)
        old = [cache_ref[j, p].astype(F32) for j in range(past)]
        for r in range(reqs):
            length = lens_ref[req * reqs + r]
            own = p * reqs + r
            for j in range(past):
                seen = (length >= past - j).astype(F32)
                joined[own, j : j + 1, :] = old[j][r : r + 1, :] * seen
            joined[own, past : past + steps, :] = proj_ref[r, p].astype(F32)
            total = joined[own, past : past + steps, :] * weight[0:1, :]
            for tap in range(1, taps):
                begin = past - tap
                total = total + joined[own, begin : begin + steps, :] * weight[tap : tap + 1, :]
            at = own * steps
            conv[at : at + steps, :] = total / (1.0 + jnp.exp(-total))

    columns[...] = jnp.zeros_like(columns)
    for s in range(blocks):
        head = z ^ s
        lanes = pl.ds(pl.multiple_of(head * head_size, head_size), head_size)
        flat[...] = conv[:, lanes].astype(BF16).astype(F32)
        parts = [
            [flat[pl.ds(p * reqs * steps + t, reqs, stride=steps), :] for t in range(steps)]
            for p in range(3)
        ]
        query, inputs = parts[0], parts[2]
        bias = bias_ref[pl.ds(head, 1), :]
        keep = [jax.nn.sigmoid(gate + bias) for gate in parts[1]]
        base = s * steps * reqs
        weights = []
        decay = live
        for t in range(steps):
            weights = [w * keep[t] for w in weights] + [1.0 - keep[t]]
            decay = decay * keep[t]
            lefts[pl.ds(base + t * reqs, reqs), :] = query[t] * decay
            values[pl.ds(base + t * reqs, reqs), :] = inputs[t]
            out = jnp.zeros_like(query[t])
            for earlier in range(t + 1):
                score = jnp.sum(query[t] * weights[earlier], axis=-1, keepdims=True)
                out = out + score * inputs[earlier]
            heard[pl.ds(base + t, reqs, stride=steps), :] = out
        for t in range(steps):
            lasting[pl.ds(base + t * reqs, reqs), :] = weights[t]
        columns[pl.ds(s * reqs, reqs), :] = decay
    turned[...] = columns[...].T


def prepare(lengths, proj, conv_cache, conv_weight, forget_bias, blocks, head_size):
    reqs, steps, _, width = proj.shape
    taps = conv_weight.shape[0]
    columns = -(-blocks * reqs // 128) * 128
    spec = pl.BlockSpec(memory_space=VMEM)
    table = VMEM((blocks * steps * reqs, head_size), F32)
    return pl.pallas_call(
        functools.partial(prepare_kernel, blocks),
        out_shape=[VMEM((head_size, columns), F32)] + [table] * 4,
        in_specs=[pl.BlockSpec(memory_space=pltpu.SMEM)] + [spec] * 4,
        out_specs=[spec] * 5,
        scratch_shapes=[
            VMEM((3 * reqs, taps + steps, width), F32),
            VMEM((3 * reqs * steps, width), F32),
            VMEM((3 * reqs * steps, head_size), F32),
            VMEM((columns, head_size), F32),
        ],
        name="prepare",
    )(
        lengths,
        proj.transpose(0, 2, 1, 3),
        conv_cache.transpose(1, 2, 0, 3),
        conv_weight.transpose(1, 0, 2),
        forget_bias.reshape(blocks, head_size),
    )


def route_kernel(blocks, index_far, *refs):
    own = in_order(refs[:blocks], order_out(blocks))
    sib = in_order(refs[blocks : 2 * blocks], order_out(blocks))
    outs = refs[2 * blocks : 3 * blocks]
    pool, index_ref, sem = refs[3 * blocks :]
    fetch = pltpu.make_async_copy(index_far, index_ref, sem)
    fetch.start()
    head_size = pool.shape[-1]
    reqs = outs[0].shape[0] // head_size
    for s in range(blocks):
        for r in range(reqs):
            here = slice(r * head_size, (r + 1) * head_size)
            pool[s * reqs + r] = own[s][here, :]
            pool[(blocks + s) * reqs + r] = sib[s][here, :]
    fetch.wait()
    for s in range(blocks):
        for r in range(reqs):
            outs[s][r * head_size : (r + 1) * head_size, :] = pool[index_ref[s * reqs + r]]


def route(index, own, sib):
    blocks = len(own)
    rows, head_size = own[0].shape
    spec = pl.BlockSpec(memory_space=VMEM)
    return pl.pallas_call(
        functools.partial(route_kernel, blocks),
        out_shape=[VMEM((rows, head_size), BF16)] * blocks,
        in_specs=[pl.BlockSpec(memory_space=pl.ANY)] + [spec] * (2 * blocks),
        out_specs=[spec] * blocks,
        scratch_shapes=[
            VMEM((2 * blocks * rows // head_size, head_size, head_size), BF16),
            pltpu.SMEM(index.shape, jnp.int32),
            pltpu.SemaphoreType.DMA(()),
        ],
        name="route",
        compiler_params=PARAMS,
    )(index, *on_chip(*[own[s] for s in order_out(blocks)], *[sib[s] for s in order_out(blocks)]))


def fetch_kernel(far_ref, out, sem):
    copy = pltpu.make_async_copy(far_ref, out, sem)
    copy.start()
    copy.wait()


def fetch(value):
    return pl.pallas_call(
        fetch_kernel,
        out_shape=VMEM(value.shape, value.dtype),
        in_specs=[pl.BlockSpec(memory_space=pl.ANY)],
        out_specs=pl.BlockSpec(memory_space=VMEM),
        scratch_shapes=[pltpu.SemaphoreType.DMA(())],
        name="fetch",
        compiler_params=PARAMS,
    )(pltpu.with_memory_space_constraint(value, pltpu.HBM))


def home_kernel(blocks, reqs, steps, *refs):
    back = in_order(refs[:blocks], order_back(blocks))
    kept, lefts, heard_in, gain_ref, weight, part, heard, normed = refs[blocks:]
    stayed = lax.axis_index("req") % 2 == lax.axis_index("head") % 2
    head_size = gain_ref.shape[-1]
    z = lax.axis_index("req") // 2
    heard[...] = heard_in[...]
    for s in range(blocks):
        here = slice(s * steps * reqs, (s + 1) * steps * reqs)
        for r in range(reqs):
            span = slice(r * head_size, (r + 1) * head_size)
            old = back[s][span, :]
            if s == 0:
                old = jnp.where(stayed, kept[span, :], old)
            wanted = lefts[pl.ds(here.start + r, steps, stride=reqs), :].astype(BF16)
            said = jnp.dot(wanted, old, preferred_element_type=F32)
            heard[pl.ds((s * reqs + r) * steps, steps), :] += said
        head_out = heard[here, :]
        scale = lax.rsqrt(jnp.mean(head_out * head_out, axis=-1, keepdims=True) + 1e-06)
        gain = gain_ref[pl.ds(z ^ s, 1), :]
        lanes = pl.ds(pl.multiple_of((z ^ s) * head_size, head_size), head_size)
        normed[:, lanes] = (head_out * scale * gain).astype(BF16)
    part[...] = jnp.dot(normed[...], weight[...], preferred_element_type=F32).astype(BF16)


def home(back, kept, lefts, heard, norm_gain, weight, reqs, steps):
    blocks = len(back)
    head_size = back[0].shape[-1]
    spec = pl.BlockSpec(memory_space=VMEM)
    gain = norm_gain.reshape(blocks, head_size)
    return pl.pallas_call(
        functools.partial(home_kernel, blocks, reqs, steps),
        out_shape=VMEM((reqs * steps, weight.shape[1]), BF16),
        in_specs=[spec] * (blocks + 5),
        out_specs=spec,
        scratch_shapes=[
            VMEM((blocks * reqs * steps, head_size), F32),
            VMEM((reqs * steps, weight.shape[0]), BF16),
        ],
        name="home",
        compiler_params=PARAMS,
    )(*on_chip(*[back[s] for s in order_back(blocks)], kept, lefts, heard, gain, weight))


def place_kernel(blocks, reqs, steps, *refs):
    back = in_order(refs[:blocks], order_back(blocks))
    kept, turned_ref, lasting, values, out, fresh, sems = refs[blocks:]
    stayed = lax.axis_index("req") % 2 == lax.axis_index("head") % 2
    head_size = turned_ref.shape[0]
    z = lax.axis_index("req") // 2
    turned = turned_ref[...]
    of_req = lax.broadcasted_iota(jnp.int32, (steps * reqs, head_size), 0) % reqs
    copies = []
    for s in range(blocks):
        here = slice(s * steps * reqs, (s + 1) * steps * reqs)
        left = lasting[here, :]
        high = left.astype(BF16)
        low = (left - high.astype(F32)).astype(BF16)
        value = values[here, :]
        spread = [jnp.where(of_req == r, value, 0.0).astype(BF16) for r in range(reqs)]
        spread = jnp.concatenate(spread, axis=1)
        added = lax.dot_general(
            jnp.concatenate([high, low], axis=0),
            jnp.concatenate([spread, spread], axis=0),
            (((0,), (0,)), ((), ())),
            preferred_element_type=F32,
        )
        for r in range(reqs):
            i = s * reqs + r
            span = slice(r * head_size, (r + 1) * head_size)
            old = back[s][span, :]
            if s == 0:
                old = jnp.where(stayed, kept[span, :], old)
            current = turned[:, i : i + 1] * old.astype(F32) + added[:, span]
            fresh[i] = current.astype(BF16)
            copy = pltpu.make_async_copy(fresh.at[i], out.at[r, z ^ s], sems.at[i])
            copy.start()
            copies.append(copy)
    for copy in copies:
        copy.wait()


def place(back, kept, turned, lasting, values, shape, steps):
    reqs, blocks, head_size, _ = shape
    return pl.pallas_call(
        functools.partial(place_kernel, blocks, reqs, steps),
        out_shape=jax.ShapeDtypeStruct(shape, BF16),
        in_specs=[pl.BlockSpec(memory_space=VMEM)] * (blocks + 4),
        out_specs=pl.BlockSpec(memory_space=pl.ANY),
        scratch_shapes=[
            VMEM((blocks * reqs, head_size, head_size), BF16),
            pltpu.SemaphoreType.DMA((blocks * reqs,)),
        ],
        name="place",
        compiler_params=PARAMS,
    )(*on_chip(*[back[s] for s in order_back(blocks)], kept, turned, lasting, values))


def add_kernel(resid, *refs):
    out = refs[-1]
    total = [value[...].astype(F32) for value in refs[:-1]]
    while len(total) > 1:
        total = [total[k] + total[k + 1] for k in range(0, len(total), 2)]
    reqs = resid.shape[0]
    steps = total[0].shape[0] // reqs
    for r in range(reqs):
        out[r] = (resid[r].astype(F32) + total[0][r * steps : (r + 1) * steps, :]).astype(BF16)


def add(resid, terms):
    spec = pl.BlockSpec(memory_space=VMEM)
    return pl.pallas_call(
        add_kernel,
        out_shape=jax.ShapeDtypeStruct(resid.shape, BF16),
        in_specs=[spec] * (1 + len(terms)),
        out_specs=spec,
        name="add",
        compiler_params=PARAMS,
    )(*on_chip(resid, *terms))


def order_out(blocks):
    half = blocks // 2
    return (blocks - 1, *range(half - 1, -1, -1), *range(half, blocks - 1))


def order_back(blocks):
    return tuple(range(blocks - 1, -1, -1))


def in_order(refs, order):
    return [refs[order.index(s)] for s in range(len(refs))]


def on_chip(*arrays):
    return [pltpu.with_memory_space_constraint(value, VMEM) for value in arrays]


def swapped_body(
    resid, proj, conv_cache, conv_weight, forget_bias, owner, lengths, old_state, norm_gain, out_weight
):
    local_reqs, steps, width = resid.shape
    blocks = old_state.shape[1]
    head_size = old_state.shape[-1]
    n_head = lax.axis_size("head")
    own_req = lax.axis_index("req")
    own_head = lax.axis_index("head")
    z, core = own_req // 2, own_head % 2

    both = ("req", "head")
    sibling = [(i, i ^ 1) for i in range(n_head)]

    def swap(value, s, cross=False):
        pairs = []
        for a in range(blocks):
            for b in range(2):
                for y in range(n_head // 2):
                    for c in range(2):
                        to = (b ^ 1, c ^ 1) if cross else (c, b)
                        here = (a * 2 + b) * n_head + y * 2 + c
                        pairs.append((here, ((a ^ s) * 2 + to[0]) * n_head + y * 2 + to[1]))
        return lax.ppermute(value, both, pairs)

    packs = pack(old_state)
    own = [swap(packs[s], s) for s in range(blocks)]
    proj, conv_cache, conv_weight, forget_bias, norm_gain, *_ = lax.optimization_barrier(
        (proj, conv_cache, conv_weight, forget_bias, norm_gain, *packs)
    )
    prepared = prepare(lengths, proj, conv_cache, conv_weight, forget_bias, blocks, head_size)
    sib = [lax.ppermute(own[s], "head", sibling) for s in range(blocks)]

    zs = z ^ jnp.arange(blocks, dtype=jnp.int32)
    slots = ((zs * 2 + core) * local_reqs)[:, None] + jnp.arange(local_reqs, dtype=jnp.int32)[None, :]
    slots = slots.reshape(-1)
    every = jnp.arange(owner.shape[0], dtype=jnp.int32)[None, :]
    source = jnp.sum(jnp.where(owner[None, :] == slots[:, None], every, 0), axis=1)
    device, pos = source // local_reqs, source % local_reqs
    away = (device % 2 != core).astype(jnp.int32)
    index = (away * blocks + ((device // 2) ^ z)) * local_reqs + pos

    routed = route(index, own, sib)
    back = [swap(routed[s], s, cross=s == 0) for s in range(blocks)]
    weight, *_ = lax.optimization_barrier((out_weight, *routed))
    turned, lefts, lasting, values, heard = prepared
    weight = fetch(weight)
    part = home(back, routed[0], lefts, heard, norm_gain, weight, local_reqs, steps)
    terms = [part] + [
        lax.ppermute(part, "head", [(i, i ^ k) for i in range(n_head)]) for k in range(1, n_head)
    ]
    *back, part = lax.optimization_barrier((*back, part))
    new_state = place(back, routed[0], turned, lasting, values, old_state.shape, steps)
    return add(resid, terms), new_state


def solution(mesh):
    in_specs = (
        P("req", None, None),
        P("req", None, None, "head"),
        P("req", None, None, "head"),
        P(None, None, "head"),
        P("head"),
        P(),
        P(),
        P("req", "head", None, None),
        P("head"),
        P("head", None),
    )
    out_specs = (P("req", None, None), P("req", "head", None, None))

    def body(*args):
        heads, parts = args[7].shape[1], mesh.shape["head"]
        swapped = mesh.shape["req"] == 2 * heads and heads & (heads - 1) == 0
        swapped = swapped and parts > 1 and parts & (parts - 1) == 0
        return (swapped_body if swapped else generic_body)(*args)

    return jax.shard_map(body, mesh=mesh, in_specs=in_specs, out_specs=out_specs, check_vma=False)
```

```python
import functools

import jax
import jax.numpy as jnp
from jax import lax
from jax.experimental import pallas as pl
from jax.experimental.pallas import tpu as pltpu
from jax.sharding import PartitionSpec as P

BF16 = jnp.bfloat16
F32 = jnp.float32
VMEM = pltpu.VMEM
PARAMS = pltpu.CompilerParams(vmem_limit_bytes=16 * 2**20)


def convolve(proj, conv_cache, conv_weight, lens):
    taps = conv_weight.shape[0]
    new_tokens = proj.shape[1]
    joined = jnp.concatenate([conv_cache, proj], axis=1).astype(F32)
    places = lens[:, None] + jnp.arange(-(taps - 1), new_tokens, dtype=jnp.int32)[None, :]
    joined = jnp.where((places >= 0)[:, :, None, None], joined, F32(0.0))
    summed = jnp.zeros(proj.shape, F32)
    for offset in range(taps):
        begin_at = taps - 1 - offset
        summed = summed + joined[:, begin_at : begin_at + new_tokens] * conv_weight[offset].astype(F32)
    return jax.nn.silu(summed).astype(BF16)


def recurrence(convolved, relocated, lens, forget_bias, norm_gain, head_size):
    local_reqs, new_tokens, _, channels = convolved.shape
    head_count = channels // head_size
    values = convolved.astype(F32).reshape(local_reqs, new_tokens, 3, head_count, head_size)
    queries = values[:, :, 0]
    keep_rate = jax.nn.sigmoid(values[:, :, 1] + forget_bias.reshape(head_count, head_size))
    inputs = values[:, :, 2]
    current = relocated.astype(F32) * (lens > 0).astype(F32)[:, None, None, None]
    outputs = []
    for position in range(new_tokens):
        rate_now = keep_rate[:, position]
        current = (
            rate_now[..., None] * current
            + (1.0 - rate_now)[..., None] * inputs[:, position][:, :, None, :]
        )
        outputs.append(jnp.einsum("rhk,rhkv->rhv", queries[:, position], current))
    stacked = jnp.stack(outputs, axis=1)
    inverse_rms = lax.rsqrt(jnp.mean(stacked * stacked, axis=-1, keepdims=True) + 1e-06)
    normed = (stacked * inverse_rms).reshape(local_reqs, new_tokens, channels) * norm_gain
    return (normed.astype(BF16), current.astype(BF16))


def generic_body(
    resid, proj, conv_cache, conv_weight, forget_bias, owner, lengths, old_state, norm_gain, out_weight
):
    local_reqs, new_tokens = resid.shape[:2]
    devices = lax.axis_size("req")
    own_index = lax.axis_index("req")
    total_reqs = owner.shape[0]
    head_size = old_state.shape[-1]
    inverse = (
        jnp.zeros((total_reqs,), jnp.int32).at[owner].set(jnp.arange(total_reqs, dtype=jnp.int32))
    )
    local_lens = lax.dynamic_slice_in_dim(lengths, own_index * local_reqs, local_reqs)
    convolved = convolve(proj, conv_cache, conv_weight, local_lens)
    pieces = old_state.reshape(local_reqs, devices, -1)
    spread = lax.all_to_all(pieces, "req", split_axis=1, concat_axis=0, tiled=True)
    spread = spread.reshape(total_reqs, -1)
    picked = jnp.take(spread, inverse, axis=0).reshape(devices, local_reqs, 1, -1)
    routed = lax.all_to_all(picked, "req", split_axis=0, concat_axis=2, tiled=True)
    relocated = routed.reshape(old_state.shape)
    normed, new_state = recurrence(
        convolved, relocated, local_lens, forget_bias, norm_gain, head_size
    )
    flat_normed = normed.reshape(local_reqs * new_tokens, -1)
    flat_resid = resid.reshape(local_reqs * new_tokens, -1)
    partial_value = jnp.dot(flat_normed, out_weight, preferred_element_type=F32)
    summed = lax.psum(partial_value, "head")
    mixed = (flat_resid.astype(F32) + summed).astype(BF16).reshape(resid.shape)
    return (mixed, new_state)


def pack_kernel(blocks, state_ref, *refs):
    outs, sems = refs[:blocks], refs[blocks]
    reqs, head_size = state_ref.shape[0], state_ref.shape[-1]
    z = lax.axis_index("req") // 2
    copies = []
    for s in range(blocks - 1, -1, -1):
        for r in range(reqs):
            copy = pltpu.make_async_copy(
                state_ref.at[r, z ^ s],
                outs[s].at[pl.ds(r * head_size, head_size), :],
                sems.at[s * reqs + r],
            )
            copy.start()
            copies.append(copy)
    for copy in copies:
        copy.wait()


def pack(old_state):
    reqs, blocks, head_size, _ = old_state.shape
    return pl.pallas_call(
        functools.partial(pack_kernel, blocks),
        out_shape=[VMEM((reqs * head_size, head_size), BF16)] * blocks,
        in_specs=[pl.BlockSpec(memory_space=pl.ANY)],
        out_specs=[pl.BlockSpec(memory_space=VMEM)] * blocks,
        scratch_shapes=[pltpu.SemaphoreType.DMA((blocks * reqs,))],
        name="pack",
    )(old_state)


def prepare_kernel(blocks, lens_ref, *refs):
    proj_ref, cache_ref, weight_ref, bias_ref = refs[:4]
    turned, lefts, lasting, values, heard = refs[4:9]
    joined, conv, flat, columns = refs[9:]
    reqs, _, steps, _ = proj_ref.shape
    head_size = turned.shape[0]
    req = lax.axis_index("req")
    z = req // 2
    taps = weight_ref.shape[1]
    past = taps - 1
    row = lax.broadcasted_iota(jnp.int32, (reqs, head_size), 0)
    live = jnp.zeros((reqs, head_size), F32)
    for r in range(reqs):
        live = jnp.where(row == r, (lens_ref[req * reqs + r] > 0).astype(F32), live)

    for p in range(3):
        weight = weight_ref[p].astype(F32)
        old = [cache_ref[j, p].astype(F32) for j in range(past)]
        for r in range(reqs):
            length = lens_ref[req * reqs + r]
            own = p * reqs + r
            for j in range(past):
                seen = (length >= past - j).astype(F32)
                joined[own, j : j + 1, :] = old[j][r : r + 1, :] * seen
            joined[own, past : past + steps, :] = proj_ref[r, p].astype(F32)
            total = joined[own, past : past + steps, :] * weight[0:1, :]
            for tap in range(1, taps):
                begin = past - tap
                total = total + joined[own, begin : begin + steps, :] * weight[tap : tap + 1, :]
            at = own * steps
            conv[at : at + steps, :] = total / (1.0 + jnp.exp(-total))

    columns[...] = jnp.zeros_like(columns)
    for s in range(blocks):
        head = z ^ s
        lanes = pl.ds(pl.multiple_of(head * head_size, head_size), head_size)
        flat[...] = conv[:, lanes].astype(BF16).astype(F32)
        parts = [
            [flat[pl.ds(p * reqs * steps + t, reqs, stride=steps), :] for t in range(steps)]
            for p in range(3)
        ]
        query, inputs = parts[0], parts[2]
        bias = bias_ref[pl.ds(head, 1), :]
        keep = [jax.nn.sigmoid(gate + bias) for gate in parts[1]]
        base = s * steps * reqs
        weights = []
        decay = live
        for t in range(steps):
            weights = [w * keep[t] for w in weights] + [1.0 - keep[t]]
            decay = decay * keep[t]
            lefts[pl.ds(base + t * reqs, reqs), :] = query[t] * decay
            values[pl.ds(base + t * reqs, reqs), :] = inputs[t]
            out = jnp.zeros_like(query[t])
            for earlier in range(t + 1):
                score = jnp.sum(query[t] * weights[earlier], axis=-1, keepdims=True)
                out = out + score * inputs[earlier]
            heard[pl.ds(base + t, reqs, stride=steps), :] = out
        for t in range(steps):
            lasting[pl.ds(base + t * reqs, reqs), :] = weights[t]
        columns[pl.ds(s * reqs, reqs), :] = decay
    turned[...] = columns[...].T


def prepare(lengths, proj, conv_cache, conv_weight, forget_bias, blocks, head_size):
    reqs, steps, _, width = proj.shape
    taps = conv_weight.shape[0]
    columns = -(-blocks * reqs // 128) * 128
    spec = pl.BlockSpec(memory_space=VMEM)
    table = VMEM((blocks * steps * reqs, head_size), F32)
    return pl.pallas_call(
        functools.partial(prepare_kernel, blocks),
        out_shape=[VMEM((head_size, columns), F32)] + [table] * 4,
        in_specs=[pl.BlockSpec(memory_space=pltpu.SMEM)] + [spec] * 4,
        out_specs=[spec] * 5,
        scratch_shapes=[
            VMEM((3 * reqs, taps + steps, width), F32),
            VMEM((3 * reqs * steps, width), F32),
            VMEM((3 * reqs * steps, head_size), F32),
            VMEM((columns, head_size), F32),
        ],
        name="prepare",
    )(
        lengths,
        proj.transpose(0, 2, 1, 3),
        conv_cache.transpose(1, 2, 0, 3),
        conv_weight.transpose(1, 0, 2),
        forget_bias.reshape(blocks, head_size),
    )


def route_kernel(blocks, index_far, *refs):
    own = in_order(refs[:blocks], order_out(blocks))
    sib = in_order(refs[blocks : 2 * blocks], order_out(blocks))
    outs = refs[2 * blocks : 3 * blocks]
    pool, index_ref, sem = refs[3 * blocks :]
    fetch = pltpu.make_async_copy(index_far, index_ref, sem)
    fetch.start()
    head_size = pool.shape[-1]
    reqs = outs[0].shape[0] // head_size
    for s in range(blocks):
        for r in range(reqs):
            here = slice(r * head_size, (r + 1) * head_size)
            pool[s * reqs + r] = own[s][here, :]
            pool[(blocks + s) * reqs + r] = sib[s][here, :]
    fetch.wait()
    for s in range(blocks):
        for r in range(reqs):
            outs[s][r * head_size : (r + 1) * head_size, :] = pool[index_ref[s * reqs + r]]


def route(index, own, sib):
    blocks = len(own)
    rows, head_size = own[0].shape
    spec = pl.BlockSpec(memory_space=VMEM)
    return pl.pallas_call(
        functools.partial(route_kernel, blocks),
        out_shape=[VMEM((rows, head_size), BF16)] * blocks,
        in_specs=[pl.BlockSpec(memory_space=pl.ANY)] + [spec] * (2 * blocks),
        out_specs=[spec] * blocks,
        scratch_shapes=[
            VMEM((2 * blocks * rows // head_size, head_size, head_size), BF16),
            pltpu.SMEM(index.shape, jnp.int32),
            pltpu.SemaphoreType.DMA(()),
        ],
        name="route",
        compiler_params=PARAMS,
    )(index, *on_chip(*[own[s] for s in order_out(blocks)], *[sib[s] for s in order_out(blocks)]))


def fetch_kernel(far_ref, out, sem):
    copy = pltpu.make_async_copy(far_ref, out, sem)
    copy.start()
    copy.wait()


def fetch(value):
    return pl.pallas_call(
        fetch_kernel,
        out_shape=VMEM(value.shape, value.dtype),
        in_specs=[pl.BlockSpec(memory_space=pl.ANY)],
        out_specs=pl.BlockSpec(memory_space=VMEM),
        scratch_shapes=[pltpu.SemaphoreType.DMA(())],
        name="fetch",
        compiler_params=PARAMS,
    )(pltpu.with_memory_space_constraint(value, pltpu.HBM))


def home_kernel(blocks, reqs, steps, *refs):
    back = in_order(refs[:blocks], order_back(blocks))
    kept, lefts, heard_in, gain_ref, weight, part, heard, normed = refs[blocks:]
    stayed = lax.axis_index("req") % 2 == lax.axis_index("head") % 2
    head_size = gain_ref.shape[-1]
    z = lax.axis_index("req") // 2
    heard[...] = heard_in[...]
    for s in range(blocks):
        here = slice(s * steps * reqs, (s + 1) * steps * reqs)
        for r in range(reqs):
            span = slice(r * head_size, (r + 1) * head_size)
            old = back[s][span, :]
            if s == 0:
                old = jnp.where(stayed, kept[span, :], old)
            wanted = lefts[pl.ds(here.start + r, steps, stride=reqs), :].astype(BF16)
            said = jnp.dot(wanted, old, preferred_element_type=F32)
            heard[pl.ds((s * reqs + r) * steps, steps), :] += said
        head_out = heard[here, :]
        scale = lax.rsqrt(jnp.mean(head_out * head_out, axis=-1, keepdims=True) + 1e-06)
        gain = gain_ref[pl.ds(z ^ s, 1), :]
        lanes = pl.ds(pl.multiple_of((z ^ s) * head_size, head_size), head_size)
        normed[:, lanes] = (head_out * scale * gain).astype(BF16)
    part[...] = jnp.dot(normed[...], weight[...], preferred_element_type=F32).astype(BF16)


def home(back, kept, lefts, heard, norm_gain, weight, reqs, steps):
    blocks = len(back)
    head_size = back[0].shape[-1]
    spec = pl.BlockSpec(memory_space=VMEM)
    gain = norm_gain.reshape(blocks, head_size)
    return pl.pallas_call(
        functools.partial(home_kernel, blocks, reqs, steps),
        out_shape=VMEM((reqs * steps, weight.shape[1]), BF16),
        in_specs=[spec] * (blocks + 5),
        out_specs=spec,
        scratch_shapes=[
            VMEM((blocks * reqs * steps, head_size), F32),
            VMEM((reqs * steps, weight.shape[0]), BF16),
        ],
        name="home",
        compiler_params=PARAMS,
    )(*on_chip(*[back[s] for s in order_back(blocks)], kept, lefts, heard, gain, weight))


def place_kernel(blocks, reqs, steps, *refs):
    back = in_order(refs[:blocks], order_back(blocks))
    kept, turned_ref, lasting, values, out, fresh, sems = refs[blocks:]
    stayed = lax.axis_index("req") % 2 == lax.axis_index("head") % 2
    head_size = turned_ref.shape[0]
    z = lax.axis_index("req") // 2
    turned = turned_ref[...]
    of_req = lax.broadcasted_iota(jnp.int32, (steps * reqs, head_size), 0) % reqs
    copies = []
    for s in range(blocks):
        here = slice(s * steps * reqs, (s + 1) * steps * reqs)
        left = lasting[here, :]
        high = left.astype(BF16)
        low = (left - high.astype(F32)).astype(BF16)
        value = values[here, :]
        spread = [jnp.where(of_req == r, value, 0.0).astype(BF16) for r in range(reqs)]
        spread = jnp.concatenate(spread, axis=1)
        added = lax.dot_general(
            jnp.concatenate([high, low], axis=0),
            jnp.concatenate([spread, spread], axis=0),
            (((0,), (0,)), ((), ())),
            preferred_element_type=F32,
        )
        for r in range(reqs):
            i = s * reqs + r
            span = slice(r * head_size, (r + 1) * head_size)
            old = back[s][span, :]
            if s == 0:
                old = jnp.where(stayed, kept[span, :], old)
            current = turned[:, i : i + 1] * old.astype(F32) + added[:, span]
            fresh[i] = current.astype(BF16)
            copy = pltpu.make_async_copy(fresh.at[i], out.at[r, z ^ s], sems.at[i])
            copy.start()
            copies.append(copy)
    for copy in copies:
        copy.wait()


def place(back, kept, turned, lasting, values, shape, steps):
    reqs, blocks, head_size, _ = shape
    return pl.pallas_call(
        functools.partial(place_kernel, blocks, reqs, steps),
        out_shape=jax.ShapeDtypeStruct(shape, BF16),
        in_specs=[pl.BlockSpec(memory_space=VMEM)] * (blocks + 4),
        out_specs=pl.BlockSpec(memory_space=pl.ANY),
        scratch_shapes=[
            VMEM((blocks * reqs, head_size, head_size), BF16),
            pltpu.SemaphoreType.DMA((blocks * reqs,)),
        ],
        name="place",
        compiler_params=PARAMS,
    )(*on_chip(*[back[s] for s in order_back(blocks)], kept, turned, lasting, values))


def add_kernel(resid, *refs):
    out = refs[-1]
    total = [value[...].astype(F32) for value in refs[:-1]]
    while len(total) > 1:
        total = [total[k] + total[k + 1] for k in range(0, len(total), 2)]
    reqs = resid.shape[0]
    steps = total[0].shape[0] // reqs
    for r in range(reqs):
        out[r] = (resid[r].astype(F32) + total[0][r * steps : (r + 1) * steps, :]).astype(BF16)


def add(resid, terms):
    spec = pl.BlockSpec(memory_space=VMEM)
    return pl.pallas_call(
        add_kernel,
        out_shape=jax.ShapeDtypeStruct(resid.shape, BF16),
        in_specs=[spec] * (1 + len(terms)),
        out_specs=spec,
        name="add",
        compiler_params=PARAMS,
    )(*on_chip(resid, *terms))


def order_out(blocks):
    half = blocks // 2
    return (blocks - 1, *range(half - 1, -1, -1), *range(half, blocks - 1))


def order_back(blocks):
    return (*range(blocks // 2, blocks), *range(blocks // 2 - 1, -1, -1))


def in_order(refs, order):
    return [refs[order.index(s)] for s in range(len(refs))]


def on_chip(*arrays):
    return [pltpu.with_memory_space_constraint(value, VMEM) for value in arrays]


def swapped_body(
    resid, proj, conv_cache, conv_weight, forget_bias, owner, lengths, old_state, norm_gain, out_weight
):
    local_reqs, steps, width = resid.shape
    blocks = old_state.shape[1]
    head_size = old_state.shape[-1]
    n_head = lax.axis_size("head")
    own_req = lax.axis_index("req")
    own_head = lax.axis_index("head")
    z, core = own_req // 2, own_head % 2

    both = ("req", "head")
    sibling = [(i, i ^ 1) for i in range(n_head)]

    def swap(value, s, cross=False):
        pairs = []
        for a in range(blocks):
            for b in range(2):
                for y in range(n_head // 2):
                    for c in range(2):
                        to = (b ^ 1, c ^ 1) if cross else (c, b)
                        here = (a * 2 + b) * n_head + y * 2 + c
                        pairs.append((here, ((a ^ s) * 2 + to[0]) * n_head + y * 2 + to[1]))
        return lax.ppermute(value, both, pairs)

    packs = pack(old_state)
    own = [swap(packs[s], s) for s in range(blocks)]
    proj, conv_cache, conv_weight, forget_bias, norm_gain, *_ = lax.optimization_barrier(
        (proj, conv_cache, conv_weight, forget_bias, norm_gain, *packs)
    )
    prepared = prepare(lengths, proj, conv_cache, conv_weight, forget_bias, blocks, head_size)
    sib = [lax.ppermute(own[s], "head", sibling) for s in range(blocks)]

    zs = z ^ jnp.arange(blocks, dtype=jnp.int32)
    slots = ((zs * 2 + core) * local_reqs)[:, None] + jnp.arange(local_reqs, dtype=jnp.int32)[None, :]
    slots = slots.reshape(-1)
    every = jnp.arange(owner.shape[0], dtype=jnp.int32)[None, :]
    source = jnp.sum(jnp.where(owner[None, :] == slots[:, None], every, 0), axis=1)
    device, pos = source // local_reqs, source % local_reqs
    away = (device % 2 != core).astype(jnp.int32)
    index = (away * blocks + ((device // 2) ^ z)) * local_reqs + pos

    routed = route(index, own, sib)
    back = [swap(routed[s], s, cross=s == 0) for s in range(blocks)]
    weight, *_ = lax.optimization_barrier((out_weight, *routed))
    turned, lefts, lasting, values, heard = prepared
    weight = fetch(weight)
    part = home(back, routed[0], lefts, heard, norm_gain, weight, local_reqs, steps)
    terms = [part, lax.ppermute(part, "head", sibling)]
    step = 2
    while step < n_head:
        part = (terms[0].astype(F32) + terms[1].astype(F32)).astype(BF16)
        terms = [part, lax.ppermute(part, "head", [(i, i ^ step) for i in range(n_head)])]
        step *= 2
    *back, part = lax.optimization_barrier((*back, part))
    new_state = place(back, routed[0], turned, lasting, values, old_state.shape, steps)
    return add(resid, terms), new_state


def solution(mesh):
    in_specs = (
        P("req", None, None),
        P("req", None, None, "head"),
        P("req", None, None, "head"),
        P(None, None, "head"),
        P("head"),
        P(),
        P(),
        P("req", "head", None, None),
        P("head"),
        P("head", None),
    )
    out_specs = (P("req", None, None), P("req", "head", None, None))

    def body(*args):
        heads, parts = args[7].shape[1], mesh.shape["head"]
        swapped = mesh.shape["req"] == 2 * heads and heads & (heads - 1) == 0
        swapped = swapped and parts > 1 and parts & (parts - 1) == 0
        return (swapped_body if swapped else generic_body)(*args)

    return jax.shard_map(body, mesh=mesh, in_specs=in_specs, out_specs=out_specs, check_vma=False)
```

```python
import functools

import jax
import jax.numpy as jnp
from jax import lax
from jax.experimental import pallas as pl
from jax.experimental.pallas import tpu as pltpu
from jax.sharding import PartitionSpec as P

BF16 = jnp.bfloat16
F32 = jnp.float32
VMEM = pltpu.VMEM
PARAMS = pltpu.CompilerParams(vmem_limit_bytes=16 * 2**20)


def convolve(proj, conv_cache, conv_weight, lens):
    taps = conv_weight.shape[0]
    new_tokens = proj.shape[1]
    joined = jnp.concatenate([conv_cache, proj], axis=1).astype(F32)
    places = lens[:, None] + jnp.arange(-(taps - 1), new_tokens, dtype=jnp.int32)[None, :]
    joined = jnp.where((places >= 0)[:, :, None, None], joined, F32(0.0))
    summed = jnp.zeros(proj.shape, F32)
    for offset in range(taps):
        begin_at = taps - 1 - offset
        summed = summed + joined[:, begin_at : begin_at + new_tokens] * conv_weight[offset].astype(F32)
    return jax.nn.silu(summed).astype(BF16)


def recurrence(convolved, relocated, lens, forget_bias, norm_gain, head_size):
    local_reqs, new_tokens, _, channels = convolved.shape
    head_count = channels // head_size
    values = convolved.astype(F32).reshape(local_reqs, new_tokens, 3, head_count, head_size)
    queries = values[:, :, 0]
    keep_rate = jax.nn.sigmoid(values[:, :, 1] + forget_bias.reshape(head_count, head_size))
    inputs = values[:, :, 2]
    current = relocated.astype(F32) * (lens > 0).astype(F32)[:, None, None, None]
    outputs = []
    for position in range(new_tokens):
        rate_now = keep_rate[:, position]
        current = (
            rate_now[..., None] * current
            + (1.0 - rate_now)[..., None] * inputs[:, position][:, :, None, :]
        )
        outputs.append(jnp.einsum("rhk,rhkv->rhv", queries[:, position], current))
    stacked = jnp.stack(outputs, axis=1)
    inverse_rms = lax.rsqrt(jnp.mean(stacked * stacked, axis=-1, keepdims=True) + 1e-06)
    normed = (stacked * inverse_rms).reshape(local_reqs, new_tokens, channels) * norm_gain
    return (normed.astype(BF16), current.astype(BF16))


def generic_body(
    resid, proj, conv_cache, conv_weight, forget_bias, owner, lengths, old_state, norm_gain, out_weight
):
    local_reqs, new_tokens = resid.shape[:2]
    devices = lax.axis_size("req")
    own_index = lax.axis_index("req")
    total_reqs = owner.shape[0]
    head_size = old_state.shape[-1]
    inverse = (
        jnp.zeros((total_reqs,), jnp.int32).at[owner].set(jnp.arange(total_reqs, dtype=jnp.int32))
    )
    local_lens = lax.dynamic_slice_in_dim(lengths, own_index * local_reqs, local_reqs)
    convolved = convolve(proj, conv_cache, conv_weight, local_lens)
    pieces = old_state.reshape(local_reqs, devices, -1)
    spread = lax.all_to_all(pieces, "req", split_axis=1, concat_axis=0, tiled=True)
    spread = spread.reshape(total_reqs, -1)
    picked = jnp.take(spread, inverse, axis=0).reshape(devices, local_reqs, 1, -1)
    routed = lax.all_to_all(picked, "req", split_axis=0, concat_axis=2, tiled=True)
    relocated = routed.reshape(old_state.shape)
    normed, new_state = recurrence(
        convolved, relocated, local_lens, forget_bias, norm_gain, head_size
    )
    flat_normed = normed.reshape(local_reqs * new_tokens, -1)
    flat_resid = resid.reshape(local_reqs * new_tokens, -1)
    partial_value = jnp.dot(flat_normed, out_weight, preferred_element_type=F32)
    summed = lax.psum(partial_value, "head")
    mixed = (flat_resid.astype(F32) + summed).astype(BF16).reshape(resid.shape)
    return (mixed, new_state)


def pack_kernel(blocks, state_ref, *refs):
    outs, sems = refs[:blocks], refs[blocks]
    reqs, head_size = state_ref.shape[0], state_ref.shape[-1]
    z = lax.axis_index("req") // 2
    copies = []
    for s in range(blocks - 1, -1, -1):
        for r in range(reqs):
            copy = pltpu.make_async_copy(
                state_ref.at[r, z ^ s],
                outs[s].at[pl.ds(r * head_size, head_size), :],
                sems.at[s * reqs + r],
            )
            copy.start()
            copies.append(copy)
    for copy in copies:
        copy.wait()


def pack(old_state):
    reqs, blocks, head_size, _ = old_state.shape
    return pl.pallas_call(
        functools.partial(pack_kernel, blocks),
        out_shape=[VMEM((reqs * head_size, head_size), BF16)] * blocks,
        in_specs=[pl.BlockSpec(memory_space=pl.ANY)],
        out_specs=[pl.BlockSpec(memory_space=VMEM)] * blocks,
        scratch_shapes=[pltpu.SemaphoreType.DMA((blocks * reqs,))],
        name="pack",
    )(old_state)


def prepare_kernel(blocks, lens_ref, *refs):
    proj_ref, cache_ref, weight_ref, bias_ref = refs[:4]
    turned, lefts, lasting, values, heard = refs[4:9]
    joined, conv, flat, columns = refs[9:]
    reqs, _, steps, _ = proj_ref.shape
    head_size = turned.shape[0]
    req = lax.axis_index("req")
    z = req // 2
    taps = weight_ref.shape[1]
    past = taps - 1
    row = lax.broadcasted_iota(jnp.int32, (reqs, head_size), 0)
    live = jnp.zeros((reqs, head_size), F32)
    for r in range(reqs):
        live = jnp.where(row == r, (lens_ref[req * reqs + r] > 0).astype(F32), live)

    for p in range(3):
        weight = weight_ref[p].astype(F32)
        old = [cache_ref[j, p].astype(F32) for j in range(past)]
        for r in range(reqs):
            length = lens_ref[req * reqs + r]
            own = p * reqs + r
            for j in range(past):
                seen = (length >= past - j).astype(F32)
                joined[own, j : j + 1, :] = old[j][r : r + 1, :] * seen
            joined[own, past : past + steps, :] = proj_ref[r, p].astype(F32)
            total = joined[own, past : past + steps, :] * weight[0:1, :]
            for tap in range(1, taps):
                begin = past - tap
                total = total + joined[own, begin : begin + steps, :] * weight[tap : tap + 1, :]
            at = own * steps
            conv[at : at + steps, :] = total / (1.0 + jnp.exp(-total))

    columns[...] = jnp.zeros_like(columns)
    for s in range(blocks):
        head = z ^ s
        lanes = pl.ds(pl.multiple_of(head * head_size, head_size), head_size)
        flat[...] = conv[:, lanes].astype(BF16).astype(F32)
        parts = [
            [flat[pl.ds(p * reqs * steps + t, reqs, stride=steps), :] for t in range(steps)]
            for p in range(3)
        ]
        query, inputs = parts[0], parts[2]
        bias = bias_ref[pl.ds(head, 1), :]
        keep = [jax.nn.sigmoid(gate + bias) for gate in parts[1]]
        base = s * steps * reqs
        weights = []
        decay = live
        for t in range(steps):
            weights = [w * keep[t] for w in weights] + [1.0 - keep[t]]
            decay = decay * keep[t]
            lefts[pl.ds(base + t * reqs, reqs), :] = query[t] * decay
            values[pl.ds(base + t * reqs, reqs), :] = inputs[t]
            out = jnp.zeros_like(query[t])
            for earlier in range(t + 1):
                score = jnp.sum(query[t] * weights[earlier], axis=-1, keepdims=True)
                out = out + score * inputs[earlier]
            heard[pl.ds(base + t, reqs, stride=steps), :] = out
        for t in range(steps):
            lasting[pl.ds(base + t * reqs, reqs), :] = weights[t]
        columns[pl.ds(s * reqs, reqs), :] = decay
    turned[...] = columns[...].T


def prepare(lengths, proj, conv_cache, conv_weight, forget_bias, blocks, head_size):
    reqs, steps, _, width = proj.shape
    taps = conv_weight.shape[0]
    columns = -(-blocks * reqs // 128) * 128
    spec = pl.BlockSpec(memory_space=VMEM)
    table = VMEM((blocks * steps * reqs, head_size), F32)
    return pl.pallas_call(
        functools.partial(prepare_kernel, blocks),
        out_shape=[VMEM((head_size, columns), F32)] + [table] * 4,
        in_specs=[pl.BlockSpec(memory_space=pltpu.SMEM)] + [spec] * 4,
        out_specs=[spec] * 5,
        scratch_shapes=[
            VMEM((3 * reqs, taps + steps, width), F32),
            VMEM((3 * reqs * steps, width), F32),
            VMEM((3 * reqs * steps, head_size), F32),
            VMEM((columns, head_size), F32),
        ],
        name="prepare",
    )(
        lengths,
        proj.transpose(0, 2, 1, 3),
        conv_cache.transpose(1, 2, 0, 3),
        conv_weight.transpose(1, 0, 2),
        forget_bias.reshape(blocks, head_size),
    )


def route_kernel(blocks, index_far, *refs):
    own = in_order(refs[:blocks], order_out(blocks))
    sib = in_order(refs[blocks : 2 * blocks], order_out(blocks))
    outs = refs[2 * blocks : 3 * blocks]
    pool, index_ref, sem = refs[3 * blocks :]
    fetch = pltpu.make_async_copy(index_far, index_ref, sem)
    fetch.start()
    head_size = pool.shape[-1]
    reqs = outs[0].shape[0] // head_size
    for s in range(blocks):
        for r in range(reqs):
            here = slice(r * head_size, (r + 1) * head_size)
            pool[s * reqs + r] = own[s][here, :]
            pool[(blocks + s) * reqs + r] = sib[s][here, :]
    fetch.wait()
    for s in range(blocks):
        for r in range(reqs):
            outs[s][r * head_size : (r + 1) * head_size, :] = pool[index_ref[s * reqs + r]]


def route(index, own, sib):
    blocks = len(own)
    rows, head_size = own[0].shape
    spec = pl.BlockSpec(memory_space=VMEM)
    return pl.pallas_call(
        functools.partial(route_kernel, blocks),
        out_shape=[VMEM((rows, head_size), BF16)] * blocks,
        in_specs=[pl.BlockSpec(memory_space=pl.ANY)] + [spec] * (2 * blocks),
        out_specs=[spec] * blocks,
        scratch_shapes=[
            VMEM((2 * blocks * rows // head_size, head_size, head_size), BF16),
            pltpu.SMEM(index.shape, jnp.int32),
            pltpu.SemaphoreType.DMA(()),
        ],
        name="route",
        compiler_params=PARAMS,
    )(index, *on_chip(*[own[s] for s in order_out(blocks)], *[sib[s] for s in order_out(blocks)]))


def fetch_kernel(far_ref, out, sem):
    copy = pltpu.make_async_copy(far_ref, out, sem)
    copy.start()
    copy.wait()


def fetch(value):
    return pl.pallas_call(
        fetch_kernel,
        out_shape=VMEM(value.shape, value.dtype),
        in_specs=[pl.BlockSpec(memory_space=pl.ANY)],
        out_specs=pl.BlockSpec(memory_space=VMEM),
        scratch_shapes=[pltpu.SemaphoreType.DMA(())],
        name="fetch",
        compiler_params=PARAMS,
    )(pltpu.with_memory_space_constraint(value, pltpu.HBM))


def home_kernel(blocks, reqs, steps, *refs):
    back = in_order(refs[:blocks], order_back(blocks))
    kept, lefts, heard_in, gain_ref, weight, part, heard, normed = refs[blocks:]
    stayed = lax.axis_index("req") % 2 == lax.axis_index("head") % 2
    head_size = gain_ref.shape[-1]
    z = lax.axis_index("req") // 2
    heard[...] = heard_in[...]
    for s in range(blocks):
        here = slice(s * steps * reqs, (s + 1) * steps * reqs)
        for r in range(reqs):
            span = slice(r * head_size, (r + 1) * head_size)
            old = back[s][span, :]
            if s == 0:
                old = jnp.where(stayed, kept[span, :], old)
            wanted = lefts[pl.ds(here.start + r, steps, stride=reqs), :].astype(BF16)
            said = jnp.dot(wanted, old, preferred_element_type=F32)
            heard[pl.ds((s * reqs + r) * steps, steps), :] += said
        head_out = heard[here, :]
        scale = lax.rsqrt(jnp.mean(head_out * head_out, axis=-1, keepdims=True) + 1e-06)
        gain = gain_ref[pl.ds(z ^ s, 1), :]
        lanes = pl.ds(pl.multiple_of((z ^ s) * head_size, head_size), head_size)
        normed[:, lanes] = (head_out * scale * gain).astype(BF16)
    part[...] = jnp.dot(normed[...], weight[...], preferred_element_type=F32).astype(BF16)


def home(back, kept, lefts, heard, norm_gain, weight, reqs, steps):
    blocks = len(back)
    head_size = back[0].shape[-1]
    spec = pl.BlockSpec(memory_space=VMEM)
    gain = norm_gain.reshape(blocks, head_size)
    return pl.pallas_call(
        functools.partial(home_kernel, blocks, reqs, steps),
        out_shape=VMEM((reqs * steps, weight.shape[1]), BF16),
        in_specs=[spec] * (blocks + 5),
        out_specs=spec,
        scratch_shapes=[
            VMEM((blocks * reqs * steps, head_size), F32),
            VMEM((reqs * steps, weight.shape[0]), BF16),
        ],
        name="home",
        compiler_params=PARAMS,
    )(*on_chip(*[back[s] for s in order_back(blocks)], kept, lefts, heard, gain, weight))


def place_kernel(blocks, reqs, steps, *refs):
    back = in_order(refs[:blocks], order_back(blocks))
    kept, turned_ref, lasting, values, out, fresh, sems = refs[blocks:]
    stayed = lax.axis_index("req") % 2 == lax.axis_index("head") % 2
    head_size = turned_ref.shape[0]
    z = lax.axis_index("req") // 2
    turned = turned_ref[...]
    of_req = lax.broadcasted_iota(jnp.int32, (steps * reqs, head_size), 0) % reqs
    copies = []
    for s in range(blocks):
        here = slice(s * steps * reqs, (s + 1) * steps * reqs)
        left = lasting[here, :]
        high = left.astype(BF16)
        low = (left - high.astype(F32)).astype(BF16)
        value = values[here, :]
        spread = [jnp.where(of_req == r, value, 0.0).astype(BF16) for r in range(reqs)]
        spread = jnp.concatenate(spread, axis=1)
        added = lax.dot_general(
            jnp.concatenate([high, low], axis=0),
            jnp.concatenate([spread, spread], axis=0),
            (((0,), (0,)), ((), ())),
            preferred_element_type=F32,
        )
        for r in range(reqs):
            i = s * reqs + r
            span = slice(r * head_size, (r + 1) * head_size)
            old = back[s][span, :]
            if s == 0:
                old = jnp.where(stayed, kept[span, :], old)
            current = turned[:, i : i + 1] * old.astype(F32) + added[:, span]
            fresh[i] = current.astype(BF16)
            copy = pltpu.make_async_copy(fresh.at[i], out.at[r, z ^ s], sems.at[i])
            copy.start()
            copies.append(copy)
    for copy in copies:
        copy.wait()


def place(back, kept, turned, lasting, values, shape, steps):
    reqs, blocks, head_size, _ = shape
    return pl.pallas_call(
        functools.partial(place_kernel, blocks, reqs, steps),
        out_shape=jax.ShapeDtypeStruct(shape, BF16),
        in_specs=[pl.BlockSpec(memory_space=VMEM)] * (blocks + 4),
        out_specs=pl.BlockSpec(memory_space=pl.ANY),
        scratch_shapes=[
            VMEM((blocks * reqs, head_size, head_size), BF16),
            pltpu.SemaphoreType.DMA((blocks * reqs,)),
        ],
        name="place",
        compiler_params=PARAMS,
    )(*on_chip(*[back[s] for s in order_back(blocks)], kept, turned, lasting, values))


def add_kernel(resid, *refs):
    out = refs[-1]
    total = [value[...].astype(F32) for value in refs[:-1]]
    while len(total) > 1:
        total = [total[k] + total[k + 1] for k in range(0, len(total), 2)]
    reqs = resid.shape[0]
    steps = total[0].shape[0] // reqs
    for r in range(reqs):
        out[r] = (resid[r].astype(F32) + total[0][r * steps : (r + 1) * steps, :]).astype(BF16)


def add(resid, terms):
    spec = pl.BlockSpec(memory_space=VMEM)
    return pl.pallas_call(
        add_kernel,
        out_shape=jax.ShapeDtypeStruct(resid.shape, BF16),
        in_specs=[spec] * (1 + len(terms)),
        out_specs=spec,
        name="add",
        compiler_params=PARAMS,
    )(*on_chip(resid, *terms))


def order_out(blocks):
    half = blocks // 2
    return (blocks - 1, *range(half - 1, -1, -1), *range(half, blocks - 1))


def order_back(blocks):
    return (*range(blocks // 2, blocks), *range(blocks // 2 - 1, -1, -1))


def in_order(refs, order):
    return [refs[order.index(s)] for s in range(len(refs))]


def on_chip(*arrays):
    return [pltpu.with_memory_space_constraint(value, VMEM) for value in arrays]


def swapped_body(
    resid, proj, conv_cache, conv_weight, forget_bias, owner, lengths, old_state, norm_gain, out_weight
):
    local_reqs, steps, width = resid.shape
    blocks = old_state.shape[1]
    head_size = old_state.shape[-1]
    n_head = lax.axis_size("head")
    own_req = lax.axis_index("req")
    own_head = lax.axis_index("head")
    z, core = own_req // 2, own_head % 2

    both = ("req", "head")
    sibling = [(i, i ^ 1) for i in range(n_head)]

    def swap(value, s, cross=False):
        pairs = []
        for a in range(blocks):
            for b in range(2):
                for y in range(n_head // 2):
                    for c in range(2):
                        to = (b ^ 1, c ^ 1) if cross else (c, b)
                        here = (a * 2 + b) * n_head + y * 2 + c
                        pairs.append((here, ((a ^ s) * 2 + to[0]) * n_head + y * 2 + to[1]))
        return lax.ppermute(value, both, pairs)

    packs = pack(old_state)
    own = [swap(packs[s], s) for s in range(blocks)]
    proj, conv_cache, conv_weight, forget_bias, norm_gain, *_ = lax.optimization_barrier(
        (proj, conv_cache, conv_weight, forget_bias, norm_gain, *packs)
    )
    prepared = prepare(lengths, proj, conv_cache, conv_weight, forget_bias, blocks, head_size)
    sib = [lax.ppermute(own[s], "head", sibling) for s in range(blocks)]

    zs = z ^ jnp.arange(blocks, dtype=jnp.int32)
    slots = ((zs * 2 + core) * local_reqs)[:, None] + jnp.arange(local_reqs, dtype=jnp.int32)[None, :]
    slots = slots.reshape(-1)
    every = jnp.arange(owner.shape[0], dtype=jnp.int32)[None, :]
    source = jnp.sum(jnp.where(owner[None, :] == slots[:, None], every, 0), axis=1)
    device, pos = source // local_reqs, source % local_reqs
    away = (device % 2 != core).astype(jnp.int32)
    index = (away * blocks + ((device // 2) ^ z)) * local_reqs + pos

    routed = route(index, own, sib)
    back = [swap(routed[s], s, cross=s == 0) for s in range(blocks)]
    weight, *_ = lax.optimization_barrier((out_weight, *routed))
    turned, lefts, lasting, values, heard = prepared
    weight = fetch(weight)
    part = home(back, routed[0], lefts, heard, norm_gain, weight, local_reqs, steps)
    step = n_head // 2
    terms = [part, lax.ppermute(part, "head", [(i, i ^ step) for i in range(n_head)])]
    while step > 1:
        step //= 2
        part = (terms[0].astype(F32) + terms[1].astype(F32)).astype(BF16)
        terms = [part, lax.ppermute(part, "head", [(i, i ^ step) for i in range(n_head)])]

    *back, part = lax.optimization_barrier((*back, part))
    new_state = place(back, routed[0], turned, lasting, values, old_state.shape, steps)
    return add(resid, terms), new_state


def solution(mesh):
    in_specs = (
        P("req", None, None),
        P("req", None, None, "head"),
        P("req", None, None, "head"),
        P(None, None, "head"),
        P("head"),
        P(),
        P(),
        P("req", "head", None, None),
        P("head"),
        P("head", None),
    )
    out_specs = (P("req", None, None), P("req", "head", None, None))

    def body(*args):
        heads, parts = args[7].shape[1], mesh.shape["head"]
        swapped = mesh.shape["req"] == 2 * heads and heads & (heads - 1) == 0
        swapped = swapped and parts > 1 and parts & (parts - 1) == 0
        return (swapped_body if swapped else generic_body)(*args)

    return jax.shard_map(body, mesh=mesh, in_specs=in_specs, out_specs=out_specs, check_vma=False)
```

```python
import functools

import jax
import jax.numpy as jnp
from jax import lax
from jax.experimental import pallas as pl
from jax.experimental.pallas import tpu as pltpu
from jax.sharding import PartitionSpec as P

BF16 = jnp.bfloat16
F32 = jnp.float32
VMEM = pltpu.VMEM
PARAMS = pltpu.CompilerParams(vmem_limit_bytes=16 * 2**20)


def convolve(proj, conv_cache, conv_weight, lens):
    taps = conv_weight.shape[0]
    new_tokens = proj.shape[1]
    joined = jnp.concatenate([conv_cache, proj], axis=1).astype(F32)
    places = lens[:, None] + jnp.arange(-(taps - 1), new_tokens, dtype=jnp.int32)[None, :]
    joined = jnp.where((places >= 0)[:, :, None, None], joined, F32(0.0))
    summed = jnp.zeros(proj.shape, F32)
    for offset in range(taps):
        begin_at = taps - 1 - offset
        summed = summed + joined[:, begin_at : begin_at + new_tokens] * conv_weight[offset].astype(F32)
    return jax.nn.silu(summed).astype(BF16)


def recurrence(convolved, relocated, lens, forget_bias, norm_gain, head_size):
    local_reqs, new_tokens, _, channels = convolved.shape
    head_count = channels // head_size
    values = convolved.astype(F32).reshape(local_reqs, new_tokens, 3, head_count, head_size)
    queries = values[:, :, 0]
    keep_rate = jax.nn.sigmoid(values[:, :, 1] + forget_bias.reshape(head_count, head_size))
    inputs = values[:, :, 2]
    current = relocated.astype(F32) * (lens > 0).astype(F32)[:, None, None, None]
    outputs = []
    for position in range(new_tokens):
        rate_now = keep_rate[:, position]
        current = (
            rate_now[..., None] * current
            + (1.0 - rate_now)[..., None] * inputs[:, position][:, :, None, :]
        )
        outputs.append(jnp.einsum("rhk,rhkv->rhv", queries[:, position], current))
    stacked = jnp.stack(outputs, axis=1)
    inverse_rms = lax.rsqrt(jnp.mean(stacked * stacked, axis=-1, keepdims=True) + 1e-06)
    normed = (stacked * inverse_rms).reshape(local_reqs, new_tokens, channels) * norm_gain
    return (normed.astype(BF16), current.astype(BF16))


def generic_body(
    resid, proj, conv_cache, conv_weight, forget_bias, owner, lengths, old_state, norm_gain, out_weight
):
    local_reqs, new_tokens = resid.shape[:2]
    devices = lax.axis_size("req")
    own_index = lax.axis_index("req")
    total_reqs = owner.shape[0]
    head_size = old_state.shape[-1]
    inverse = (
        jnp.zeros((total_reqs,), jnp.int32).at[owner].set(jnp.arange(total_reqs, dtype=jnp.int32))
    )
    local_lens = lax.dynamic_slice_in_dim(lengths, own_index * local_reqs, local_reqs)
    convolved = convolve(proj, conv_cache, conv_weight, local_lens)
    pieces = old_state.reshape(local_reqs, devices, -1)
    spread = lax.all_to_all(pieces, "req", split_axis=1, concat_axis=0, tiled=True)
    spread = spread.reshape(total_reqs, -1)
    picked = jnp.take(spread, inverse, axis=0).reshape(devices, local_reqs, 1, -1)
    routed = lax.all_to_all(picked, "req", split_axis=0, concat_axis=2, tiled=True)
    relocated = routed.reshape(old_state.shape)
    normed, new_state = recurrence(
        convolved, relocated, local_lens, forget_bias, norm_gain, head_size
    )
    flat_normed = normed.reshape(local_reqs * new_tokens, -1)
    flat_resid = resid.reshape(local_reqs * new_tokens, -1)
    partial_value = jnp.dot(flat_normed, out_weight, preferred_element_type=F32)
    summed = lax.psum(partial_value, "head")
    mixed = (flat_resid.astype(F32) + summed).astype(BF16).reshape(resid.shape)
    return (mixed, new_state)


def pack_kernel(blocks, state_ref, *refs):
    outs, sems = refs[:blocks], refs[blocks]
    reqs, head_size = state_ref.shape[0], state_ref.shape[-1]
    z = lax.axis_index("req") // 2
    copies = []
    for s in range(blocks - 1, -1, -1):
        for r in range(reqs):
            copy = pltpu.make_async_copy(
                state_ref.at[r, z ^ s],
                outs[s].at[pl.ds(r * head_size, head_size), :],
                sems.at[s * reqs + r],
            )
            copy.start()
            copies.append(copy)
    for copy in copies:
        copy.wait()


def pack(old_state):
    reqs, blocks, head_size, _ = old_state.shape
    return pl.pallas_call(
        functools.partial(pack_kernel, blocks),
        out_shape=[VMEM((reqs * head_size, head_size), BF16)] * blocks,
        in_specs=[pl.BlockSpec(memory_space=pl.ANY)],
        out_specs=[pl.BlockSpec(memory_space=VMEM)] * blocks,
        scratch_shapes=[pltpu.SemaphoreType.DMA((blocks * reqs,))],
        name="pack",
    )(old_state)


def prepare_kernel(blocks, lens_ref, *refs):
    proj_ref, cache_ref, weight_ref, bias_ref = refs[:4]
    turned, lefts, lasting, values, heard = refs[4:9]
    joined, conv, flat, columns = refs[9:]
    reqs, _, steps, _ = proj_ref.shape
    head_size = turned.shape[0]
    req = lax.axis_index("req")
    z = req // 2
    taps = weight_ref.shape[1]
    past = taps - 1
    row = lax.broadcasted_iota(jnp.int32, (reqs, head_size), 0)
    live = jnp.zeros((reqs, head_size), F32)
    for r in range(reqs):
        live = jnp.where(row == r, (lens_ref[req * reqs + r] > 0).astype(F32), live)

    for p in range(3):
        weight = weight_ref[p].astype(F32)
        old = [cache_ref[j, p].astype(F32) for j in range(past)]
        for r in range(reqs):
            length = lens_ref[req * reqs + r]
            own = p * reqs + r
            for j in range(past):
                seen = (length >= past - j).astype(F32)
                joined[own, j : j + 1, :] = old[j][r : r + 1, :] * seen
            joined[own, past : past + steps, :] = proj_ref[r, p].astype(F32)
            total = joined[own, past : past + steps, :] * weight[0:1, :]
            for tap in range(1, taps):
                begin = past - tap
                total = total + joined[own, begin : begin + steps, :] * weight[tap : tap + 1, :]
            at = own * steps
            conv[at : at + steps, :] = total / (1.0 + jnp.exp(-total))

    columns[...] = jnp.zeros_like(columns)
    for s in range(blocks):
        head = z ^ s
        lanes = pl.ds(pl.multiple_of(head * head_size, head_size), head_size)
        flat[...] = conv[:, lanes].astype(BF16).astype(F32)
        parts = [
            [flat[pl.ds(p * reqs * steps + t, reqs, stride=steps), :] for t in range(steps)]
            for p in range(3)
        ]
        query, inputs = parts[0], parts[2]
        bias = bias_ref[pl.ds(head, 1), :]
        keep = [jax.nn.sigmoid(gate + bias) for gate in parts[1]]
        base = s * steps * reqs
        weights = []
        decay = live
        for t in range(steps):
            weights = [w * keep[t] for w in weights] + [1.0 - keep[t]]
            decay = decay * keep[t]
            lefts[pl.ds(base + t * reqs, reqs), :] = query[t] * decay
            values[pl.ds(base + t * reqs, reqs), :] = inputs[t]
            out = jnp.zeros_like(query[t])
            for earlier in range(t + 1):
                score = jnp.sum(query[t] * weights[earlier], axis=-1, keepdims=True)
                out = out + score * inputs[earlier]
            heard[pl.ds(base + t, reqs, stride=steps), :] = out
        for t in range(steps):
            lasting[pl.ds(base + t * reqs, reqs), :] = weights[t]
        columns[pl.ds(s * reqs, reqs), :] = decay
    turned[...] = columns[...].T


def prepare(lengths, proj, conv_cache, conv_weight, forget_bias, blocks, head_size):
    reqs, steps, _, width = proj.shape
    taps = conv_weight.shape[0]
    columns = -(-blocks * reqs // 128) * 128
    spec = pl.BlockSpec(memory_space=VMEM)
    table = VMEM((blocks * steps * reqs, head_size), F32)
    return pl.pallas_call(
        functools.partial(prepare_kernel, blocks),
        out_shape=[VMEM((head_size, columns), F32)] + [table] * 4,
        in_specs=[pl.BlockSpec(memory_space=pltpu.SMEM)] + [spec] * 4,
        out_specs=[spec] * 5,
        scratch_shapes=[
            VMEM((3 * reqs, taps + steps, width), F32),
            VMEM((3 * reqs * steps, width), F32),
            VMEM((3 * reqs * steps, head_size), F32),
            VMEM((columns, head_size), F32),
        ],
        name="prepare",
    )(
        lengths,
        proj.transpose(0, 2, 1, 3),
        conv_cache.transpose(1, 2, 0, 3),
        conv_weight.transpose(1, 0, 2),
        forget_bias.reshape(blocks, head_size),
    )


def route_kernel(blocks, index_far, *refs):
    own = in_order(refs[:blocks], order_out(blocks))
    sib = in_order(refs[blocks : 2 * blocks], order_out(blocks))
    outs = refs[2 * blocks : 3 * blocks]
    pool, index_ref, sem = refs[3 * blocks :]
    fetch = pltpu.make_async_copy(index_far, index_ref, sem)
    fetch.start()
    head_size = pool.shape[-1]
    reqs = outs[0].shape[0] // head_size
    for s in range(blocks):
        for r in range(reqs):
            here = slice(r * head_size, (r + 1) * head_size)
            pool[s * reqs + r] = own[s][here, :]
            pool[(blocks + s) * reqs + r] = sib[s][here, :]
    fetch.wait()
    for s in range(blocks):
        for r in range(reqs):
            outs[s][r * head_size : (r + 1) * head_size, :] = pool[index_ref[s * reqs + r]]


def route(index, own, sib):
    blocks = len(own)
    rows, head_size = own[0].shape
    spec = pl.BlockSpec(memory_space=VMEM)
    return pl.pallas_call(
        functools.partial(route_kernel, blocks),
        out_shape=[VMEM((rows, head_size), BF16)] * blocks,
        in_specs=[pl.BlockSpec(memory_space=pl.ANY)] + [spec] * (2 * blocks),
        out_specs=[spec] * blocks,
        scratch_shapes=[
            VMEM((2 * blocks * rows // head_size, head_size, head_size), BF16),
            pltpu.SMEM(index.shape, jnp.int32),
            pltpu.SemaphoreType.DMA(()),
        ],
        name="route",
        compiler_params=PARAMS,
    )(index, *on_chip(*[own[s] for s in order_out(blocks)], *[sib[s] for s in order_out(blocks)]))


def fetch_kernel(far_ref, out, sem):
    copy = pltpu.make_async_copy(far_ref, out, sem)
    copy.start()
    copy.wait()


def fetch(value):
    return pl.pallas_call(
        fetch_kernel,
        out_shape=VMEM(value.shape, value.dtype),
        in_specs=[pl.BlockSpec(memory_space=pl.ANY)],
        out_specs=pl.BlockSpec(memory_space=VMEM),
        scratch_shapes=[pltpu.SemaphoreType.DMA(())],
        name="fetch",
        compiler_params=PARAMS,
    )(pltpu.with_memory_space_constraint(value, pltpu.HBM))


def home_kernel(blocks, reqs, steps, *refs):
    back = in_order(refs[:blocks], order_back(blocks))
    kept, lefts, heard_in, gain_ref, weight, part, heard, normed = refs[blocks:]
    stayed = lax.axis_index("req") % 2 == lax.axis_index("head") % 2
    head_size = gain_ref.shape[-1]
    z = lax.axis_index("req") // 2
    heard[...] = heard_in[...]
    for s in range(blocks):
        here = slice(s * steps * reqs, (s + 1) * steps * reqs)
        for r in range(reqs):
            span = slice(r * head_size, (r + 1) * head_size)
            old = back[s][span, :]
            if s == 0:
                old = jnp.where(stayed, kept[span, :], old)
            wanted = lefts[pl.ds(here.start + r, steps, stride=reqs), :].astype(BF16)
            said = jnp.dot(wanted, old, preferred_element_type=F32)
            heard[pl.ds((s * reqs + r) * steps, steps), :] += said
        head_out = heard[here, :]
        scale = lax.rsqrt(jnp.mean(head_out * head_out, axis=-1, keepdims=True) + 1e-06)
        gain = gain_ref[pl.ds(z ^ s, 1), :]
        lanes = pl.ds(pl.multiple_of((z ^ s) * head_size, head_size), head_size)
        normed[:, lanes] = (head_out * scale * gain).astype(BF16)
    part[...] = jnp.dot(normed[...], weight[...], preferred_element_type=F32).astype(BF16)


def home(back, kept, lefts, heard, norm_gain, weight, reqs, steps):
    blocks = len(back)
    head_size = back[0].shape[-1]
    spec = pl.BlockSpec(memory_space=VMEM)
    gain = norm_gain.reshape(blocks, head_size)
    return pl.pallas_call(
        functools.partial(home_kernel, blocks, reqs, steps),
        out_shape=VMEM((reqs * steps, weight.shape[1]), BF16),
        in_specs=[spec] * (blocks + 5),
        out_specs=spec,
        scratch_shapes=[
            VMEM((blocks * reqs * steps, head_size), F32),
            VMEM((reqs * steps, weight.shape[0]), BF16),
        ],
        name="home",
        compiler_params=PARAMS,
    )(*on_chip(*[back[s] for s in order_back(blocks)], kept, lefts, heard, gain, weight))


def place_kernel(blocks, reqs, steps, *refs):
    back = in_order(refs[:blocks], order_back(blocks))
    kept, turned_ref, lasting, values, out, fresh, sems = refs[blocks:]
    stayed = lax.axis_index("req") % 2 == lax.axis_index("head") % 2
    head_size = turned_ref.shape[0]
    z = lax.axis_index("req") // 2
    turned = turned_ref[...]
    of_req = lax.broadcasted_iota(jnp.int32, (steps * reqs, head_size), 0) % reqs
    copies = []
    for s in range(blocks):
        here = slice(s * steps * reqs, (s + 1) * steps * reqs)
        left = lasting[here, :]
        high = left.astype(BF16)
        low = (left - high.astype(F32)).astype(BF16)
        value = values[here, :]
        spread = [jnp.where(of_req == r, value, 0.0).astype(BF16) for r in range(reqs)]
        spread = jnp.concatenate(spread, axis=1)
        added = lax.dot_general(
            jnp.concatenate([high, low], axis=0),
            jnp.concatenate([spread, spread], axis=0),
            (((0,), (0,)), ((), ())),
            preferred_element_type=F32,
        )
        for r in range(reqs):
            i = s * reqs + r
            span = slice(r * head_size, (r + 1) * head_size)
            old = back[s][span, :]
            if s == 0:
                old = jnp.where(stayed, kept[span, :], old)
            current = turned[:, i : i + 1] * old.astype(F32) + added[:, span]
            fresh[i] = current.astype(BF16)
            copy = pltpu.make_async_copy(fresh.at[i], out.at[r, z ^ s], sems.at[i])
            copy.start()
            copies.append(copy)
    for copy in copies:
        copy.wait()


def place(back, kept, turned, lasting, values, shape, steps):
    reqs, blocks, head_size, _ = shape
    return pl.pallas_call(
        functools.partial(place_kernel, blocks, reqs, steps),
        out_shape=jax.ShapeDtypeStruct(shape, BF16),
        in_specs=[pl.BlockSpec(memory_space=VMEM)] * (blocks + 4),
        out_specs=pl.BlockSpec(memory_space=pl.ANY),
        scratch_shapes=[
            VMEM((blocks * reqs, head_size, head_size), BF16),
            pltpu.SemaphoreType.DMA((blocks * reqs,)),
        ],
        name="place",
        compiler_params=PARAMS,
    )(*on_chip(*[back[s] for s in order_back(blocks)], kept, turned, lasting, values))


def add_kernel(resid, *refs):
    out = refs[-1]
    total = [value[...].astype(F32) for value in refs[:-1]]
    while len(total) > 1:
        total = [total[k] + total[k + 1] for k in range(0, len(total), 2)]
    reqs = resid.shape[0]
    steps = total[0].shape[0] // reqs
    for r in range(reqs):
        out[r] = (resid[r].astype(F32) + total[0][r * steps : (r + 1) * steps, :]).astype(BF16)


def add(resid, terms):
    spec = pl.BlockSpec(memory_space=VMEM)
    return pl.pallas_call(
        add_kernel,
        out_shape=jax.ShapeDtypeStruct(resid.shape, BF16),
        in_specs=[spec] * (1 + len(terms)),
        out_specs=spec,
        name="add",
        compiler_params=PARAMS,
    )(*on_chip(resid, *terms))


def order_out(blocks):
    half = blocks // 2
    return (blocks - 1, *range(half - 1, -1, -1), *range(half, blocks - 1))


def order_back(blocks):
    return (*range(blocks // 2, blocks), *range(blocks // 2 - 1, -1, -1))


def in_order(refs, order):
    return [refs[order.index(s)] for s in range(len(refs))]


def on_chip(*arrays):
    return [pltpu.with_memory_space_constraint(value, VMEM) for value in arrays]


def swapped_body(
    resid, proj, conv_cache, conv_weight, forget_bias, owner, lengths, old_state, norm_gain, out_weight
):
    local_reqs, steps, width = resid.shape
    blocks = old_state.shape[1]
    head_size = old_state.shape[-1]
    n_head = lax.axis_size("head")
    own_req = lax.axis_index("req")
    own_head = lax.axis_index("head")
    z, core = own_req // 2, own_head % 2

    both = ("req", "head")
    sibling = [(i, i ^ 1) for i in range(n_head)]

    def swap(value, s, cross=False):
        pairs = []
        for a in range(blocks):
            for b in range(2):
                for y in range(n_head // 2):
                    for c in range(2):
                        to = (b ^ 1, c ^ 1) if cross else (c, b)
                        here = (a * 2 + b) * n_head + y * 2 + c
                        pairs.append((here, ((a ^ s) * 2 + to[0]) * n_head + y * 2 + to[1]))
        return lax.ppermute(value, both, pairs)

    packs = pack(old_state)
    own = [swap(packs[s], s, cross=s == 0) for s in range(blocks)]
    own[0] = jnp.where(own_req % 2 == core, packs[0], own[0])
    proj, conv_cache, conv_weight, forget_bias, norm_gain, *_ = lax.optimization_barrier(
        (proj, conv_cache, conv_weight, forget_bias, norm_gain, *packs)
    )
    prepared = prepare(lengths, proj, conv_cache, conv_weight, forget_bias, blocks, head_size)
    sib = [lax.ppermute(own[s], "head", sibling) for s in range(blocks)]

    zs = z ^ jnp.arange(blocks, dtype=jnp.int32)
    slots = ((zs * 2 + core) * local_reqs)[:, None] + jnp.arange(local_reqs, dtype=jnp.int32)[None, :]
    slots = slots.reshape(-1)
    every = jnp.arange(owner.shape[0], dtype=jnp.int32)[None, :]
    source = jnp.sum(jnp.where(owner[None, :] == slots[:, None], every, 0), axis=1)
    device, pos = source // local_reqs, source % local_reqs
    away = (device % 2 != core).astype(jnp.int32)
    index = (away * blocks + ((device // 2) ^ z)) * local_reqs + pos

    routed = route(index, own, sib)
    back = [swap(routed[s], s, cross=s == 0) for s in range(blocks)]
    weight, *_ = lax.optimization_barrier((out_weight, *routed))
    turned, lefts, lasting, values, heard = prepared
    weight = fetch(weight)
    part = home(back, routed[0], lefts, heard, norm_gain, weight, local_reqs, steps)
    terms = [part, lax.ppermute(part, "head", sibling)]
    step = 2
    while step < n_head:
        part = (terms[0].astype(F32) + terms[1].astype(F32)).astype(BF16)
        terms = [part, lax.ppermute(part, "head", [(i, i ^ step) for i in range(n_head)])]
        step *= 2
    *back, part = lax.optimization_barrier((*back, part))
    new_state = place(back, routed[0], turned, lasting, values, old_state.shape, steps)
    return add(resid, terms), new_state


def solution(mesh):
    in_specs = (
        P("req", None, None),
        P("req", None, None, "head"),
        P("req", None, None, "head"),
        P(None, None, "head"),
        P("head"),
        P(),
        P(),
        P("req", "head", None, None),
        P("head"),
        P("head", None),
    )
    out_specs = (P("req", None, None), P("req", "head", None, None))

    def body(*args):
        heads, parts = args[7].shape[1], mesh.shape["head"]
        swapped = mesh.shape["req"] == 2 * heads and heads & (heads - 1) == 0
        swapped = swapped and parts > 1 and parts & (parts - 1) == 0
        return (swapped_body if swapped else generic_body)(*args)

    return jax.shard_map(body, mesh=mesh, in_specs=in_specs, out_specs=out_specs, check_vma=False)
```
